32 devices in a mesh: lat: 4 (over y, core), lon: 8 (over z, x).
Axes of the slice: x: 2, y: 2, z: 4, core: 2. Of those that a mesh axis runs over, the one named last changes fastest.
Arguments:
- source_fields: bfloat16 [8192, 64, 128], P(('lat', 'lon')), may hold values from -16 to 16
- weight_blocks: bfloat16 [8192, 128, 128], P(('lat', 'lon')), may hold values from -0.5 to 0.5
- pair_source: int32 [8192], P(('lat', 'lon')), may hold values from 0 to 255
- pair_target: int32 [8192, 1], P(('lat', 'lon')), may hold values from 0 to 7; in each aligned block of 256 rows (0 to 255, 256 to 511, ...) at most 64 rows name the same one
- pair_block: int32 [8192], P(('lat', 'lon')), may hold values from 0 to 255
Outputs:
- correlation: float32 [256, 4096], P('lat', 'lon')
The draws below stay inside these ranges and needn't reach their ends.
Inputs may be any that keep to these rules, and one draw needn't show every extreme that they name: `pair_target`: among the rows of one device, no longitude tile is named by more than 64 pairs, a bound that some block reaches of them.
All inputs are finite; a program needn't handle non-finite values.
Results may differ from the reference program's by a relative error of at most 0.0006.
Values may be sent and summed in bfloat16 or wider, within the bound.
No kernel may reach another device: no remote copies, remote signals or barrier semaphores. Data moves between devices by JAX's collectives and lax.ppermute only.
A program may use at most 128 MiB of HBM per device.

```python
import math
import jax
import jax.numpy as jnp
import numpy as np
from jax import lax

DAYS = 32
CELL_BLK = 128
WINDOW_HALF = 16
LAT_DEV = 64
LON_DEV = 512
PAIRS_DEV = 256
CAP = 64
SRC_BLK = 256
SRC_BLOCKS = 8192
PAIRS = 8192
N_LAT = 4
N_LON = 8


def draw_source_fields(key, part):
    first, second, third = jax.random.split(jax.random.fold_in(key, 4711), 3)
    shape = (SRC_BLOCKS, DAYS, CELL_BLK)
    temper = jnp.clip(jax.random.normal(first, shape, jnp.float32), -5.0, 5.0)
    slope = jax.random.uniform(second, (SRC_BLOCKS, 1, 1), jnp.float32, -1.0, 2.0)
    noise = jnp.clip(jax.random.normal(third, shape, jnp.float32), -5.0, 5.0)
    moist = slope * temper + noise
    return jnp.concatenate([temper, moist], axis=1).astype(jnp.bfloat16)


def plant(values, stream_key, low, high):
    extent = values.shape
    index_at = [jax.random.randint(jax.random.fold_in(stream_key, axis), (), 0, extent[axis]) for axis in range(len(extent))]
    values = values.at[tuple(index_at)].set(low)
    longest = extent.index(max(extent))
    index_at[longest] = (index_at[longest] + 1) % extent[longest]
    return values.at[tuple(index_at)].set(high)


def levels(rng, dims, shards, low, largest):
    def one(dim, shards_of):
        draws = jax.random.uniform(jax.random.fold_in(jax.random.fold_in(rng, 6), dim), (shards_of,), jnp.float32, low / len(shards), largest / len(shards))
        return jnp.repeat(jnp.exp(draws), dims[dim] // shards_of).reshape((-1,) + (1,) * (len(dims) - dim - 1))

    factor_of = one(*shards[0])
    for cut in shards[1:]:
        factor_of = factor_of * one(*cut)
    return factor_of


def assign_block(rng, own, number, rows, count, top, limit, lean):
    order = jax.random.permutation(rng, count)
    heavy_load, usual = load_shares(count, rows * top, limit, lean, True), load_shares(count, rows * top, limit, lean, False)
    places = jnp.arange(count)

    def named(tallies, offset_by):
        used = int((tallies > 0).sum())
        fixed = max(1, used // 4)
        moved = fixed + (places - fixed + offset_by * (used - fixed)) % max(1, count - fixed)
        return jnp.zeros((count,), jnp.int32).at[order[jnp.where(places < fixed, places, moved)]].set(jnp.asarray(tallies, jnp.int32))

    tallies = jnp.where(number % 4 == 0, named(heavy_load, number // 4), named(usual, number - number // 4 - 1))
    mixed = jax.random.permutation(jax.random.fold_in(own, 3), count)
    source_of, sink = mixed[0:count // 2 * 2:2], mixed[1:count // 2 * 2:2]
    slack = jnp.minimum(tallies[source_of] - 1, limit - tallies[sink]) // 2
    slack = jnp.where((source_of == order[0]) | (sink == order[0]) | (tallies[sink] == 0), 0, jnp.maximum(slack, 0))
    moved = jax.random.randint(jax.random.fold_in(own, 4), (count // 2,), 0, 1 << 20) % (slack + 1)
    tallies = tallies.at[source_of].add(-moved).at[sink].add(moved)
    items = jnp.searchsorted(jnp.cumsum(tallies), jnp.arange(rows * top), side="right").astype(jnp.int32)
    table = items.reshape(top, rows).T
    table = table[jax.random.permutation(jax.random.fold_in(own, 1), rows)]
    offset_by = jax.random.randint(jax.random.fold_in(own, 2), (rows, 1), 0, top)
    return jnp.take_along_axis(table, (jnp.arange(top)[None, :] + offset_by) % top, axis=1)


def load_shares(count, total, reach, lean, full):
    weights = [(1 << 20) // math.isqrt(rank ** lean) + 1 for rank in range(1, count + 1)]
    largest = reach if full else min(reach, max(-(-total // count), total * weights[0] // sum(weights)))
    least = 1 if total - largest >= count - 1 else 0
    given, rest = [largest] + [least] * (count - 1), total - largest - least * (count - 1)
    while rest > 0:
        candidates = [i for i in range(1, count) if given[i] < largest] or [i for i in range(1, count) if given[i] < reach]
        pool, left = sum([weights[i] for i in candidates]), rest
        for i in candidates:
            extra = min(reach - given[i], max(1, left * weights[i] // pool), rest)
            given[i] = given[i] + extra
            rest = rest - extra
    return np.array(given)


def centred(rng, dims, deviation, reach, shards=(), held_as=jnp.bfloat16):
    result = deviation * jax.random.normal(rng, dims, jnp.float32)
    if shards:
        result = result * levels(rng, dims, shards, -0.22, 0.18)
    return jnp.clip(result, -reach, reach).astype(held_as)


def setup_inputs(seed: int = 0) -> dict:
    splits = jax.random.split(jax.random.key(seed), 6)
    source_fields = draw_source_fields(jax.random.fold_in(splits[5], 71), 0)
    weight_blocks = centred(splits[1], (PAIRS, CELL_BLK, CELL_BLK), CELL_BLK ** -0.5, 0.5, ((0, 32),))
    pair_source = plant(jax.random.randint(splits[2], (PAIRS,), 0, SRC_BLK), jax.random.fold_in(splits[2], 1), 0, SRC_BLK - 1).astype(jnp.int32)
    pair_target_keys = jax.random.split(jax.random.fold_in(splits[3], 1), PAIRS // PAIRS_DEV)
    pair_target_turns = jax.random.permutation(jax.random.fold_in(splits[3], 3), PAIRS // PAIRS_DEV)
    pair_target = jax.vmap(lambda own, number: assign_block(jax.random.fold_in(splits[3], 2), own, number, PAIRS_DEV, N_LON, 1, CAP, 1))(pair_target_keys, pair_target_turns).reshape((PAIRS, 1))
    pair_block = plant(jax.random.randint(splits[4], (PAIRS,), 0, SRC_BLK), jax.random.fold_in(splits[4], 1), 0, SRC_BLK - 1).astype(jnp.int32)
    return {"source_fields": source_fields, "weight_blocks": weight_blocks, "pair_source": pair_source, "pair_target": pair_target, "pair_block": pair_block}


def gaussian_taps():
    offsets = jnp.arange(2 * WINDOW_HALF + 1).astype(jnp.float32) - WINDOW_HALF
    return jnp.exp(-offsets * offsets / (0.5 * WINDOW_HALF * WINDOW_HALF))

def reference(source_fields, weight_blocks, pair_source, pair_target, pair_block):
    devices = N_LAT * N_LON
    blocks_dev = LAT_DEV * LON_DEV // CELL_BLK
    channels = 2 * DAYS
    sources = source_fields.reshape(devices, blocks_dev, channels, CELL_BLK)
    weights = weight_blocks.reshape(devices, PAIRS_DEV, CELL_BLK, CELL_BLK)
    anchors = pair_source.reshape(devices, PAIRS_DEV)
    targets = pair_target.reshape(devices, PAIRS_DEV)
    places = pair_block.reshape(devices, PAIRS_DEV)

    def deliver(total, item):
        device, block_set, weight_set, anchor, target, place = item
        picked = block_set[anchor].astype(jnp.float32)
        terms = jnp.einsum('pck,pjk->pcj', picked, weight_set.astype(jnp.float32), precision=lax.Precision.HIGHEST)
        row = (device // N_LON * N_LON + target) * blocks_dev + place
        return (total.at[row.astype(jnp.int32)].add(terms), None)
    start = jnp.zeros((devices * blocks_dev, channels, CELL_BLK), jnp.float32)
    remapped, _ = lax.scan(deliver, start, (jnp.arange(devices, dtype=jnp.int32), sources, weights, anchors, targets, places))
    temper = remapped[:, :DAYS]
    moist = remapped[:, DAYS:]
    moments = jnp.stack([temper.sum(1), moist.sum(1), (temper * temper).sum(1), (moist * moist).sum(1), (temper * moist).sum(1)])
    height = LAT_DEV * N_LAT
    width = LON_DEV * N_LON
    moments = moments.reshape(5, N_LAT, N_LON, LAT_DEV, LON_DEV).transpose(0, 1, 3, 2, 4).reshape(5, height, width)
    kernel = gaussian_taps()
    padded = jnp.concatenate([moments[:, :, width - WINDOW_HALF:], moments, moments[:, :, :WINDOW_HALF]], axis=2)
    along = jnp.zeros_like(moments)
    for offset in range(2 * WINDOW_HALF + 1):
        along = along + kernel[offset] * padded[:, :, offset:offset + width]
    padded = jnp.pad(along, ((0, 0), (WINDOW_HALF, WINDOW_HALF), (0, 0)))
    smoothed = jnp.zeros_like(moments)
    for offset in range(2 * WINDOW_HALF + 1):
        smoothed = smoothed + kernel[offset] * padded[:, offset:offset + height, :]
    rows = jnp.arange(height, dtype=jnp.int32)[:, None] + jnp.arange(2 * WINDOW_HALF + 1, dtype=jnp.int32)[None, :] - WINDOW_HALF
    inside = ((rows >= 0) & (rows < height)).astype(jnp.float32)
    lat_total = lax.optimization_barrier(jnp.sum(inside * kernel[None, :], axis=1))
    weight_total = lat_total[:, None] * (jnp.sum(kernel) * DAYS)
    mean_temper = smoothed[0] / weight_total
    mean_moist = smoothed[1] / weight_total
    var_temper = smoothed[2] / weight_total - mean_temper * mean_temper
    var_moist = smoothed[3] / weight_total - mean_moist * mean_moist
    covar = smoothed[4] / weight_total - mean_temper * mean_moist
    return covar / jnp.sqrt(var_temper * var_moist + 1e-06)
```

```python
import functools

import jax
import jax.numpy as jnp
from jax import lax
from jax.experimental import pallas as pl
from jax.experimental.pallas import tpu as pltpu
from jax.sharding import PartitionSpec as P

WINDOW_HALF = 16
LAT_DEV = 64
LON_DEV = 512
LANES = 128
RING = 32
GROUP = 8
CHUNK = 16
F32 = jnp.float32
BF16 = jnp.bfloat16
I32 = jnp.int32


def padded(x, sides, width, wrap):
    for axis, dim in sides:
        count, length = (lax.axis_size(axis), x.shape[dim])
        up = [(i, (i + 1) % count) for i in range(count if wrap else count - 1)]
        down = [(j, i) for i, j in up]
        last = lax.slice_in_dim(x, length - width, length, axis=dim)
        leading = lax.slice_in_dim(x, 0, width, axis=dim)
        before = lax.ppermute(last, axis, up)
        after = lax.ppermute(leading, axis, down)
        x = jnp.concatenate([before, x, after], axis=dim)
    return x


def gaussian_taps():
    offsets = jnp.arange(2 * WINDOW_HALF + 1).astype(jnp.float32) - WINDOW_HALF
    return jnp.exp(-offsets * offsets / (0.5 * WINDOW_HALF * WINDOW_HALF))


def band_matrix(length):
    outer = jnp.arange(length + 2 * WINDOW_HALF, dtype=jnp.int32)[:, None]
    inner = jnp.arange(length, dtype=jnp.int32)[None, :]
    offsets = (outer - inner - WINDOW_HALF).astype(jnp.float32)
    values = jnp.exp(-offsets * offsets / (0.5 * WINDOW_HALF * WINDOW_HALF))
    return jnp.where(jnp.abs(offsets) <= WINDOW_HALF, values, 0.0)


def smooth_lon(fields, lon_band):
    return jnp.einsum("krb,bj->krj", fields, lon_band, precision=lax.Precision.HIGHEST)


def smooth_lat(fields, lat_band):
    return jnp.einsum("ai,kaj->kij", lat_band, fields, precision=lax.Precision.HIGHEST)


def iota(shape, dim):
    return lax.broadcasted_iota(I32, shape, dim)


def dot(a, b, dims=((1,), (0,)), exact=False):
    return lax.dot_general(
        a,
        b,
        (dims, ((), ())),
        preferred_element_type=F32,
        precision=lax.Precision.HIGHEST if exact else None,
    )


def repeat(count, body, carry):
    if count <= 8:
        for step in range(count):
            carry = body(step, carry)
        return carry
    return lax.fori_loop(0, count, body, carry)


def one_hots(row, height):
    pairs = row.shape[1]
    high = (iota((height, pairs), 0) == (row >> 7)).astype(F32)
    low = (iota((LANES, pairs), 0) == (row & (LANES - 1))).astype(F32)
    return high, low


def look_up(table, high, low):
    return jnp.sum(dot(table, low, exact=True) * high, axis=0, keepdims=True)


def plan_kernel(
    count, blocks, cap, mcap, me_ref, keys_ref, src_ref, table_ref, entry_ref, spot_ref, pres
):
    me = me_ref[0]
    pairs = keys_ref.shape[1]
    height = count * blocks // LANES
    tile_rows = blocks // LANES
    sends = count * cap

    def held(d, carry):
        high, low = one_hots(keys_ref[pl.ds(d, 1), :], height)
        found = dot(high.astype(BF16), low.astype(BF16), ((1,), (1,)))
        pres[d] = (found > 0.5).astype(F32)
        return carry

    repeat(count, held, 0)

    row_at = iota((height, LANES), 0)
    turn = (row_at * LANES + iota((height, LANES), 1)) % count

    zero = jnp.zeros((height, LANES), F32)
    holders = repeat(count, lambda d, total: total + pres[d], zero)

    def choose(d, carry):
        best, owner = carry
        rank = (d - turn + count) % count
        rank = jnp.where(pres[d] > 0.5, rank, 4 * count)
        better = rank < best
        return jnp.where(better, rank, best), jnp.where(better, d, owner)

    _, owner = repeat(
        count,
        choose,
        (jnp.full((height, LANES), 4 * count, I32), jnp.full((height, LANES), -1, I32)),
    )

    ahead = (iota((LANES, LANES), 0) < iota((LANES, LANES), 1)).astype(BF16)
    ones = jnp.ones((LANES, LANES), BF16)
    ahead_total = jnp.concatenate([ahead, ones], axis=1)
    up, down = iota((height, height), 1), iota((height, height), 0)
    rows_ahead = (up < down).astype(BF16)
    same_tile = ((up < down) & (up // tile_rows == down // tile_rows)).astype(BF16)

    def prefix(mask, rows):
        both = dot(mask.astype(BF16), ahead_total)
        return both[:, :LANES] + dot(rows, both[:, LANES:].astype(BF16))

    mine = (owner == me).astype(F32)
    several = mine * (holders > 1.5).astype(F32)
    single = mine - several
    rank_several = prefix(several, rows_ahead)
    rank_single = prefix(single, rows_ahead)
    total_several = jnp.sum(several, axis=(0, 1), keepdims=True)
    total_mine = jnp.sum(mine, axis=(0, 1), keepdims=True)
    held_here = pres[me]
    entry_rows = entry_ref.shape[0] - 8
    lane_at = iota((entry_rows, LANES), 1)
    first_lane = iota((8, LANES), 1)

    def route(d, carry):
        place, finished, most, entries, counts = carry
        away = jnp.where(d == me, 0.0, 1.0)
        theirs = (owner == d).astype(F32)
        rank_theirs = prefix(theirs, same_tile)
        base = lax.convert_element_type(d, F32) if not isinstance(d, int) else float(d)
        finished = finished + theirs * (base * mcap + rank_theirs + 1.0)
        most = jnp.maximum(most, theirs * (rank_theirs + 1.0))
        leaving = held_here * theirs * away
        rank_leaving = prefix(leaving, rows_ahead)
        place = place + leaving * (base * cap + rank_leaving + 1.0)
        coming = pres[d] * mine * away
        rank_coming = prefix(coming, rows_ahead)
        code = coming * (rank_coming * 1024.0 + rank_several + 1.0)
        high, low = one_hots(keys_ref[pl.ds(d, 1), :], height)
        seen = (look_up(code, high, low) + 0.5).astype(I32) - 1
        rank, local = seen >> 10, seen & 1023
        hit = iota((entry_rows, pairs), 0) == rank
        column = jnp.max(jnp.where(hit, local, -1), axis=1, keepdims=True)
        entries = jnp.where(lane_at == d, column, entries)
        arrivals = jnp.sum(coming, axis=(0, 1), keepdims=True).astype(I32)
        counts = jnp.where(first_lane == d, arrivals, counts)
        return place, finished, most, entries, counts

    place, finished, most, entries, counts = repeat(
        count,
        route,
        (
            zero,
            zero,
            zero,
            jnp.full((entry_rows, LANES), -1, I32),
            jnp.zeros((8, LANES), I32),
        ),
    )
    entry_ref[:entry_rows, :] = entries
    entry_ref[entry_rows:, :] = counts

    pick = (iota((8, height), 1) == me * tile_rows + iota((8, height), 0)).astype(F32)
    spot_ref[...] = (dot(pick, finished, exact=True) + 0.5).astype(I32) - 1

    wide = -(-count // 8) * 8
    which = iota((wide, LANES), 0)
    which_one = iota((wide, 1), 0)

    def load_of(s, worst):
        here = pres[s]

        def into(d, sums):
            part = jnp.sum(here * (owner == d).astype(F32), axis=0, keepdims=True)
            return jnp.where(which == d, part, sums)

        sums = repeat(count, into, jnp.zeros((wide, LANES), F32))
        loads = jnp.sum(sums, axis=1, keepdims=True)
        return jnp.maximum(worst, jnp.where(which_one == s, 0.0, loads))

    worst = repeat(count, load_of, jnp.zeros((wide, 1), F32))
    worst = jnp.max(worst, axis=0, keepdims=True)
    most = jnp.max(jnp.max(most, axis=1, keepdims=True), axis=0, keepdims=True)
    over = jnp.where((worst > cap + 0.5) | (most > mcap + 0.5), 1, 0)

    place = place + several * (sends + rank_several + 1.0)
    place = place + single * (sends + total_several + rank_single + 1.0)
    tile_of = (row_at // tile_rows).astype(F32)
    moment_place = mine * (tile_of * mcap + finished - 1.0 - me.astype(F32) * mcap)
    high, low = one_hots(keys_ref[pl.ds(me, 1), :], height)
    goes = look_up(place, high, low) - 1.0
    lands = look_up(moment_place, high, low)
    leaves = (goes < sends - 0.5).astype(F32)
    square = (iota((pairs, pairs), 0) < iota((pairs, pairs), 1)).astype(BF16)
    before = dot(jnp.broadcast_to(leaves, (8, pairs)).astype(BF16), square)[0:1, :]
    leaving = jnp.sum(leaves, axis=1, keepdims=True)
    at = iota((1, pairs), 1).astype(F32)
    position = jnp.where(leaves > 0.5, before, leaving + at - before)
    kind = iota((8, pairs), 0)
    values = jnp.where(
        kind == 0,
        at,
        jnp.where(kind == 1, goes, jnp.where(kind == 2, src_ref[...].astype(F32), 0.0)),
    )
    column_at = iota((pairs, pairs), 0)
    order = (column_at == (position + 0.5).astype(I32)).astype(F32)
    ordered = dot(values, order, ((1,), (1,)), exact=True)
    slot = jnp.where(leaves > 0.5, -1, (goes - sends + 0.5).astype(I32))
    in_slot = (column_at == slot).astype(F32)
    weighed = jnp.where(kind == 0, lands, 1.0)
    summed = dot(weighed, in_slot, ((1,), (1,)), exact=True)
    landing = summed[0:1, :] / jnp.maximum(summed[1:2, :], 1.0)
    result = (ordered + 0.5).astype(I32)
    result = jnp.where(kind == 3, (landing + 0.25).astype(I32), result)
    lane = iota((8, pairs), 1)
    facts = jnp.where(
        lane == 0,
        leaving.astype(I32),
        jnp.where(
            lane == 1,
            total_mine.astype(I32),
            jnp.where(lane == 2, total_several.astype(I32), over),
        ),
    )
    table_ref[...] = jnp.where(kind == 4, facts, result)


def make_plan(keys, pair_source, count, blocks, cap, mcap):
    pairs = keys.shape[1]
    height = count * blocks // LANES
    entry_rows = -(-cap // 8) * 8 + 8
    vmem = pl.BlockSpec(memory_space=pltpu.VMEM)
    return pl.pallas_call(
        functools.partial(plan_kernel, count, blocks, cap, mcap),
        out_shape=(
            jax.ShapeDtypeStruct((8, pairs), I32),
            jax.ShapeDtypeStruct((entry_rows, LANES), I32),
            jax.ShapeDtypeStruct((8, LANES), I32),
        ),
        in_specs=[pl.BlockSpec(memory_space=pltpu.SMEM), vmem, vmem],
        out_specs=(vmem, vmem, vmem),
        scratch_shapes=[pltpu.VMEM((count, height, LANES), F32)],
        name="plan",
    )(lax.axis_index("lon").astype(I32)[None], keys, pair_source[None, :])


def pair_copies(table, src, weights, xs, ws, x_sem, w_sem, i):
    slot = i % RING
    return (
        pltpu.make_async_copy(src.at[table[2, i]], xs.at[slot], x_sem.at[slot]),
        pltpu.make_async_copy(weights.at[table[0, i]], ws.at[slot], w_sem.at[slot]),
    )


def products(table, src, weights, xs, ws, x_sem, w_sem, low, high, target, first, last, dummy, while_loading):
    copies = functools.partial(pair_copies, table, src, weights, xs, ws, x_sem, w_sem)

    def start(i):
        for copy in copies(i):
            copy.start()

    def prime(i, carry):
        @pl.when(i < high)
        def _():
            start(i)

        return carry

    lax.fori_loop(low, low + RING, prime, 0)
    while_loading()

    def step(g, carry):
        base = g * GROUP
        for u in range(GROUP):
            for copy in copies(base + u):
                copy.wait()
        results = []
        for u in range(GROUP):
            slot = (base + u) % RING
            results.append(dot(xs[slot], ws[slot], ((1,), (1,))))
        for u in range(GROUP):
            place = table[1, base + u]
            inside = (place >= first) & (place < last)
            where = jnp.where(inside, place - first, dummy)
            target[where] = target[where] + results[u]

        @pl.when(base + RING < high)
        def _():
            for u in range(GROUP):
                start(base + RING + u)

        return carry

    lax.fori_loop(low // GROUP, high // GROUP, step, 0)


def send_kernel(sends, table, src, weights, out_ref, total, xs, ws, x_sem, w_sem):
    leaving = table[4, 0]
    high = (leaving + GROUP - 1) // GROUP * GROUP

    def clear():
        def one(i, carry):
            total[i] = jnp.zeros(total.shape[1:], F32)
            return carry

        lax.fori_loop(0, sends, one, 0)

    products(
        table, src, weights, xs, ws, x_sem, w_sem, 0, high, total, 0, sends, sends, clear
    )

    def finish(i, carry):
        out_ref[i] = total[i].astype(BF16)
        return carry

    lax.fori_loop(0, sends, finish, 0)


def moment_rows(value):
    days = value.shape[0] // 2
    temper, moist = value[:days], value[days:]
    return [
        jnp.sum(each, axis=0, keepdims=True)
        for each in (temper, moist, temper * temper, moist * moist, temper * moist)
    ]


def put_moments(table, total, moments, spare, begin, end):
    def some(g, carry):
        for u in range(4):
            i = begin + g * 4 + u
            good = i < end
            at = jnp.where(good, i, 0)
            place = jnp.where(good, table[3, at], spare)
            for k, row in enumerate(moment_rows(total[at])):
                moments[k, pl.ds(place, 1), :] = row
        return carry

    lax.fori_loop(0, (end - begin + 3) // 4, some, 0)


def chunk_copies(source, target, sem, c):
    rows = pl.ds(c * CHUNK, CHUNK)
    return pltpu.make_async_copy(source.at[rows], target.at[rows], sem.at[c])


def local_kernel(
    sends, table, src, weights, local_ref, moments, total, xs, ws, x_sem, w_sem, out_sem
):
    pairs = weights.shape[0]
    leaving, owned, several = table[4, 0], table[4, 1], table[4, 2]
    low = leaving // GROUP * GROUP

    def clear():
        def one(i, carry):
            total[i] = jnp.zeros(total.shape[1:], F32)
            return carry

        lax.fori_loop(0, owned, one, 0)
        moments[...] = jnp.zeros(moments.shape, F32)

    products(
        table,
        src,
        weights,
        xs,
        ws,
        x_sem,
        w_sem,
        low,
        pairs,
        total,
        sends,
        sends + pairs,
        pairs,
        clear,
    )
    chunks = (several + CHUNK - 1) // CHUNK

    def begin(c, carry):
        chunk_copies(total, local_ref, out_sem, c).start()
        return carry

    lax.fori_loop(0, chunks, begin, 0)
    put_moments(table, total, moments, moments.shape[1] - 8, several, owned)

    def end(c, carry):
        chunk_copies(total, local_ref, out_sem, c).wait()
        return carry

    lax.fori_loop(0, chunks, end, 0)


def merge_kernel(
    count, cap, mcap, table, entry, local_ref, came, moments_in, out_ref, total, moments, in_sem
):
    several = table[4, 2]
    spare = total.shape[0] - 1
    counts_row = entry.shape[0] - 8
    chunks = (several + CHUNK - 1) // CHUNK

    def begin(c, carry):
        chunk_copies(local_ref, total, in_sem, c).start()
        return carry

    lax.fori_loop(0, chunks, begin, 0)
    moments[...] = moments_in[...]

    def end(c, carry):
        chunk_copies(local_ref, total, in_sem, c).wait()
        return carry

    lax.fori_loop(0, chunks, end, 0)

    def from_one(s, carry):
        number = entry[counts_row, s]

        def some(g, inner):
            for u in range(4):
                r = g * 4 + u
                good = r < number
                at = jnp.where(good, r, 0)
                where = jnp.where(good, entry[at, s], spare)
                total[where] = total[where] + came[s * cap + at].astype(F32)
            return inner

        lax.fori_loop(0, (number + 3) // 4, some, 0)
        return carry

    lax.fori_loop(0, count, from_one, 0)
    put_moments(table, total, moments, moments.shape[1] - 8, 0, several)
    for o in range(count):
        for k in range(5):
            out_ref[o, k] = moments[k, o * mcap : (o + 1) * mcap, :].astype(BF16)


def spread_kernel(count, mcap, spot_ref, came, map_ref, flat):
    rows, blocks_wide = map_ref.shape[1], map_ref.shape[2] // LANES
    for a in range(count):
        for k in range(5):
            flat[a * mcap : (a + 1) * mcap, k * LANES : (k + 1) * LANES] = came[a, k]
    chosen = (iota((spot_ref.shape[0], count * mcap), 1) == spot_ref[...]).astype(F32)
    laid = dot(chosen.astype(BF16), flat[...])
    for q in range(blocks_wide):
        for k in range(5):
            map_ref[k, :, q * LANES : (q + 1) * LANES] = laid[
                q * rows : (q + 1) * rows, k * LANES : (k + 1) * LANES
            ].astype(BF16)


def direct(cap, mcap, source_fields, weight_blocks, table, entry, spot):
    count = lax.axis_size("lon")
    blocks, channels, cells = source_fields.shape
    pairs = weight_blocks.shape[0]
    sends = count * cap
    smem = pl.BlockSpec(memory_space=pltpu.SMEM)
    vmem = pl.BlockSpec(memory_space=pltpu.VMEM)
    hbm = pl.BlockSpec(memory_space=pl.ANY)
    buffers = [
        pltpu.VMEM((RING, channels, cells), BF16),
        pltpu.VMEM((RING, cells, cells), BF16),
        pltpu.SemaphoreType.DMA((RING,)),
        pltpu.SemaphoreType.DMA((RING,)),
    ]
    packed = pl.pallas_call(
        functools.partial(send_kernel, sends),
        out_shape=jax.ShapeDtypeStruct((sends, channels, cells), BF16),
        in_specs=[smem, hbm, hbm],
        out_specs=vmem,
        scratch_shapes=[pltpu.VMEM((sends + 1, channels, cells), F32)] + buffers,
        name="leaving",
    )(table, source_fields, weight_blocks)
    came = lax.all_to_all(
        packed.reshape(count, cap, channels, cells), "lon", split_axis=0, concat_axis=0, tiled=True
    ).reshape(sends, channels, cells)
    chunk_count = -(-pairs // CHUNK)
    local, moments = pl.pallas_call(
        functools.partial(local_kernel, sends),
        out_shape=(
            jax.ShapeDtypeStruct((pairs, channels, cells), F32),
            jax.ShapeDtypeStruct((5, count * mcap + 8, cells), F32),
        ),
        in_specs=[smem, hbm, hbm],
        out_specs=(hbm, vmem),
        scratch_shapes=[pltpu.VMEM((pairs + 1, channels, cells), F32)]
        + buffers
        + [pltpu.SemaphoreType.DMA((chunk_count,))],
        name="staying",
    )(table, source_fields, weight_blocks)
    finished = pl.pallas_call(
        functools.partial(merge_kernel, count, cap, mcap),
        out_shape=jax.ShapeDtypeStruct((count, 5, mcap, cells), BF16),
        in_specs=[smem, smem, hbm, vmem, vmem],
        out_specs=vmem,
        scratch_shapes=[
            pltpu.VMEM((pairs + 1, channels, cells), F32),
            pltpu.VMEM((5, count * mcap + 8, cells), F32),
            pltpu.SemaphoreType.DMA((chunk_count,)),
        ],
        name="merge",
    )(table, entry, local, came, moments)
    arrived = lax.all_to_all(finished, "lon", split_axis=0, concat_axis=0, tiled=True)
    wide = LON_DEV // cells
    where = spot.reshape(-1)[:blocks].reshape(LAT_DEV, wide).T.reshape(blocks, 1)
    return pl.pallas_call(
        functools.partial(spread_kernel, count, mcap),
        out_shape=jax.ShapeDtypeStruct((5, LAT_DEV, LON_DEV), BF16),
        in_specs=[vmem, vmem],
        out_specs=vmem,
        scratch_shapes=[pltpu.VMEM((count * mcap, 5 * cells), BF16)],
        name="spread",
    )(where, arrived)


def padded_exchange(source_fields, weight_blocks, pair_source, targets, pair_block):
    lon_count = lax.axis_size("lon")
    pair_count = pair_source.shape[0]
    capacity = max(2, 2 * pair_count // lon_count)
    blocks_dev, channels, cell_count = source_fields.shape
    lanes = jnp.arange(lon_count, dtype=jnp.int32)
    matches = (targets[:, None] == lanes[None, :]).astype(jnp.int32)
    earlier = jnp.cumsum(matches, axis=0) - matches
    slots = jnp.sum(earlier * matches, axis=1)
    position = targets * capacity + slots
    outgoing = jnp.zeros((lon_count * capacity,), jnp.int32).at[position].set(pair_block)
    arriving = lax.all_to_all(
        outgoing.reshape(lon_count, capacity), "lon", split_axis=0, concat_axis=0, tiled=True
    )
    picked = source_fields[pair_source]
    terms = jnp.einsum("pck,pjk->pcj", picked, weight_blocks, preferred_element_type=jnp.float32)
    packed = (
        jnp.zeros((lon_count * capacity, channels, cell_count), jnp.float32).at[position].set(terms)
    )
    received = lax.all_to_all(
        packed.reshape(lon_count, capacity, channels, cell_count).astype(jnp.bfloat16),
        "lon",
        split_axis=0,
        concat_axis=0,
        tiled=True,
    ).astype(jnp.float32)
    remapped = jax.ops.segment_sum(
        received.reshape(lon_count * capacity, channels, cell_count),
        arriving.reshape(-1),
        num_segments=blocks_dev,
    )
    days = channels // 2
    temper = remapped[:, :days]
    moist = remapped[:, days:]
    moments = jnp.stack(
        [
            temper.sum(1),
            moist.sum(1),
            (temper * temper).sum(1),
            (moist * moist).sum(1),
            (temper * moist).sum(1),
        ]
    )
    return moments.reshape(5, LAT_DEV, LON_DEV).astype(BF16)


def local(source_fields, weight_blocks, pair_source, pair_target, pair_block):
    count = lax.axis_size("lon")
    blocks, channels, _ = source_fields.shape
    days = channels // 2
    pairs = pair_source.shape[0]
    share = -(-pairs // count)
    cap = share
    mcap = -(-share * 3 // 2 // 16) * 16
    targets = pair_target[:, 0]
    keys = targets * blocks + pair_block
    all_keys = lax.all_to_all(
        jnp.broadcast_to(keys[None, :], (count, pairs)), "lon", split_axis=0, concat_axis=0, tiled=True
    )
    table, entry, spot = make_plan(all_keys, pair_source, count, blocks, cap, mcap)
    moments = lax.cond(
        table[4, 3] == 0,
        lambda: direct(cap, mcap, source_fields, weight_blocks, table, entry, spot),
        lambda: padded_exchange(source_fields, weight_blocks, pair_source, targets, pair_block),
    )
    lon_band = band_matrix(LON_DEV)
    lat_band = band_matrix(LAT_DEV)
    taller = padded(moments, (("lat", 1),), WINDOW_HALF, False)
    wider = padded(taller, (("lon", 2),), WINDOW_HALF, True).astype(F32)
    smoothed = smooth_lat(smooth_lon(wider, lon_band), lat_band)
    kernel = gaussian_taps()
    height = LAT_DEV * lax.axis_size("lat")
    rows = (
        lax.axis_index("lat") * LAT_DEV
        + jnp.arange(LAT_DEV, dtype=jnp.int32)[:, None]
        + jnp.arange(2 * WINDOW_HALF + 1, dtype=jnp.int32)[None, :]
        - WINDOW_HALF
    )
    inside = ((rows >= 0) & (rows < height)).astype(jnp.float32)
    lat_total = jnp.sum(inside * kernel[None, :], axis=1)
    weight_total = lat_total[:, None] * (jnp.sum(kernel) * days)
    mean_temper = smoothed[0] / weight_total
    mean_moist = smoothed[1] / weight_total
    var_temper = smoothed[2] / weight_total - mean_temper * mean_temper
    var_moist = smoothed[3] / weight_total - mean_moist * mean_moist
    covar = smoothed[4] / weight_total - mean_temper * mean_moist
    return covar / jnp.sqrt(var_temper * var_moist + 1e-06)


def solution(mesh):
    placed = (
        P(("lat", "lon"), None, None),
        P(("lat", "lon"), None, None),
        P(("lat", "lon")),
        P(("lat", "lon"), None),
        P(("lat", "lon")),
    )
    return jax.shard_map(
        local, mesh=mesh, in_specs=placed, out_specs=P("lat", "lon"), check_vma=False
    )
```

```python
import functools

import jax
import jax.numpy as jnp
from jax import lax
from jax.experimental import pallas as pl
from jax.experimental.pallas import tpu as pltpu
from jax.sharding import PartitionSpec as P

WINDOW_HALF = 16
LAT_DEV = 64
LON_DEV = 512
LANES = 128
RING = 32
GROUP = 8
CHUNK = 16
F32 = jnp.float32
BF16 = jnp.bfloat16
I32 = jnp.int32


def padded(x, sides, width, wrap):
    for axis, dim in sides:
        count, length = (lax.axis_size(axis), x.shape[dim])
        up = [(i, (i + 1) % count) for i in range(count if wrap else count - 1)]
        down = [(j, i) for i, j in up]
        last = lax.slice_in_dim(x, length - width, length, axis=dim)
        leading = lax.slice_in_dim(x, 0, width, axis=dim)
        before = lax.ppermute(last, axis, up)
        after = lax.ppermute(leading, axis, down)
        x = jnp.concatenate([before, x, after], axis=dim)
    return x


def gaussian_taps():
    offsets = jnp.arange(2 * WINDOW_HALF + 1).astype(jnp.float32) - WINDOW_HALF
    return jnp.exp(-offsets * offsets / (0.5 * WINDOW_HALF * WINDOW_HALF))


def band_matrix(length):
    outer = jnp.arange(length + 2 * WINDOW_HALF, dtype=jnp.int32)[:, None]
    inner = jnp.arange(length, dtype=jnp.int32)[None, :]
    offsets = (outer - inner - WINDOW_HALF).astype(jnp.float32)
    values = jnp.exp(-offsets * offsets / (0.5 * WINDOW_HALF * WINDOW_HALF))
    return jnp.where(jnp.abs(offsets) <= WINDOW_HALF, values, 0.0)


def smooth_lon(fields, lon_band):
    return jnp.einsum("krb,bj->krj", fields, lon_band, precision=lax.Precision.HIGHEST)


def smooth_lat(fields, lat_band):
    return jnp.einsum("ai,kaj->kij", lat_band, fields, precision=lax.Precision.HIGHEST)


def iota(shape, dim):
    return lax.broadcasted_iota(I32, shape, dim)


def dot(a, b, dims=((1,), (0,)), exact=False):
    return lax.dot_general(
        a,
        b,
        (dims, ((), ())),
        preferred_element_type=F32,
        precision=lax.Precision.HIGHEST if exact else None,
    )


def repeat(count, body, carry):
    if count <= 8:
        for step in range(count):
            carry = body(step, carry)
        return carry
    return lax.fori_loop(0, count, body, carry)


def one_hots(row, height):
    pairs = row.shape[1]
    high = (iota((height, pairs), 0) == (row >> 7)).astype(F32)
    low = (iota((LANES, pairs), 0) == (row & (LANES - 1))).astype(F32)
    return high, low


def look_up(table, high, low):
    return jnp.sum(dot(table, low, exact=True) * high, axis=0, keepdims=True)


def plan_kernel(
    count, blocks, cap, mcap, me_ref, keys_ref, src_ref, table_ref, entry_ref, spot_ref, pres, tall
):
    me = me_ref[0]
    pairs = keys_ref.shape[1]
    height = count * blocks // LANES
    tile_rows = blocks // LANES
    sends = count * cap

    def held(d, carry):
        high, low = one_hots(keys_ref[pl.ds(d, 1), :], height)
        found = dot(high.astype(BF16), low.astype(BF16), ((1,), (1,)))
        found = (found > 0.5).astype(F32)
        pres[d] = found
        tall[pl.ds(d, height, stride=count), :] = found
        return carry

    repeat(count, held, 0)

    row_at = iota((height, LANES), 0)
    zero = jnp.zeros((height, LANES), F32)
    holders = repeat(count, lambda d, total: total + pres[d], zero)
    device = iota((count, LANES), 0)
    turn = (device + count - iota((count, LANES), 1) % count) % count
    turn = turn.astype(F32)
    others = [(device != s).astype(F32) for s in range(count)]

    part = iota((count, LANES), 1) * 2 // LANES
    halves = [(part == h).astype(F32) for h in range(2)]

    def expect(r, sums):
        here = tall[pl.ds(pl.multiple_of(r * count, count), count), :]
        even = here / jnp.maximum(jnp.sum(here, axis=0, keepdims=True), 1.0)
        return tuple(sums[s] + even * here[s : s + 1, :] for s in range(count))

    nothing = tuple(jnp.zeros((count, LANES), F32) for _ in range(count))
    sums = lax.fori_loop(0, height, expect, nothing)
    loads = tuple(
        jnp.broadcast_to(jnp.sum(sums[s], axis=1, keepdims=True), (count, LANES)) * others[s]
        for s in range(count)
    )

    def settle(r, loads):
        rows = pl.ds(pl.multiple_of(r * count, count), count)
        here = tall[rows, :]
        even = here / jnp.maximum(jnp.sum(here, axis=0, keepdims=True), 1.0)
        picks = jnp.zeros((count, LANES), F32)
        for half in halves:
            cost = jnp.zeros((count, LANES), F32)
            for s in range(count):
                growth = loads[s] * loads[s]
                cost = cost + growth * growth * here[s : s + 1, :]
            cost = jnp.where(here > 0.5, cost, 1e30)
            best = jnp.min(cost, axis=0, keepdims=True)
            place_in_turn = jnp.where(cost == best, turn, 1e30)
            nearest = jnp.min(place_in_turn, axis=0, keepdims=True)
            pick = jnp.where(place_in_turn == nearest, here, 0.0) * half
            picks = picks + pick
            change = pick - even * half
            loads = tuple(
                loads[s] + others[s] * jnp.sum(change * here[s : s + 1, :], axis=1, keepdims=True)
                for s in range(count)
            )
        tall[rows, :] = picks
        return loads

    loads = lax.fori_loop(0, height, settle, loads)
    worst = loads[0]
    for s in range(1, count):
        worst = jnp.maximum(worst, loads[s])
    worst = jnp.max(jnp.max(worst, axis=1, keepdims=True), axis=0, keepdims=True)

    def own(d, owner):
        return jnp.where(tall[pl.ds(d, height, stride=count), :] > 0.5, d, owner)

    owner = repeat(count, own, jnp.full((height, LANES), -1, I32))

    ahead = (iota((LANES, LANES), 0) < iota((LANES, LANES), 1)).astype(BF16)
    ones = jnp.ones((LANES, LANES), BF16)
    ahead_total = jnp.concatenate([ahead, ones], axis=1)
    up, down = iota((height, height), 1), iota((height, height), 0)
    rows_ahead = (up < down).astype(BF16)
    same_tile = ((up < down) & (up // tile_rows == down // tile_rows)).astype(BF16)

    def prefix(mask, rows):
        both = dot(mask.astype(BF16), ahead_total)
        return both[:, :LANES] + dot(rows, both[:, LANES:].astype(BF16))

    mine = (owner == me).astype(F32)
    several = mine * (holders > 1.5).astype(F32)
    single = mine - several
    rank_several = prefix(several, rows_ahead)
    rank_single = prefix(single, rows_ahead)
    total_several = jnp.sum(several, axis=(0, 1), keepdims=True)
    total_mine = jnp.sum(mine, axis=(0, 1), keepdims=True)
    held_here = pres[me]
    entry_rows = entry_ref.shape[0] - 8
    lane_at = iota((entry_rows, LANES), 1)
    first_lane = iota((8, LANES), 1)

    def route(d, carry):
        place, finished, most, entries, counts = carry
        away = jnp.where(d == me, 0.0, 1.0)
        theirs = (owner == d).astype(F32)
        rank_theirs = prefix(theirs, same_tile)
        base = lax.convert_element_type(d, F32) if not isinstance(d, int) else float(d)
        finished = finished + theirs * (base * mcap + rank_theirs + 1.0)
        most = jnp.maximum(most, theirs * (rank_theirs + 1.0))
        leaving = held_here * theirs * away
        rank_leaving = prefix(leaving, rows_ahead)
        place = place + leaving * (base * cap + rank_leaving + 1.0)
        coming = pres[d] * mine * away
        rank_coming = prefix(coming, rows_ahead)
        code = coming * (rank_coming * 1024.0 + rank_several + 1.0)
        high, low = one_hots(keys_ref[pl.ds(d, 1), :], height)
        seen = (look_up(code, high, low) + 0.5).astype(I32) - 1
        rank, local = seen >> 10, seen & 1023
        hit = iota((entry_rows, pairs), 0) == rank
        column = jnp.max(jnp.where(hit, local, -1), axis=1, keepdims=True)
        entries = jnp.where(lane_at == d, column, entries)
        arrivals = jnp.sum(coming, axis=(0, 1), keepdims=True).astype(I32)
        counts = jnp.where(first_lane == d, arrivals, counts)
        return place, finished, most, entries, counts

    place, finished, most, entries, counts = repeat(
        count,
        route,
        (
            zero,
            zero,
            zero,
            jnp.full((entry_rows, LANES), -1, I32),
            jnp.zeros((8, LANES), I32),
        ),
    )
    entry_ref[:entry_rows, :] = entries
    entry_ref[entry_rows:, :] = counts

    pick = (iota((8, height), 1) == me * tile_rows + iota((8, height), 0)).astype(F32)
    spot_ref[...] = (dot(pick, finished, exact=True) + 0.5).astype(I32) - 1

    most = jnp.max(jnp.max(most, axis=1, keepdims=True), axis=0, keepdims=True)
    over = jnp.where((worst > cap + 0.25) | (most > mcap + 0.5), 1, 0)

    place = place + several * (sends + rank_several + 1.0)
    place = place + single * (sends + total_several + rank_single + 1.0)
    tile_of = (row_at // tile_rows).astype(F32)
    moment_place = mine * (tile_of * mcap + finished - 1.0 - me.astype(F32) * mcap)
    high, low = one_hots(keys_ref[pl.ds(me, 1), :], height)
    goes = look_up(place, high, low) - 1.0
    lands = look_up(moment_place, high, low)
    leaves = (goes < sends - 0.5).astype(F32)
    leaving = jnp.sum(leaves, axis=1, keepdims=True)
    first_at, second_at = iota((pairs, pairs), 0), iota((pairs, pairs), 1)
    same = (first_at == second_at).astype(F32)
    upright = dot(same, jnp.broadcast_to(goes, (8, pairs)), ((1,), (1,)), exact=True)[:, 0:1]
    earlier = (upright < goes - 0.5) | ((jnp.abs(upright - goes) < 0.5) & (first_at < second_at))
    position = jnp.sum(earlier.astype(F32), axis=0, keepdims=True)
    at = iota((1, pairs), 1).astype(F32)
    kind = iota((8, pairs), 0)
    values = jnp.where(
        kind == 0,
        at,
        jnp.where(kind == 1, goes, jnp.where(kind == 2, src_ref[...].astype(F32), 0.0)),
    )
    column_at = first_at
    order = (column_at == (position + 0.5).astype(I32)).astype(F32)
    ordered = dot(values, order, ((1,), (1,)), exact=True)
    slot = jnp.where(leaves > 0.5, -1, (goes - sends + 0.5).astype(I32))
    in_slot = (column_at == slot).astype(F32)
    weighed = jnp.where(kind == 0, lands, 1.0)
    summed = dot(weighed, in_slot, ((1,), (1,)), exact=True)
    landing = summed[0:1, :] / jnp.maximum(summed[1:2, :], 1.0)
    result = (ordered + 0.5).astype(I32)
    result = jnp.where(kind == 3, (landing + 0.25).astype(I32), result)
    lane = iota((8, pairs), 1)
    facts = jnp.where(
        lane == 0,
        leaving.astype(I32),
        jnp.where(
            lane == 1,
            total_mine.astype(I32),
            jnp.where(lane == 2, total_several.astype(I32), over),
        ),
    )
    table_ref[...] = jnp.where(kind == 4, facts, result)


def make_plan(keys, pair_source, count, blocks, cap, mcap):
    pairs = keys.shape[1]
    height = count * blocks // LANES
    entry_rows = -(-cap // 8) * 8 + 8
    vmem = pl.BlockSpec(memory_space=pltpu.VMEM)
    return pl.pallas_call(
        functools.partial(plan_kernel, count, blocks, cap, mcap),
        out_shape=(
            jax.ShapeDtypeStruct((8, pairs), I32),
            jax.ShapeDtypeStruct((entry_rows, LANES), I32),
            jax.ShapeDtypeStruct((8, LANES), I32),
        ),
        in_specs=[pl.BlockSpec(memory_space=pltpu.SMEM), vmem, vmem],
        out_specs=(vmem, vmem, vmem),
        scratch_shapes=[
            pltpu.VMEM((count, height, LANES), F32),
            pltpu.VMEM((height * count, LANES), F32),
        ],
        name="plan",
    )(lax.axis_index("lon").astype(I32)[None], keys, pair_source[None, :])


def pair_copies(table, src, weights, xs, ws, x_sem, w_sem, i):
    slot = i % RING
    return (
        pltpu.make_async_copy(src.at[table[2, i]], xs.at[slot], x_sem.at[slot]),
        pltpu.make_async_copy(weights.at[table[0, i]], ws.at[slot], w_sem.at[slot]),
    )


def products(table, src, weights, xs, ws, x_sem, w_sem, low, high, target, packed, first, last, dummy):
    copies = functools.partial(pair_copies, table, src, weights, xs, ws, x_sem, w_sem)

    def start(i):
        for copy in copies(i):
            copy.start()

    def prime(i, carry):
        @pl.when(i < high)
        def _():
            start(i)

        return carry

    lax.fori_loop(low, low + RING, prime, 0)

    def step(g, carry):
        base = g * GROUP
        for u in range(GROUP):
            for copy in copies(base + u):
                copy.wait()
        results = []
        for u in range(GROUP):
            slot = (base + u) % RING
            results.append(dot(xs[slot], ws[slot], ((1,), (1,))))
        for u in range(GROUP):
            i = base + u
            place = table[1, i]
            again = (i > low) & (table[1, jnp.maximum(i - 1, 0)] == place)
            inside = (place >= first) & (place < last)
            where = jnp.where(inside, place - first, dummy)
            value = results[u] + jnp.where(again, target[where], 0.0)
            target[where] = value
            if packed is not None:
                packed[where] = value.astype(BF16)

        @pl.when(base + RING < high)
        def _():
            for u in range(GROUP):
                start(base + RING + u)

        return carry

    lax.fori_loop(low // GROUP, high // GROUP, step, 0)


def send_kernel(sends, table, src, weights, out_ref, total, packed, xs, ws, x_sem, w_sem, out_sem):
    leaving = table[4, 0]
    high = (leaving + GROUP - 1) // GROUP * GROUP
    products(table, src, weights, xs, ws, x_sem, w_sem, 0, high, total, packed, 0, sends, sends)
    out = pltpu.make_async_copy(packed.at[pl.ds(0, sends)], out_ref, out_sem)
    out.start()
    out.wait()


def moment_rows(value):
    days = value.shape[0] // 2
    temper, moist = value[:days], value[days:]
    return [
        jnp.sum(each, axis=0, keepdims=True)
        for each in (temper, moist, temper * temper, moist * moist, temper * moist)
    ]


def put_moments(table, total, moments, spare, begin, end):
    def some(g, carry):
        for u in range(4):
            i = begin + g * 4 + u
            good = i < end
            at = jnp.where(good, i, 0)
            place = jnp.where(good, table[3, at], spare)
            for k, row in enumerate(moment_rows(total[at])):
                moments[k, pl.ds(place, 1), :] = row
        return carry

    lax.fori_loop(0, (end - begin + 3) // 4, some, 0)


def chunk_copies(source, target, sem, c):
    rows = pl.ds(c * CHUNK, CHUNK)
    return pltpu.make_async_copy(source.at[rows], target.at[rows], sem.at[c])


def local_kernel(
    sends, table, src, weights, local_ref, moments, total, xs, ws, x_sem, w_sem, out_sem
):
    pairs = weights.shape[0]
    leaving, owned, several = table[4, 0], table[4, 1], table[4, 2]
    low = leaving // GROUP * GROUP

    moments[...] = jnp.zeros(moments.shape, F32)
    products(
        table, src, weights, xs, ws, x_sem, w_sem, low, pairs, total, None, sends, sends + pairs, pairs
    )
    chunks = (several + CHUNK - 1) // CHUNK

    def begin(c, carry):
        chunk_copies(total, local_ref, out_sem, c).start()
        return carry

    lax.fori_loop(0, chunks, begin, 0)
    put_moments(table, total, moments, moments.shape[1] - 8, several, owned)

    def end(c, carry):
        chunk_copies(total, local_ref, out_sem, c).wait()
        return carry

    lax.fori_loop(0, chunks, end, 0)


def merge_kernel(
    count, cap, mcap, table, entry, local_ref, came, moments_in, out_ref, total, moments, in_sem
):
    several = table[4, 2]
    spare = total.shape[0] - 1
    counts_row = entry.shape[0] - 8
    chunks = (several + CHUNK - 1) // CHUNK

    def begin(c, carry):
        chunk_copies(local_ref, total, in_sem, c).start()
        return carry

    lax.fori_loop(0, chunks, begin, 0)
    moments[...] = moments_in[...]

    def end(c, carry):
        chunk_copies(local_ref, total, in_sem, c).wait()
        return carry

    lax.fori_loop(0, chunks, end, 0)

    def from_one(s, carry):
        number = entry[counts_row, s]

        def some(g, inner):
            for u in range(4):
                r = g * 4 + u
                good = r < number
                at = jnp.where(good, r, 0)
                where = jnp.where(good, entry[at, s], spare)
                total[where] = total[where] + came[s * cap + at].astype(F32)
            return inner

        lax.fori_loop(0, (number + 3) // 4, some, 0)
        return carry

    lax.fori_loop(0, count, from_one, 0)
    put_moments(table, total, moments, moments.shape[1] - 8, 0, several)
    for o in range(count):
        for k in range(5):
            out_ref[o, k] = moments[k, o * mcap : (o + 1) * mcap, :].astype(BF16)


def spread_kernel(count, mcap, spot_ref, came, map_ref, flat):
    rows, blocks_wide = map_ref.shape[1], map_ref.shape[2] // LANES
    for a in range(count):
        for k in range(5):
            flat[a * mcap : (a + 1) * mcap, k * LANES : (k + 1) * LANES] = came[a, k]
    chosen = (iota((spot_ref.shape[0], count * mcap), 1) == spot_ref[...]).astype(F32)
    laid = dot(chosen.astype(BF16), flat[...])
    for q in range(blocks_wide):
        for k in range(5):
            map_ref[k, :, q * LANES : (q + 1) * LANES] = laid[
                q * rows : (q + 1) * rows, k * LANES : (k + 1) * LANES
            ].astype(BF16)


def direct(cap, mcap, source_fields, weight_blocks, table, entry, spot):
    count = lax.axis_size("lon")
    blocks, channels, cells = source_fields.shape
    pairs = weight_blocks.shape[0]
    sends = count * cap
    smem = pl.BlockSpec(memory_space=pltpu.SMEM)
    vmem = pl.BlockSpec(memory_space=pltpu.VMEM)
    hbm = pl.BlockSpec(memory_space=pl.ANY)
    buffers = [
        pltpu.VMEM((RING, channels, cells), BF16),
        pltpu.VMEM((RING, cells, cells), BF16),
        pltpu.SemaphoreType.DMA((RING,)),
        pltpu.SemaphoreType.DMA((RING,)),
    ]
    packed = pl.pallas_call(
        functools.partial(send_kernel, sends),
        out_shape=jax.ShapeDtypeStruct((sends, channels, cells), BF16),
        in_specs=[smem, hbm, hbm],
        out_specs=hbm,
        scratch_shapes=[
            pltpu.VMEM((sends + 1, channels, cells), F32),
            pltpu.VMEM((sends + 1, channels, cells), BF16),
        ]
        + buffers
        + [pltpu.SemaphoreType.DMA],
        name="leaving",
    )(table, source_fields, weight_blocks)
    came = lax.all_to_all(
        packed.reshape(count, cap, channels, cells), "lon", split_axis=0, concat_axis=0, tiled=True
    ).reshape(sends, channels, cells)
    chunk_count = -(-pairs // CHUNK)
    local, moments = pl.pallas_call(
        functools.partial(local_kernel, sends),
        out_shape=(
            jax.ShapeDtypeStruct((pairs, channels, cells), F32),
            jax.ShapeDtypeStruct((5, count * mcap + 8, cells), F32),
        ),
        in_specs=[smem, hbm, hbm],
        out_specs=(hbm, vmem),
        scratch_shapes=[pltpu.VMEM((pairs + 1, channels, cells), F32)]
        + buffers
        + [pltpu.SemaphoreType.DMA((chunk_count,))],
        name="staying",
    )(table, source_fields, weight_blocks)
    finished = pl.pallas_call(
        functools.partial(merge_kernel, count, cap, mcap),
        out_shape=jax.ShapeDtypeStruct((count, 5, mcap, cells), BF16),
        in_specs=[smem, smem, hbm, vmem, vmem],
        out_specs=vmem,
        scratch_shapes=[
            pltpu.VMEM((pairs + 1, channels, cells), F32),
            pltpu.VMEM((5, count * mcap + 8, cells), F32),
            pltpu.SemaphoreType.DMA((chunk_count,)),
        ],
        name="merge",
    )(table, entry, local, came, moments)
    arrived = lax.all_to_all(finished, "lon", split_axis=0, concat_axis=0, tiled=True)
    wide = LON_DEV // cells
    where = spot.reshape(-1)[:blocks].reshape(LAT_DEV, wide).T.reshape(blocks, 1)
    return pl.pallas_call(
        functools.partial(spread_kernel, count, mcap),
        out_shape=jax.ShapeDtypeStruct((5, LAT_DEV, LON_DEV), BF16),
        in_specs=[vmem, vmem],
        out_specs=vmem,
        scratch_shapes=[pltpu.VMEM((count * mcap, 5 * cells), BF16)],
        name="spread",
    )(where, arrived)


def padded_exchange(source_fields, weight_blocks, pair_source, targets, pair_block):
    lon_count = lax.axis_size("lon")
    pair_count = pair_source.shape[0]
    capacity = max(2, 2 * pair_count // lon_count)
    blocks_dev, channels, cell_count = source_fields.shape
    lanes = jnp.arange(lon_count, dtype=jnp.int32)
    matches = (targets[:, None] == lanes[None, :]).astype(jnp.int32)
    earlier = jnp.cumsum(matches, axis=0) - matches
    slots = jnp.sum(earlier * matches, axis=1)
    position = targets * capacity + slots
    outgoing = jnp.zeros((lon_count * capacity,), jnp.int32).at[position].set(pair_block)
    arriving = lax.all_to_all(
        outgoing.reshape(lon_count, capacity), "lon", split_axis=0, concat_axis=0, tiled=True
    )
    picked = source_fields[pair_source]
    terms = jnp.einsum("pck,pjk->pcj", picked, weight_blocks, preferred_element_type=jnp.float32)
    packed = (
        jnp.zeros((lon_count * capacity, channels, cell_count), jnp.float32).at[position].set(terms)
    )
    received = lax.all_to_all(
        packed.reshape(lon_count, capacity, channels, cell_count).astype(jnp.bfloat16),
        "lon",
        split_axis=0,
        concat_axis=0,
        tiled=True,
    ).astype(jnp.float32)
    remapped = jax.ops.segment_sum(
        received.reshape(lon_count * capacity, channels, cell_count),
        arriving.reshape(-1),
        num_segments=blocks_dev,
    )
    days = channels // 2
    temper = remapped[:, :days]
    moist = remapped[:, days:]
    moments = jnp.stack(
        [
            temper.sum(1),
            moist.sum(1),
            (temper * temper).sum(1),
            (moist * moist).sum(1),
            (temper * moist).sum(1),
        ]
    )
    return moments.reshape(5, LAT_DEV, LON_DEV).astype(BF16)


def local(source_fields, weight_blocks, pair_source, pair_target, pair_block):
    count = lax.axis_size("lon")
    blocks, channels, _ = source_fields.shape
    days = channels // 2
    pairs = pair_source.shape[0]
    share = -(-pairs // count)
    cap = max(share * 17 // 32, min(share, 8))
    mcap = -(-share * 3 // 2 // 16) * 16
    targets = pair_target[:, 0]
    keys = targets * blocks + pair_block
    all_keys = lax.all_to_all(
        jnp.broadcast_to(keys[None, :], (count, pairs)), "lon", split_axis=0, concat_axis=0, tiled=True
    )
    table, entry, spot = make_plan(all_keys, pair_source, count, blocks, cap, mcap)
    moments = lax.cond(
        table[4, 3] == 0,
        lambda: direct(cap, mcap, source_fields, weight_blocks, table, entry, spot),
        lambda: padded_exchange(source_fields, weight_blocks, pair_source, targets, pair_block),
    )
    lon_band = band_matrix(LON_DEV)
    lat_band = band_matrix(LAT_DEV)
    taller = padded(moments, (("lat", 1),), WINDOW_HALF, False)
    wider = padded(taller, (("lon", 2),), WINDOW_HALF, True).astype(F32)
    smoothed = smooth_lat(smooth_lon(wider, lon_band), lat_band)
    kernel = gaussian_taps()
    height = LAT_DEV * lax.axis_size("lat")
    rows = (
        lax.axis_index("lat") * LAT_DEV
        + jnp.arange(LAT_DEV, dtype=jnp.int32)[:, None]
        + jnp.arange(2 * WINDOW_HALF + 1, dtype=jnp.int32)[None, :]
        - WINDOW_HALF
    )
    inside = ((rows >= 0) & (rows < height)).astype(jnp.float32)
    lat_total = jnp.sum(inside * kernel[None, :], axis=1)
    weight_total = lat_total[:, None] * (jnp.sum(kernel) * days)
    mean_temper = smoothed[0] / weight_total
    mean_moist = smoothed[1] / weight_total
    var_temper = smoothed[2] / weight_total - mean_temper * mean_temper
    var_moist = smoothed[3] / weight_total - mean_moist * mean_moist
    covar = smoothed[4] / weight_total - mean_temper * mean_moist
    return covar / jnp.sqrt(var_temper * var_moist + 1e-06)


def solution(mesh):
    placed = (
        P(("lat", "lon"), None, None),
        P(("lat", "lon"), None, None),
        P(("lat", "lon")),
        P(("lat", "lon"), None),
        P(("lat", "lon")),
    )
    return jax.shard_map(
        local, mesh=mesh, in_specs=placed, out_specs=P("lat", "lon"), check_vma=False
    )
```

```python
import functools

import jax
import jax.numpy as jnp
from jax import lax
from jax.experimental import pallas as pl
from jax.experimental.pallas import tpu as pltpu
from jax.sharding import PartitionSpec as P

WINDOW_HALF = 16
LAT_DEV = 64
LON_DEV = 512
LANES = 128
RING = 32
GROUP = 8
CHUNK = 16
F32 = jnp.float32
BF16 = jnp.bfloat16
I32 = jnp.int32


def padded(x, sides, width, wrap):
    for axis, dim in sides:
        count, length = (lax.axis_size(axis), x.shape[dim])
        up = [(i, (i + 1) % count) for i in range(count if wrap else count - 1)]
        down = [(j, i) for i, j in up]
        last = lax.slice_in_dim(x, length - width, length, axis=dim)
        leading = lax.slice_in_dim(x, 0, width, axis=dim)
        before = lax.ppermute(last, axis, up)
        after = lax.ppermute(leading, axis, down)
        x = jnp.concatenate([before, x, after], axis=dim)
    return x


def gaussian_taps():
    offsets = jnp.arange(2 * WINDOW_HALF + 1).astype(jnp.float32) - WINDOW_HALF
    return jnp.exp(-offsets * offsets / (0.5 * WINDOW_HALF * WINDOW_HALF))


def band_matrix(length):
    outer = jnp.arange(length + 2 * WINDOW_HALF, dtype=jnp.int32)[:, None]
    inner = jnp.arange(length, dtype=jnp.int32)[None, :]
    offsets = (outer - inner - WINDOW_HALF).astype(jnp.float32)
    values = jnp.exp(-offsets * offsets / (0.5 * WINDOW_HALF * WINDOW_HALF))
    return jnp.where(jnp.abs(offsets) <= WINDOW_HALF, values, 0.0)


def smooth_lon(fields, lon_band):
    return jnp.einsum("krb,bj->krj", fields, lon_band, precision=lax.Precision.HIGHEST)


def smooth_lat(fields, lat_band):
    return jnp.einsum("ai,kaj->kij", lat_band, fields, precision=lax.Precision.HIGHEST)


def iota(shape, dim):
    return lax.broadcasted_iota(I32, shape, dim)


def dot(a, b, dims=((1,), (0,)), exact=False):
    return lax.dot_general(
        a,
        b,
        (dims, ((), ())),
        preferred_element_type=F32,
        precision=lax.Precision.HIGHEST if exact else None,
    )


def repeat(count, body, carry):
    if count <= 8:
        for step in range(count):
            carry = body(step, carry)
        return carry
    return lax.fori_loop(0, count, body, carry)


def one_hots(row, height):
    pairs = row.shape[1]
    high = (iota((height, pairs), 0) == (row >> 7)).astype(F32)
    low = (iota((LANES, pairs), 0) == (row & (LANES - 1))).astype(F32)
    return high, low


def look_up(table, high, low):
    return jnp.sum(dot(table, low, exact=True) * high, axis=0, keepdims=True)


def prefixes(height, tile_rows):
    ahead = (iota((LANES, LANES), 0) < iota((LANES, LANES), 1)).astype(BF16)
    ones = jnp.ones((LANES, LANES), BF16)
    ahead_total = jnp.concatenate([ahead, ones], axis=1)
    up, down = iota((height, height), 1), iota((height, height), 0)
    rows_ahead = (up < down).astype(BF16)
    same_tile = ((up < down) & (up // tile_rows == down // tile_rows)).astype(BF16)

    def prefix(mask, rows):
        both = dot(mask.astype(BF16), ahead_total)
        return both[:, :LANES] + dot(rows, both[:, LANES:].astype(BF16))

    return prefix, rows_ahead, same_tile


def as_float(d):
    return float(d) if isinstance(d, int) else lax.convert_element_type(d, F32)


def plan_kernel(
    count, blocks, cap, extra, mcap, me_ref, keys_ref, src_ref, table_ref, owner_ref, pres, tall
):
    me = me_ref[0]
    pairs = keys_ref.shape[2]
    height = count * blocks // LANES
    tile_rows = blocks // LANES
    half = count // 2
    sends = count * cap + (half - 1) * extra

    def held(d, carry):
        high, low = one_hots(keys_ref[d], height)
        found = dot(high.astype(BF16), low.astype(BF16), ((1,), (1,)))
        found = (found > 0.5).astype(F32)
        pres[d] = found
        tall[pl.ds(d, height, stride=count), :] = found
        return carry

    repeat(count, held, 0)

    zero = jnp.zeros((height, LANES), F32)
    holders = repeat(count, lambda d, total: total + pres[d], zero)
    device = iota((count, LANES), 0)
    turn = (device + count - iota((count, LANES), 1) % count) % count
    turn = turn.astype(F32)
    others = [(device != s).astype(F32) for s in range(count)]
    near = [(device // half == s // half).astype(F32) for s in range(count)]
    weight = [1.0 - 0.8 * near[s] for s in range(count)]
    part = iota((count, LANES), 1) * 2 // LANES
    sides = [(part == h).astype(F32) for h in range(2)]

    def rows_of(r):
        return pl.ds(pl.multiple_of(r * count, count), count)

    def expect(r, sums):
        here = tall[rows_of(r), :]
        even = here / jnp.maximum(jnp.sum(here, axis=0, keepdims=True), 1.0)
        return tuple(sums[s] + even * here[s : s + 1, :] for s in range(count))

    nothing = tuple(jnp.zeros((count, LANES), F32) for _ in range(count))
    sums = lax.fori_loop(0, height, expect, nothing)
    loads = tuple(
        jnp.broadcast_to(jnp.sum(sums[s], axis=1, keepdims=True), (count, LANES)) * others[s]
        for s in range(count)
    )

    def settle(r, loads):
        here = tall[rows_of(r), :]
        even = here / jnp.maximum(jnp.sum(here, axis=0, keepdims=True), 1.0)
        picks = jnp.zeros((count, LANES), F32)
        for side in sides:
            cost = jnp.zeros((count, LANES), F32)
            for s in range(count):
                growth = loads[s] * loads[s]
                cost = cost + weight[s] * growth * growth * here[s : s + 1, :]
            cost = jnp.where(here > 0.5, cost, 1e30)
            best = jnp.min(cost, axis=0, keepdims=True)
            place_in_turn = jnp.where(cost == best, turn, 1e30)
            nearest = jnp.min(place_in_turn, axis=0, keepdims=True)
            pick = jnp.where(place_in_turn == nearest, here, 0.0) * side
            picks = picks + pick
            change = pick - even * side
            loads = tuple(
                loads[s] + others[s] * jnp.sum(change * here[s : s + 1, :], axis=1, keepdims=True)
                for s in range(count)
            )
        tall[rows_of(r), :] = picks
        return loads

    loads = lax.fori_loop(0, height, settle, loads)
    far_most, near_most = loads[0] * (1.0 - near[0]), loads[0] * near[0]
    for s in range(1, count):
        far_most = jnp.maximum(far_most, loads[s] * (1.0 - near[s]))
        near_most = jnp.maximum(near_most, loads[s] * near[s])

    def tile_most(o, most):
        sums = tall[rows_of(o * tile_rows), :]
        for i in range(1, tile_rows):
            sums = sums + tall[rows_of(o * tile_rows + i), :]
        return jnp.maximum(most, jnp.sum(sums, axis=1, keepdims=True))

    most = repeat(count, tile_most, jnp.zeros((count, 1), F32))
    fits = (far_most < cap + 0.25) & (near_most < cap + extra + 0.25) & (most < mcap + 0.5)
    fits = jnp.min(jnp.min(fits.astype(F32), axis=1, keepdims=True), axis=0, keepdims=True)
    over = 1 - fits.astype(I32)

    def own(d, owner):
        return jnp.where(tall[pl.ds(d, height, stride=count), :] > 0.5, d, owner)

    owner = repeat(count, own, jnp.full((height, LANES), -1, I32))
    owner_ref[...] = owner
    prefix, rows_ahead, _ = prefixes(height, tile_rows)
    mine = (owner == me).astype(F32)
    several = mine * (holders > 1.5).astype(F32)
    single = mine - several
    rank_several = prefix(several, rows_ahead)
    rank_single = prefix(single, rows_ahead)
    total_several = jnp.sum(several, axis=(0, 1), keepdims=True)
    total_mine = jnp.sum(mine, axis=(0, 1), keepdims=True)
    held_here = pres[me]

    def route(d, place):
        away = jnp.where(d == me, 0.0, 1.0)
        leaving = held_here * (owner == d).astype(F32) * away
        rank = prefix(leaving, rows_ahead)
        first = as_float(d) * cap + rank
        steps = ((d % half + half - me % half) % half).astype(F32)
        second = count * cap + (steps - 1.0) * extra + rank - cap
        return place + leaving * (jnp.where(rank < cap - 0.5, first, second) + 1.0)

    place = repeat(count, route, zero)
    place = place + several * (sends + rank_several + 1.0)
    place = place + single * (sends + total_several + rank_single + 1.0)
    high, low = one_hots(keys_ref[me], height)
    goes = look_up(place, high, low) - 1.0
    leaving = jnp.sum((goes < sends - 0.5).astype(F32), axis=1, keepdims=True)
    first_at, second_at = iota((pairs, pairs), 0), iota((pairs, pairs), 1)
    same = (first_at == second_at).astype(F32)
    upright = dot(same, jnp.broadcast_to(goes, (8, pairs)), ((1,), (1,)), exact=True)[:, 0:1]
    earlier = (upright < goes - 0.5) | ((jnp.abs(upright - goes) < 0.5) & (first_at < second_at))
    position = jnp.sum(earlier.astype(F32), axis=0, keepdims=True)
    at = iota((1, pairs), 1).astype(F32)
    kind = iota((8, pairs), 0)
    values = jnp.where(
        kind == 0,
        at,
        jnp.where(kind == 1, goes, jnp.where(kind == 2, src_ref[...].astype(F32), 0.0)),
    )
    order = (first_at == (position + 0.5).astype(I32)).astype(F32)
    result = (dot(values, order, ((1,), (1,)), exact=True) + 0.5).astype(I32)
    lane = iota((8, pairs), 1)
    facts = jnp.where(lane == 0, leaving.astype(I32), over)
    facts = jnp.where(lane == 1, total_mine.astype(I32), facts)
    facts = jnp.where(lane == 2, total_several.astype(I32), facts)
    facts = jnp.where(lane == 4, me, facts)
    result = jnp.where(kind == 4, facts, result)
    table_ref[...] = jnp.where(kind == 5, (goes + 0.5).astype(I32), result)


def finish_kernel(
    count, blocks, sends, mcap, me_ref, keys_ref, owner_ref, pres, table_ref, entry_ref, spot_ref, landing_ref
):
    me = me_ref[0]
    pairs = keys_ref.shape[2]
    height = count * blocks // LANES
    tile_rows = blocks // LANES
    prefix, rows_ahead, same_tile = prefixes(height, tile_rows)
    owner = owner_ref[...]
    zero = jnp.zeros((height, LANES), F32)
    holders = repeat(count, lambda d, total: total + pres[d], zero)
    mine = (owner == me).astype(F32)
    rank_several = prefix(mine * (holders > 1.5).astype(F32), rows_ahead)
    entry_rows = entry_ref.shape[0] - 8
    lane_at = iota((entry_rows, LANES), 1)
    first_lane = iota((8, LANES), 1)

    def route(d, carry):
        finished, entries, counts = carry
        away = jnp.where(d == me, 0.0, 1.0)
        theirs = (owner == d).astype(F32)
        rank_theirs = prefix(theirs, same_tile)
        finished = finished + theirs * (as_float(d) * mcap + rank_theirs + 1.0)
        coming = pres[d] * mine * away
        rank_coming = prefix(coming, rows_ahead)
        code = coming * (rank_coming * 1024.0 + rank_several + 1.0)
        high, low = one_hots(keys_ref[d], height)
        seen = (look_up(code, high, low) + 0.5).astype(I32) - 1
        rank, local = seen >> 10, seen & 1023
        hit = iota((entry_rows, pairs), 0) == rank
        column = jnp.max(jnp.where(hit, local, -1), axis=1, keepdims=True)
        entries = jnp.where(lane_at == d, column, entries)
        arrivals = jnp.sum(coming, axis=(0, 1), keepdims=True).astype(I32)
        counts = jnp.where(first_lane == d, arrivals, counts)
        return finished, entries, counts

    finished, entries, counts = repeat(
        count,
        route,
        (zero, jnp.full((entry_rows, LANES), -1, I32), jnp.zeros((8, LANES), I32)),
    )
    entry_ref[:entry_rows, :] = entries
    entry_ref[entry_rows:, :] = counts
    pick = (iota((8, height), 1) == me * tile_rows + iota((8, height), 0)).astype(F32)
    spot_ref[...] = (dot(pick, finished, exact=True) + 0.5).astype(I32) - 1
    tile_of = (iota((height, LANES), 0) // tile_rows).astype(F32)
    moment_place = mine * (tile_of * mcap + finished - 1.0 - me.astype(F32) * mcap)
    high, low = one_hots(keys_ref[me], height)
    lands = look_up(moment_place, high, low)
    goes = table_ref[5:6, :]
    slot = jnp.where(goes < sends, -1, goes - sends)
    in_slot = (iota((pairs, pairs), 0) == slot).astype(F32)
    weighed = jnp.where(iota((8, pairs), 0) == 0, lands, 1.0)
    summed = dot(weighed, in_slot, ((1,), (1,)), exact=True)
    landing = summed[0:1, :] / jnp.maximum(summed[1:2, :], 1.0)
    landing_ref[...] = jnp.broadcast_to((landing + 0.25).astype(I32), landing_ref.shape)


def make_plan(me, keys, pair_source, count, blocks, cap, extra, mcap):
    pairs = keys.shape[2]
    height = count * blocks // LANES
    vmem = pl.BlockSpec(memory_space=pltpu.VMEM)
    return pl.pallas_call(
        functools.partial(plan_kernel, count, blocks, cap, extra, mcap),
        out_shape=(
            jax.ShapeDtypeStruct((8, pairs), I32),
            jax.ShapeDtypeStruct((height, LANES), I32),
            jax.ShapeDtypeStruct((count, height, LANES), F32),
        ),
        in_specs=[pl.BlockSpec(memory_space=pltpu.SMEM), vmem, vmem],
        out_specs=(vmem, vmem, vmem),
        scratch_shapes=[pltpu.VMEM((height * count, LANES), F32)],
        name="plan",
    )(me, keys, pair_source[None, :])


def finish_plan(me, keys, owner, pres, table, count, blocks, cap, extra, mcap):
    pairs = keys.shape[2]
    entry_rows = -(-(cap + extra) // 8) * 8 + 8
    sends = count * cap + (count // 2 - 1) * extra
    vmem = pl.BlockSpec(memory_space=pltpu.VMEM)
    return pl.pallas_call(
        functools.partial(finish_kernel, count, blocks, sends, mcap),
        out_shape=(
            jax.ShapeDtypeStruct((entry_rows, LANES), I32),
            jax.ShapeDtypeStruct((8, LANES), I32),
            jax.ShapeDtypeStruct((8, pairs), I32),
        ),
        in_specs=[pl.BlockSpec(memory_space=pltpu.SMEM)] + [vmem] * 4,
        out_specs=(vmem, vmem, vmem),
        compiler_params=pltpu.CompilerParams(vmem_limit_bytes=8 << 20),
        name="finish",
    )(me, keys, owner, pres, table)


def pair_copies(table, src, weights, xs, ws, x_sem, w_sem, i):
    slot = i % RING
    return (
        pltpu.make_async_copy(src.at[table[2, i]], xs.at[slot], x_sem.at[slot]),
        pltpu.make_async_copy(weights.at[table[0, i]], ws.at[slot], w_sem.at[slot]),
    )


def products(table, src, weights, xs, ws, x_sem, w_sem, low, high, target, packed, first, last, dummy):
    copies = functools.partial(pair_copies, table, src, weights, xs, ws, x_sem, w_sem)

    def start(i):
        for copy in copies(i):
            copy.start()

    def prime(i, carry):
        @pl.when(i < high)
        def _():
            start(i)

        return carry

    lax.fori_loop(low, low + RING, prime, 0)

    def step(g, carry):
        base = g * GROUP
        for u in range(GROUP):
            for copy in copies(base + u):
                copy.wait()
        results = []
        for u in range(GROUP):
            slot = (base + u) % RING
            results.append(dot(xs[slot], ws[slot], ((1,), (1,))))
        for u in range(GROUP):
            i = base + u
            place = table[1, i]
            again = (i > low) & (table[1, jnp.maximum(i - 1, 0)] == place)
            inside = (place >= first) & (place < last)
            where = jnp.where(inside, place - first, dummy)
            value = results[u] + jnp.where(again, target[where], 0.0)
            target[where] = value
            if packed is not None:
                packed[where] = value.astype(BF16)

        @pl.when(base + RING < high)
        def _():
            for u in range(GROUP):
                start(base + RING + u)

        return carry

    lax.fori_loop(low // GROUP, high // GROUP, step, 0)


def send_kernel(first, extra, parts, table, src, weights, *refs):
    far_ref, near_refs = refs[0], refs[1 : 1 + parts]
    total, packed, xs, ws, x_sem, w_sem, out_sem = refs[1 + parts :]
    sends = packed.shape[0] - 1
    leaving = table[4, 0]
    high = (leaving + GROUP - 1) // GROUP * GROUP
    products(table, src, weights, xs, ws, x_sem, w_sem, 0, high, total, packed, 0, sends, sends)
    outs = [pltpu.make_async_copy(packed.at[pl.ds(0, first)], far_ref, out_sem.at[0])]
    for j in range(parts):
        rows = pl.ds(first + j * extra, extra)
        outs.append(pltpu.make_async_copy(packed.at[rows], near_refs[j], out_sem.at[1 + j]))
    for out in outs:
        out.start()
    for out in outs:
        out.wait()


def moment_rows(value):
    days = value.shape[0] // 2
    temper, moist = value[:days], value[days:]
    return [
        jnp.sum(each, axis=0, keepdims=True)
        for each in (temper, moist, temper * temper, moist * moist, temper * moist)
    ]


def put_moments(landing, total, moments, spare, begin, end):
    def some(g, carry):
        for u in range(4):
            i = begin + g * 4 + u
            good = i < end
            at = jnp.where(good, i, 0)
            place = jnp.where(good, landing[0, at], spare)
            for k, row in enumerate(moment_rows(total[at])):
                moments[k, pl.ds(place, 1), :] = row
        return carry

    lax.fori_loop(0, (end - begin + 3) // 4, some, 0)


def chunk_copies(source, target, sem, c):
    rows = pl.ds(c * CHUNK, CHUNK)
    return pltpu.make_async_copy(source.at[rows], target.at[rows], sem.at[c])


def local_kernel(
    sends, table, landing, src, weights, local_ref, moments, total, xs, ws, x_sem, w_sem, out_sem
):
    pairs = weights.shape[0]
    leaving, owned, several = table[4, 0], table[4, 1], table[4, 2]
    low = leaving // GROUP * GROUP

    moments[...] = jnp.zeros(moments.shape, F32)
    products(
        table, src, weights, xs, ws, x_sem, w_sem, low, pairs, total, None, sends, sends + pairs, pairs
    )
    chunks = (several + CHUNK - 1) // CHUNK

    def begin(c, carry):
        chunk_copies(total, local_ref, out_sem, c).start()
        return carry

    lax.fori_loop(0, chunks, begin, 0)
    put_moments(landing, total, moments, moments.shape[1] - 8, several, owned)

    def end(c, carry):
        chunk_copies(total, local_ref, out_sem, c).wait()
        return carry

    lax.fori_loop(0, chunks, end, 0)


def merge_kernel(count, cap, extra, mcap, table, landing, entry, local_ref, moments_in, far_ref, *refs):
    parts = count // 2 - 1
    near_refs = refs[:parts]
    out_ref, total, near, moments, in_sem, near_sem, moment_sem = refs[parts:]
    several, me = table[4, 2], table[4, 4]
    half = count // 2
    spare = total.shape[0] - 1
    counts_row = entry.shape[0] - 8
    chunks = (several + CHUNK - 1) // CHUNK

    def begin(c, carry):
        chunk_copies(local_ref, total, in_sem, c).start()
        return carry

    near_copies = [
        pltpu.make_async_copy(near_refs[j], near.at[pl.ds(j * extra, extra)], near_sem.at[j])
        for j in range(parts)
    ]
    lax.fori_loop(0, chunks, begin, 0)
    for near_copy in near_copies:
        near_copy.start()
    moment_copy = pltpu.make_async_copy(moments_in, moments, moment_sem)
    moment_copy.start()

    def end(c, carry):
        chunk_copies(local_ref, total, in_sem, c).wait()
        return carry

    lax.fori_loop(0, chunks, end, 0)

    def add(s, low, high, came, shift):
        def some(g, inner):
            for u in range(4):
                r = low + g * 4 + u
                good = r < high
                at = jnp.where(good, r, low)
                where = jnp.where(good, entry[at, s], spare)
                total[where] = total[where] + came[shift + at].astype(F32)
            return inner

        lax.fori_loop(0, (high - low + 3) // 4, some, 0)

    def from_far(s, carry):
        add(s, 0, jnp.minimum(entry[counts_row, s], cap), far_ref, s * cap)
        return carry

    lax.fori_loop(0, count, from_far, 0)
    for near_copy in near_copies:
        near_copy.wait()

    def from_near(j, carry):
        s = me // half * half + (me % half + half - j - 1) % half
        number = jnp.maximum(entry[counts_row, s], cap)
        add(s, cap, number, near, j * extra - cap)
        return carry

    lax.fori_loop(0, parts, from_near, 0)
    moment_copy.wait()
    put_moments(landing, total, moments, moments.shape[1] - 8, 0, several)
    for o in range(count):
        for k in range(5):
            out_ref[o, k] = moments[k, o * mcap : (o + 1) * mcap, :].astype(BF16)


def spread_kernel(count, mcap, spot_ref, came, map_ref, flat):
    rows, blocks_wide = map_ref.shape[1], map_ref.shape[2] // LANES
    for a in range(count):
        for k in range(5):
            flat[a * mcap : (a + 1) * mcap, k * LANES : (k + 1) * LANES] = came[a, k]
    chosen = (iota((spot_ref.shape[0], count * mcap), 1) == spot_ref[...]).astype(F32)
    laid = dot(chosen.astype(BF16), flat[...])
    for q in range(blocks_wide):
        for k in range(5):
            map_ref[k, :, q * LANES : (q + 1) * LANES] = laid[
                q * rows : (q + 1) * rows, k * LANES : (k + 1) * LANES
            ].astype(BF16)


def direct(cap, extra, mcap, source_fields, weight_blocks, me, keys, table, owner, pres):
    count = lax.axis_size("lon")
    half = count // 2
    blocks, channels, cells = source_fields.shape
    pairs = weight_blocks.shape[0]
    parts = half - 1
    first = count * cap
    sends = first + parts * extra
    smem = pl.BlockSpec(memory_space=pltpu.SMEM)
    vmem = pl.BlockSpec(memory_space=pltpu.VMEM)
    hbm = pl.BlockSpec(memory_space=pl.ANY)
    buffers = [
        pltpu.VMEM((RING, channels, cells), BF16),
        pltpu.VMEM((RING, cells, cells), BF16),
        pltpu.SemaphoreType.DMA((RING,)),
        pltpu.SemaphoreType.DMA((RING,)),
    ]
    sent = pl.pallas_call(
        functools.partial(send_kernel, first, extra, parts),
        out_shape=[jax.ShapeDtypeStruct((first, channels, cells), BF16)]
        + [jax.ShapeDtypeStruct((extra, channels, cells), BF16)] * parts,
        in_specs=[smem, hbm, hbm],
        out_specs=[hbm] + [hbm] * parts,
        scratch_shapes=[
            pltpu.VMEM((sends + 1, channels, cells), F32),
            pltpu.VMEM((sends + 1, channels, cells), BF16),
        ]
        + buffers
        + [pltpu.SemaphoreType.DMA((1 + parts,))],
        name="leaving",
    )(table, source_fields, weight_blocks)
    sent, owner = lax.optimization_barrier((sent, owner))
    far = lax.all_to_all(
        sent[0].reshape(count, cap, channels, cells), "lon", split_axis=0, concat_axis=0, tiled=True
    ).reshape(first, channels, cells)
    near = []
    for j in range(parts):
        turn = [(i, i // half * half + (i % half + j + 1) % half) for i in range(count)]
        near.append(lax.ppermute(sent[1 + j], "lon", turn))
    entry, spot, landing = finish_plan(
        me, keys, owner, pres, table, count, blocks, cap, extra, mcap
    )
    chunk_count = -(-pairs // CHUNK)
    local, moments = pl.pallas_call(
        functools.partial(local_kernel, sends),
        out_shape=(
            jax.ShapeDtypeStruct((pairs, channels, cells), F32),
            jax.ShapeDtypeStruct((5, count * mcap + 8, cells), F32),
        ),
        in_specs=[smem, smem, hbm, hbm],
        out_specs=(hbm, vmem),
        scratch_shapes=[pltpu.VMEM((pairs + 1, channels, cells), F32)]
        + buffers
        + [pltpu.SemaphoreType.DMA((chunk_count,))],
        name="staying",
    )(table, landing, source_fields, weight_blocks)
    finished = pl.pallas_call(
        functools.partial(merge_kernel, count, cap, extra, mcap),
        out_shape=jax.ShapeDtypeStruct((count, 5, mcap, cells), BF16),
        in_specs=[smem, smem, smem, hbm, hbm, vmem] + [hbm] * parts,
        out_specs=vmem,
        scratch_shapes=[
            pltpu.VMEM((pairs + 1, channels, cells), F32),
            pltpu.VMEM((parts * extra, channels, cells), BF16),
            pltpu.VMEM((5, count * mcap + 8, cells), F32),
            pltpu.SemaphoreType.DMA((chunk_count,)),
            pltpu.SemaphoreType.DMA((parts,)),
            pltpu.SemaphoreType.DMA,
        ],
        compiler_params=pltpu.CompilerParams(vmem_limit_bytes=50 << 20),
        name="merge",
    )(table, landing, entry, local, moments, far, *near)
    arrived = lax.all_to_all(finished, "lon", split_axis=0, concat_axis=0, tiled=True)
    wide = LON_DEV // cells
    where = spot.reshape(-1)[:blocks].reshape(LAT_DEV, wide).T.reshape(blocks, 1)
    return pl.pallas_call(
        functools.partial(spread_kernel, count, mcap),
        out_shape=jax.ShapeDtypeStruct((5, LAT_DEV, LON_DEV), BF16),
        in_specs=[vmem, vmem],
        out_specs=vmem,
        scratch_shapes=[pltpu.VMEM((count * mcap, 5 * cells), BF16)],
        compiler_params=pltpu.CompilerParams(vmem_limit_bytes=8 << 20),
        name="spread",
    )(where, arrived)


def padded_exchange(source_fields, weight_blocks, pair_source, targets, pair_block):
    lon_count = lax.axis_size("lon")
    pair_count = pair_source.shape[0]
    capacity = max(2, 2 * pair_count // lon_count)
    blocks_dev, channels, cell_count = source_fields.shape
    lanes = jnp.arange(lon_count, dtype=jnp.int32)
    matches = (targets[:, None] == lanes[None, :]).astype(jnp.int32)
    earlier = jnp.cumsum(matches, axis=0) - matches
    slots = jnp.sum(earlier * matches, axis=1)
    position = targets * capacity + slots
    outgoing = jnp.zeros((lon_count * capacity,), jnp.int32).at[position].set(pair_block)
    arriving = lax.all_to_all(
        outgoing.reshape(lon_count, capacity), "lon", split_axis=0, concat_axis=0, tiled=True
    )
    picked = source_fields[pair_source]
    terms = jnp.einsum("pck,pjk->pcj", picked, weight_blocks, preferred_element_type=jnp.float32)
    packed = (
        jnp.zeros((lon_count * capacity, channels, cell_count), jnp.float32).at[position].set(terms)
    )
    received = lax.all_to_all(
        packed.reshape(lon_count, capacity, channels, cell_count).astype(jnp.bfloat16),
        "lon",
        split_axis=0,
        concat_axis=0,
        tiled=True,
    ).astype(jnp.float32)
    remapped = jax.ops.segment_sum(
        received.reshape(lon_count * capacity, channels, cell_count),
        arriving.reshape(-1),
        num_segments=blocks_dev,
    )
    days = channels // 2
    temper = remapped[:, :days]
    moist = remapped[:, days:]
    moments = jnp.stack(
        [
            temper.sum(1),
            moist.sum(1),
            (temper * temper).sum(1),
            (moist * moist).sum(1),
            (temper * moist).sum(1),
        ]
    )
    return moments.reshape(5, LAT_DEV, LON_DEV).astype(BF16)


def local(source_fields, weight_blocks, pair_source, pair_target, pair_block):
    count = lax.axis_size("lon")
    blocks, channels, _ = source_fields.shape
    days = channels // 2
    pairs = pair_source.shape[0]
    share = -(-pairs // count)
    cap = max(share * 7 // 16, min(share, 8))
    extra = max(share * 3 // 16, 1)
    mcap = -(-share * 3 // 2 // 16) * 16
    targets = pair_target[:, 0]
    keys = pair_target.reshape(1, 1, pairs) * blocks + pair_block[None, None, :]
    all_keys = lax.all_to_all(
        jnp.broadcast_to(keys, (count, 1, pairs)), "lon", split_axis=0, concat_axis=0, tiled=True
    )
    me = lax.axis_index("lon").astype(I32)[None]
    table, owner, pres = make_plan(me, all_keys, pair_source, count, blocks, cap, extra, mcap)
    moments = lax.cond(
        table[4, 3] == 0,
        lambda: direct(
            cap, extra, mcap, source_fields, weight_blocks, me, all_keys, table, owner, pres
        ),
        lambda: padded_exchange(source_fields, weight_blocks, pair_source, targets, pair_block),
    )
    lon_band = band_matrix(LON_DEV)
    lat_band = band_matrix(LAT_DEV)
    taller = padded(moments, (("lat", 1),), WINDOW_HALF, False)
    wider = padded(taller, (("lon", 2),), WINDOW_HALF, True).astype(F32)
    smoothed = smooth_lat(smooth_lon(wider, lon_band), lat_band)
    kernel = gaussian_taps()
    height = LAT_DEV * lax.axis_size("lat")
    rows = (
        lax.axis_index("lat") * LAT_DEV
        + jnp.arange(LAT_DEV, dtype=jnp.int32)[:, None]
        + jnp.arange(2 * WINDOW_HALF + 1, dtype=jnp.int32)[None, :]
        - WINDOW_HALF
    )
    inside = ((rows >= 0) & (rows < height)).astype(jnp.float32)
    lat_total = jnp.sum(inside * kernel[None, :], axis=1)
    weight_total = lat_total[:, None] * (jnp.sum(kernel) * days)
    mean_temper = smoothed[0] / weight_total
    mean_moist = smoothed[1] / weight_total
    var_temper = smoothed[2] / weight_total - mean_temper * mean_temper
    var_moist = smoothed[3] / weight_total - mean_moist * mean_moist
    covar = smoothed[4] / weight_total - mean_temper * mean_moist
    return covar / jnp.sqrt(var_temper * var_moist + 1e-06)


def solution(mesh):
    placed = (
        P(("lat", "lon"), None, None),
        P(("lat", "lon"), None, None),
        P(("lat", "lon")),
        P(("lat", "lon"), None),
        P(("lat", "lon")),
    )
    return jax.shard_map(
        local, mesh=mesh, in_specs=placed, out_specs=P("lat", "lon"), check_vma=False
    )
```

```python
import functools

import jax
import jax.numpy as jnp
from jax import lax
from jax.experimental import pallas as pl
from jax.experimental.pallas import tpu as pltpu
from jax.sharding import PartitionSpec as P

WINDOW_HALF = 16
LAT_DEV = 64
LON_DEV = 512
LANES = 128
GROUP = 8
CHUNK = 16
F32 = jnp.float32
BF16 = jnp.bfloat16
I32 = jnp.int32


def padded(x, sides, width, wrap):
    for axis, dim in sides:
        count, length = (lax.axis_size(axis), x.shape[dim])
        up = [(i, (i + 1) % count) for i in range(count if wrap else count - 1)]
        down = [(j, i) for i, j in up]
        last = lax.slice_in_dim(x, length - width, length, axis=dim)
        leading = lax.slice_in_dim(x, 0, width, axis=dim)
        before = lax.ppermute(last, axis, up)
        after = lax.ppermute(leading, axis, down)
        x = jnp.concatenate([before, x, after], axis=dim)
    return x


def gaussian_taps():
    offsets = jnp.arange(2 * WINDOW_HALF + 1).astype(jnp.float32) - WINDOW_HALF
    return jnp.exp(-offsets * offsets / (0.5 * WINDOW_HALF * WINDOW_HALF))


def band_matrix(length):
    outer = jnp.arange(length + 2 * WINDOW_HALF, dtype=jnp.int32)[:, None]
    inner = jnp.arange(length, dtype=jnp.int32)[None, :]
    offsets = (outer - inner - WINDOW_HALF).astype(jnp.float32)
    values = jnp.exp(-offsets * offsets / (0.5 * WINDOW_HALF * WINDOW_HALF))
    return jnp.where(jnp.abs(offsets) <= WINDOW_HALF, values, 0.0)


def smooth_lon(fields, lon_band):
    return jnp.einsum("krb,bj->krj", fields, lon_band, precision=lax.Precision.HIGHEST)


def smooth_lat(fields, lat_band):
    return jnp.einsum("ai,kaj->kij", lat_band, fields, precision=lax.Precision.HIGHEST)


def iota(shape, dim):
    return lax.broadcasted_iota(I32, shape, dim)


def dot(a, b, dims=((1,), (0,)), exact=False):
    return lax.dot_general(
        a,
        b,
        (dims, ((), ())),
        preferred_element_type=F32,
        precision=lax.Precision.HIGHEST if exact else None,
    )


def repeat(count, body, carry):
    if count <= 8:
        for step in range(count):
            carry = body(step, carry)
        return carry
    return lax.fori_loop(0, count, body, carry)


def one_hots(row, height):
    pairs = row.shape[1]
    high = (iota((height, pairs), 0) == (row >> 7)).astype(F32)
    low = (iota((LANES, pairs), 0) == (row & (LANES - 1))).astype(F32)
    return high, low


def split_dot(table, other, dims=((1,), (0,))):
    upper = jnp.floor(table * (1.0 / 256.0))
    lower = table - upper * 256.0
    other = other.astype(BF16)
    return dot(upper.astype(BF16), other, dims) * 256.0 + dot(lower.astype(BF16), other, dims)


def look_up(table, high, low):
    return jnp.sum(split_dot(table, low) * high, axis=0, keepdims=True)


def prefixes(height, tile_rows):
    ahead = (iota((LANES, LANES), 0) < iota((LANES, LANES), 1)).astype(BF16)
    ones = jnp.ones((LANES, LANES), BF16)
    ahead_total = jnp.concatenate([ahead, ones], axis=1)
    up, down = iota((height, height), 1), iota((height, height), 0)
    rows_ahead = (up < down).astype(BF16)
    same_tile = ((up < down) & (up // tile_rows == down // tile_rows)).astype(BF16)

    def prefix(mask, rows):
        both = dot(mask.astype(BF16), ahead_total)
        return both[:, :LANES] + dot(rows, both[:, LANES:].astype(BF16))

    return prefix, rows_ahead, same_tile


def as_float(d):
    return float(d) if isinstance(d, int) else lax.convert_element_type(d, F32)


def load_all(sources, targets, sem):
    copies = []
    for source, target in zip(sources, targets):
        rows = source.shape[0] // 4
        for c in range(4):
            part = pl.ds(c * rows, rows)
            copies.append(pltpu.make_async_copy(source.at[part], target.at[part], sem.at[len(copies)]))
    return copies


def plan_kernel(
    count, blocks, cap, extra, mcap, parts, me_ref, keys_ref, src_ref, fields, weights, *refs
):
    table_ref, owner_ref, pres, far_ref = refs[:4]
    near_refs = refs[4 : 4 + parts]
    tall, xs, ws, total, packed, table, load_sem, table_sem, out_sem = refs[4 + parts :]
    loading = load_all((fields, weights), (xs, ws), load_sem)
    for copy in loading:
        copy.start()
    make_table(count, blocks, cap, extra, mcap, me_ref, keys_ref, src_ref, table_ref, owner_ref, pres, tall)
    to_scalar = pltpu.make_async_copy(table_ref, table, table_sem)
    to_scalar.start()
    for copy in loading:
        copy.wait()
    to_scalar.wait()
    sends = packed.shape[0] - 1
    first = count * cap
    high = (table[4, 0] + GROUP - 1) // GROUP * GROUP
    products(table, xs, ws, 0, high, total, packed, 0, sends, sends)
    outs = [pltpu.make_async_copy(packed.at[pl.ds(0, first)], far_ref, out_sem.at[0])]
    for j in range(parts):
        rows = pl.ds(first + j * extra, extra)
        outs.append(pltpu.make_async_copy(packed.at[rows], near_refs[j], out_sem.at[1 + j]))
    for out in outs:
        out.start()
    for out in outs:
        out.wait()


def make_table(
    count, blocks, cap, extra, mcap, me_ref, keys_ref, src_ref, table_ref, owner_ref, pres, tall
):
    me = me_ref[0]
    pairs = keys_ref.shape[2]
    height = count * blocks // LANES
    tile_rows = blocks // LANES
    half = count // 2
    sends = count * cap + (half - 1) * extra

    def held(d, carry):
        high, low = one_hots(keys_ref[d], height)
        found = dot(high.astype(BF16), low.astype(BF16), ((1,), (1,)))
        found = (found > 0.5).astype(F32)
        pres[d] = found
        tall[pl.ds(d, height, stride=count), :] = found
        return carry

    repeat(count, held, 0)

    zero = jnp.zeros((height, LANES), F32)
    holders = repeat(count, lambda d, total: total + pres[d], zero)
    device = iota((count, LANES), 0)
    turn = (device + count - iota((count, LANES), 1) % count) % count
    turn = turn.astype(F32)
    others = [(device != s).astype(F32) for s in range(count)]
    near = [(device // half == s // half).astype(F32) for s in range(count)]
    weight = [1.0 - 0.8 * near[s] for s in range(count)]
    part = iota((count, LANES), 1) * 2 // LANES
    sides = [(part == h).astype(F32) for h in range(2)]

    def rows_of(r):
        return pl.ds(pl.multiple_of(r * count, count), count)

    def expect(r, sums):
        here = tall[rows_of(r), :]
        even = here / jnp.maximum(jnp.sum(here, axis=0, keepdims=True), 1.0)
        return tuple(sums[s] + even * here[s : s + 1, :] for s in range(count))

    nothing = tuple(jnp.zeros((count, LANES), F32) for _ in range(count))
    sums = lax.fori_loop(0, height, expect, nothing)
    loads = tuple(
        jnp.broadcast_to(jnp.sum(sums[s], axis=1, keepdims=True), (count, LANES)) * others[s]
        for s in range(count)
    )

    def settle(r, loads):
        here = tall[rows_of(r), :]
        even = here / jnp.maximum(jnp.sum(here, axis=0, keepdims=True), 1.0)
        picks = jnp.zeros((count, LANES), F32)
        for side in sides:
            cost = jnp.zeros((count, LANES), F32)
            for s in range(count):
                growth = loads[s] * loads[s]
                cost = cost + weight[s] * growth * growth * here[s : s + 1, :]
            cost = jnp.where(here > 0.5, cost, 1e30)
            best = jnp.min(cost, axis=0, keepdims=True)
            place_in_turn = jnp.where(cost == best, turn, 1e30)
            nearest = jnp.min(place_in_turn, axis=0, keepdims=True)
            pick = jnp.where(place_in_turn == nearest, here, 0.0) * side
            picks = picks + pick
            change = pick - even * side
            loads = tuple(
                loads[s] + others[s] * jnp.sum(change * here[s : s + 1, :], axis=1, keepdims=True)
                for s in range(count)
            )
        tall[rows_of(r), :] = picks
        return loads

    loads = lax.fori_loop(0, height, settle, loads)
    far_most, near_most = loads[0] * (1.0 - near[0]), loads[0] * near[0]
    for s in range(1, count):
        far_most = jnp.maximum(far_most, loads[s] * (1.0 - near[s]))
        near_most = jnp.maximum(near_most, loads[s] * near[s])

    def tile_most(o, most):
        sums = tall[rows_of(o * tile_rows), :]
        for i in range(1, tile_rows):
            sums = sums + tall[rows_of(o * tile_rows + i), :]
        return jnp.maximum(most, jnp.sum(sums, axis=1, keepdims=True))

    most = repeat(count, tile_most, jnp.zeros((count, 1), F32))
    fits = (far_most < cap + 0.25) & (near_most < cap + extra + 0.25) & (most < mcap + 0.5)
    fits = jnp.min(jnp.min(fits.astype(F32), axis=1, keepdims=True), axis=0, keepdims=True)
    over = 1 - fits.astype(I32)

    def own(d, owner):
        return jnp.where(tall[pl.ds(d, height, stride=count), :] > 0.5, d, owner)

    owner = repeat(count, own, jnp.full((height, LANES), -1, I32))
    owner_ref[...] = owner
    prefix, rows_ahead, _ = prefixes(height, tile_rows)
    mine = (owner == me).astype(F32)
    several = mine * (holders > 1.5).astype(F32)
    single = mine - several
    rank_several = prefix(several, rows_ahead)
    rank_single = prefix(single, rows_ahead)
    total_several = jnp.sum(several, axis=(0, 1), keepdims=True)
    total_mine = jnp.sum(mine, axis=(0, 1), keepdims=True)
    held_here = pres[me]

    def route(d, place):
        away = jnp.where(d == me, 0.0, 1.0)
        leaving = held_here * (owner == d).astype(F32) * away
        rank = prefix(leaving, rows_ahead)
        first = as_float(d) * cap + rank
        steps = ((d % half + half - me % half) % half).astype(F32)
        second = count * cap + (steps - 1.0) * extra + rank - cap
        return place + leaving * (jnp.where(rank < cap - 0.5, first, second) + 1.0)

    place = repeat(count, route, zero)
    place = place + several * (sends + rank_several + 1.0)
    place = place + single * (sends + total_several + rank_single + 1.0)
    high, low = one_hots(keys_ref[me], height)
    goes = look_up(place, high, low) - 1.0
    leaving = jnp.sum((goes < sends - 0.5).astype(F32), axis=1, keepdims=True)
    first_at, second_at = iota((pairs, pairs), 0), iota((pairs, pairs), 1)
    kind = iota((8, pairs), 0)
    same = (first_at == second_at).astype(F32)
    parts = jnp.where(kind == 0, jnp.floor(goes * (1.0 / 256.0)), 0.0)
    parts = jnp.where(kind == 1, goes - 256.0 * parts[0:1, :], parts)
    upright = dot(same.astype(BF16), parts.astype(BF16), ((1,), (1,)))
    upright = upright[:, 0:1] * 256.0 + upright[:, 1:2]
    earlier = (upright < goes - 0.5) | ((jnp.abs(upright - goes) < 0.5) & (first_at < second_at))
    position = jnp.sum(earlier.astype(F32), axis=0, keepdims=True)
    at = iota((1, pairs), 1).astype(F32)
    values = jnp.where(
        kind == 0,
        at,
        jnp.where(kind == 1, goes, jnp.where(kind == 2, src_ref[...].astype(F32), 0.0)),
    )
    order = (first_at == (position + 0.5).astype(I32)).astype(F32)
    result = (split_dot(values, order, ((1,), (1,))) + 0.5).astype(I32)
    lane = iota((8, pairs), 1)
    facts = jnp.where(lane == 0, leaving.astype(I32), over)
    facts = jnp.where(lane == 1, total_mine.astype(I32), facts)
    facts = jnp.where(lane == 2, total_several.astype(I32), facts)
    facts = jnp.where(lane == 4, me, facts)
    result = jnp.where(kind == 4, facts, result)
    table_ref[...] = jnp.where(kind == 5, (goes + 0.5).astype(I32), result)


def finish_kernel(
    count, blocks, sends, mcap, me_ref, keys_ref, owner_ref, pres, table_ref, entry_ref, spot_ref, landing_ref
):
    me = me_ref[0]
    pairs = keys_ref.shape[2]
    height = count * blocks // LANES
    tile_rows = blocks // LANES
    prefix, rows_ahead, same_tile = prefixes(height, tile_rows)
    owner = owner_ref[...]
    zero = jnp.zeros((height, LANES), F32)
    holders = repeat(count, lambda d, total: total + pres[d], zero)
    mine = (owner == me).astype(F32)
    rank_several = prefix(mine * (holders > 1.5).astype(F32), rows_ahead)
    entry_rows = entry_ref.shape[0] - 8
    lane_at = iota((entry_rows, LANES), 1)
    first_lane = iota((8, LANES), 1)

    def route(d, carry):
        finished, entries, counts = carry
        away = jnp.where(d == me, 0.0, 1.0)
        theirs = (owner == d).astype(F32)
        rank_theirs = prefix(theirs, same_tile)
        finished = finished + theirs * (as_float(d) * mcap + rank_theirs + 1.0)
        coming = pres[d] * mine * away
        rank_coming = prefix(coming, rows_ahead)
        code = coming * (rank_coming * 1024.0 + rank_several + 1.0)
        high, low = one_hots(keys_ref[d], height)
        seen = jnp.sum(dot(code, low, exact=True) * high, axis=0, keepdims=True)
        seen = (seen + 0.5).astype(I32) - 1
        rank, local = seen >> 10, seen & 1023
        hit = iota((entry_rows, pairs), 0) == rank
        column = jnp.max(jnp.where(hit, local, -1), axis=1, keepdims=True)
        entries = jnp.where(lane_at == d, column, entries)
        arrivals = jnp.sum(coming, axis=(0, 1), keepdims=True).astype(I32)
        counts = jnp.where(first_lane == d, arrivals, counts)
        return finished, entries, counts

    finished, entries, counts = repeat(
        count,
        route,
        (zero, jnp.full((entry_rows, LANES), -1, I32), jnp.zeros((8, LANES), I32)),
    )
    entry_ref[:entry_rows, :] = entries
    entry_ref[entry_rows:, :] = counts
    pick = (iota((8, height), 1) == me * tile_rows + iota((8, height), 0)).astype(F32)
    spot_ref[...] = (dot(pick, finished, exact=True) + 0.5).astype(I32) - 1
    tile_of = (iota((height, LANES), 0) // tile_rows).astype(F32)
    moment_place = mine * (tile_of * mcap + finished - 1.0 - me.astype(F32) * mcap)
    high, low = one_hots(keys_ref[me], height)
    lands = look_up(moment_place, high, low)
    goes = table_ref[5:6, :]
    slot = jnp.where(goes < sends, -1, goes - sends)
    in_slot = (iota((pairs, pairs), 0) == slot).astype(F32)
    weighed = jnp.where(iota((8, pairs), 0) == 0, lands, 1.0)
    summed = split_dot(weighed, in_slot, ((1,), (1,)))
    landing = summed[0:1, :] / jnp.maximum(summed[1:2, :], 1.0)
    landing_ref[...] = jnp.broadcast_to((landing + 0.25).astype(I32), landing_ref.shape)


def make_plan(me, keys, pair_source, fields, weights, cap, extra, mcap):
    count, _, pairs = keys.shape
    blocks, channels, cells = fields.shape
    height = count * blocks // LANES
    parts = count // 2 - 1
    first = count * cap
    sends = first + parts * extra
    vmem = pl.BlockSpec(memory_space=pltpu.VMEM)
    hbm = pl.BlockSpec(memory_space=pl.ANY)
    table, owner, pres, *sent = pl.pallas_call(
        functools.partial(plan_kernel, count, blocks, cap, extra, mcap, parts),
        out_shape=[
            jax.ShapeDtypeStruct((8, pairs), I32),
            jax.ShapeDtypeStruct((height, LANES), I32),
            jax.ShapeDtypeStruct((count, height, LANES), F32),
            jax.ShapeDtypeStruct((first, channels, cells), BF16),
        ]
        + [jax.ShapeDtypeStruct((extra, channels, cells), BF16)] * parts,
        in_specs=[pl.BlockSpec(memory_space=pltpu.SMEM), vmem, vmem, hbm, hbm],
        out_specs=[vmem] * 3 + [hbm] * (1 + parts),
        scratch_shapes=[
            pltpu.VMEM((height * count, LANES), F32),
            pltpu.VMEM(fields.shape, BF16),
            pltpu.VMEM(weights.shape, BF16),
            pltpu.VMEM((sends + 1, channels, cells), F32),
            pltpu.VMEM((sends + 1, channels, cells), BF16),
            pltpu.SMEM((8, pairs), I32),
            pltpu.SemaphoreType.DMA((8,)),
            pltpu.SemaphoreType.DMA,
            pltpu.SemaphoreType.DMA((1 + parts,)),
        ],
        compiler_params=pltpu.CompilerParams(vmem_limit_bytes=53 << 20),
        name="leaving",
    )(me, keys, pair_source[None, :], fields, weights)
    return table, owner, pres, sent


def finish_plan(me, keys, owner, pres, table, count, blocks, cap, extra, mcap):
    pairs = keys.shape[2]
    entry_rows = -(-(cap + extra) // 8) * 8 + 8
    sends = count * cap + (count // 2 - 1) * extra
    vmem = pl.BlockSpec(memory_space=pltpu.VMEM)
    return pl.pallas_call(
        functools.partial(finish_kernel, count, blocks, sends, mcap),
        out_shape=(
            jax.ShapeDtypeStruct((entry_rows, LANES), I32),
            jax.ShapeDtypeStruct((8, LANES), I32),
            jax.ShapeDtypeStruct((8, pairs), I32),
        ),
        in_specs=[pl.BlockSpec(memory_space=pltpu.SMEM)] + [vmem] * 4,
        out_specs=(vmem, vmem, vmem),
        compiler_params=pltpu.CompilerParams(vmem_limit_bytes=8 << 20),
        name="finish",
    )(me, keys, owner, pres, table)


def products(table, xs, ws, low, high, target, packed, first, last, dummy):
    def step(g, carry):
        base = g * GROUP
        results = []
        for u in range(GROUP):
            x, w = xs[table[2, base + u]], ws[table[0, base + u]]
            results.append(dot(x, w, ((1,), (1,))))
        for u in range(GROUP):
            i = base + u
            place = table[1, i]
            again = (i > low) & (table[1, jnp.maximum(i - 1, 0)] == place)
            inside = (place >= first) & (place < last)
            where = jnp.where(inside, place - first, dummy)
            value = results[u] + jnp.where(again, target[where], 0.0)
            target[where] = value
            if packed is not None:
                packed[where] = value.astype(BF16)
        return carry

    lax.fori_loop(low // GROUP, high // GROUP, step, 0)


def moment_rows(value):
    days = value.shape[0] // 2
    temper, moist = value[:days], value[days:]
    return [
        jnp.sum(each, axis=0, keepdims=True)
        for each in (temper, moist, temper * temper, moist * moist, temper * moist)
    ]


def put_moments(landing, total, moments, spare, begin, end):
    def some(g, carry):
        for u in range(4):
            i = begin + g * 4 + u
            good = i < end
            at = jnp.where(good, i, 0)
            place = jnp.where(good, jnp.minimum(landing[0, at], spare), spare)
            for k, row in enumerate(moment_rows(total[at])):
                moments[k, pl.ds(place, 1), :] = row
        return carry

    lax.fori_loop(0, (end - begin + 3) // 4, some, 0)


def chunk_copies(source, target, sem, c):
    rows = pl.ds(c * CHUNK, CHUNK)
    return pltpu.make_async_copy(source.at[rows], target.at[rows], sem.at[c])


def local_kernel(
    sends, table, landing, fields, weights, local_ref, moments, total, xs, ws, load_sem, out_sem
):
    pairs = weights.shape[0]
    leaving, owned, several = table[4, 0], table[4, 1], table[4, 2]
    low = leaving // GROUP * GROUP
    loading = load_all((fields, weights), (xs, ws), load_sem)
    for copy in loading:
        copy.start()
    moments[...] = jnp.zeros(moments.shape, F32)
    for copy in loading:
        copy.wait()
    products(table, xs, ws, low, pairs, total, None, sends, sends + pairs, pairs)
    chunks = (several + CHUNK - 1) // CHUNK

    def begin(c, carry):
        chunk_copies(total, local_ref, out_sem, c).start()
        return carry

    lax.fori_loop(0, chunks, begin, 0)
    put_moments(landing, total, moments, moments.shape[1] - 8, several, owned)

    def end(c, carry):
        chunk_copies(total, local_ref, out_sem, c).wait()
        return carry

    lax.fori_loop(0, chunks, end, 0)


def merge_kernel(count, cap, extra, mcap, table, landing, entry, local_ref, moments_in, far_ref, *refs):
    parts = count // 2 - 1
    near_refs = refs[:parts]
    out_ref, total, near, moments, in_sem, near_sem, moment_sem = refs[parts:]
    several, me = table[4, 2], table[4, 4]
    half = count // 2
    spare = total.shape[0] - 1
    counts_row = entry.shape[0] - 8
    chunks = (several + CHUNK - 1) // CHUNK

    def begin(c, carry):
        chunk_copies(local_ref, total, in_sem, c).start()
        return carry

    near_copies = [
        pltpu.make_async_copy(near_refs[j], near.at[pl.ds(j * extra, extra)], near_sem.at[j])
        for j in range(parts)
    ]
    lax.fori_loop(0, chunks, begin, 0)
    for near_copy in near_copies:
        near_copy.start()
    moment_copy = pltpu.make_async_copy(moments_in, moments, moment_sem)
    moment_copy.start()

    def end(c, carry):
        chunk_copies(local_ref, total, in_sem, c).wait()
        return carry

    lax.fori_loop(0, chunks, end, 0)

    def add(s, low, high, came, shift):
        def some(g, inner):
            for u in range(4):
                r = low + g * 4 + u
                good = r < high
                at = jnp.where(good, r, low)
                where = jnp.where(good, jnp.maximum(entry[at, s], 0), spare)
                total[where] = total[where] + came[shift + at].astype(F32)
            return inner

        lax.fori_loop(0, (high - low + 3) // 4, some, 0)

    def from_far(s, carry):
        add(s, 0, jnp.minimum(entry[counts_row, s], cap), far_ref, s * cap)
        return carry

    lax.fori_loop(0, count, from_far, 0)
    for near_copy in near_copies:
        near_copy.wait()

    def from_near(j, carry):
        s = me // half * half + (me % half + half - j - 1) % half
        number = jnp.clip(entry[counts_row, s], cap, cap + extra)
        add(s, cap, number, near, j * extra - cap)
        return carry

    lax.fori_loop(0, parts, from_near, 0)
    moment_copy.wait()
    put_moments(landing, total, moments, moments.shape[1] - 8, 0, several)
    for o in range(count):
        for k in range(5):
            out_ref[o, k] = moments[k, o * mcap : (o + 1) * mcap, :].astype(BF16)


def spread_kernel(count, mcap, spot_ref, came, map_ref, flat):
    rows, blocks_wide = map_ref.shape[1], map_ref.shape[2] // LANES
    for a in range(count):
        for k in range(5):
            flat[a * mcap : (a + 1) * mcap, k * LANES : (k + 1) * LANES] = came[a, k]
    chosen = (iota((spot_ref.shape[0], count * mcap), 1) == spot_ref[...]).astype(F32)
    laid = dot(chosen.astype(BF16), flat[...])
    for q in range(blocks_wide):
        for k in range(5):
            map_ref[k, :, q * LANES : (q + 1) * LANES] = laid[
                q * rows : (q + 1) * rows, k * LANES : (k + 1) * LANES
            ].astype(BF16)


def direct(cap, extra, mcap, source_fields, weight_blocks, me, keys, table, owner, pres, sent):
    count = lax.axis_size("lon")
    half = count // 2
    blocks, channels, cells = source_fields.shape
    pairs = weight_blocks.shape[0]
    parts = half - 1
    first = count * cap
    sends = first + parts * extra
    smem = pl.BlockSpec(memory_space=pltpu.SMEM)
    vmem = pl.BlockSpec(memory_space=pltpu.VMEM)
    hbm = pl.BlockSpec(memory_space=pl.ANY)
    far = lax.all_to_all(
        sent[0].reshape(count, cap, channels, cells), "lon", split_axis=0, concat_axis=0, tiled=True
    ).reshape(first, channels, cells)
    near = []
    for j in range(parts):
        turn = [(i, i // half * half + (i % half + j + 1) % half) for i in range(count)]
        near.append(lax.ppermute(sent[1 + j], "lon", turn))
    entry, spot, landing = finish_plan(
        me, keys, owner, pres, table, count, blocks, cap, extra, mcap
    )
    chunk_count = -(-pairs // CHUNK)
    local, moments = pl.pallas_call(
        functools.partial(local_kernel, sends),
        out_shape=(
            jax.ShapeDtypeStruct((pairs, channels, cells), F32),
            jax.ShapeDtypeStruct((5, count * mcap + 8, cells), F32),
        ),
        in_specs=[smem, smem, hbm, hbm],
        out_specs=(hbm, vmem),
        scratch_shapes=[
            pltpu.VMEM((pairs + 1, channels, cells), F32),
            pltpu.VMEM(source_fields.shape, BF16),
            pltpu.VMEM(weight_blocks.shape, BF16),
            pltpu.SemaphoreType.DMA((8,)),
            pltpu.SemaphoreType.DMA((chunk_count,)),
        ],
        compiler_params=pltpu.CompilerParams(vmem_limit_bytes=50 << 20),
        name="staying",
    )(table, landing, source_fields, weight_blocks)
    finished = pl.pallas_call(
        functools.partial(merge_kernel, count, cap, extra, mcap),
        out_shape=jax.ShapeDtypeStruct((count, 5, mcap, cells), BF16),
        in_specs=[smem, smem, smem, hbm, hbm, vmem] + [hbm] * parts,
        out_specs=vmem,
        scratch_shapes=[
            pltpu.VMEM((pairs + 1, channels, cells), F32),
            pltpu.VMEM((parts * extra, channels, cells), BF16),
            pltpu.VMEM((5, count * mcap + 8, cells), F32),
            pltpu.SemaphoreType.DMA((chunk_count,)),
            pltpu.SemaphoreType.DMA((parts,)),
            pltpu.SemaphoreType.DMA,
        ],
        compiler_params=pltpu.CompilerParams(vmem_limit_bytes=50 << 20),
        name="merge",
    )(table, landing, entry, local, moments, far, *near)
    arrived = lax.all_to_all(finished, "lon", split_axis=0, concat_axis=0, tiled=True)
    wide = LON_DEV // cells
    where = spot.reshape(-1)[:blocks].reshape(LAT_DEV, wide).T.reshape(blocks, 1)
    return pl.pallas_call(
        functools.partial(spread_kernel, count, mcap),
        out_shape=jax.ShapeDtypeStruct((5, LAT_DEV, LON_DEV), BF16),
        in_specs=[vmem, vmem],
        out_specs=vmem,
        scratch_shapes=[pltpu.VMEM((count * mcap, 5 * cells), BF16)],
        compiler_params=pltpu.CompilerParams(vmem_limit_bytes=8 << 20),
        name="spread",
    )(where, arrived)


def padded_exchange(source_fields, weight_blocks, pair_source, targets, pair_block):
    lon_count = lax.axis_size("lon")
    pair_count = pair_source.shape[0]
    capacity = max(2, 2 * pair_count // lon_count)
    blocks_dev, channels, cell_count = source_fields.shape
    lanes = jnp.arange(lon_count, dtype=jnp.int32)
    matches = (targets[:, None] == lanes[None, :]).astype(jnp.int32)
    earlier = jnp.cumsum(matches, axis=0) - matches
    slots = jnp.sum(earlier * matches, axis=1)
    position = targets * capacity + slots
    outgoing = jnp.zeros((lon_count * capacity,), jnp.int32).at[position].set(pair_block)
    arriving = lax.all_to_all(
        outgoing.reshape(lon_count, capacity), "lon", split_axis=0, concat_axis=0, tiled=True
    )
    picked = source_fields[pair_source]
    terms = jnp.einsum("pck,pjk->pcj", picked, weight_blocks, preferred_element_type=jnp.float32)
    packed = (
        jnp.zeros((lon_count * capacity, channels, cell_count), jnp.float32).at[position].set(terms)
    )
    received = lax.all_to_all(
        packed.reshape(lon_count, capacity, channels, cell_count).astype(jnp.bfloat16),
        "lon",
        split_axis=0,
        concat_axis=0,
        tiled=True,
    ).astype(jnp.float32)
    remapped = jax.ops.segment_sum(
        received.reshape(lon_count * capacity, channels, cell_count),
        arriving.reshape(-1),
        num_segments=blocks_dev,
    )
    days = channels // 2
    temper = remapped[:, :days]
    moist = remapped[:, days:]
    moments = jnp.stack(
        [
            temper.sum(1),
            moist.sum(1),
            (temper * temper).sum(1),
            (moist * moist).sum(1),
            (temper * moist).sum(1),
        ]
    )
    return moments.reshape(5, LAT_DEV, LON_DEV).astype(BF16)


def local(source_fields, weight_blocks, pair_source, pair_target, pair_block):
    count = lax.axis_size("lon")
    blocks, channels, _ = source_fields.shape
    days = channels // 2
    pairs = pair_source.shape[0]
    share = -(-pairs // count)
    cap = max(share * 7 // 16, min(share, 8))
    extra = max(share * 3 // 16, 1)
    mcap = -(-share * 3 // 2 // 16) * 16
    targets = pair_target[:, 0]
    keys = pair_target.reshape(1, 1, pairs) * blocks + pair_block[None, None, :]
    all_keys = lax.all_to_all(
        jnp.broadcast_to(keys, (count, 1, pairs)), "lon", split_axis=0, concat_axis=0, tiled=True
    )
    me = lax.axis_index("lon").astype(I32)[None]
    table, owner, pres, sent = make_plan(
        me, all_keys, pair_source, source_fields, weight_blocks, cap, extra, mcap
    )
    sent, owner = lax.optimization_barrier((sent, owner))
    moments = direct(
        cap, extra, mcap, source_fields, weight_blocks, me, all_keys, table, owner, pres, sent
    )
    moments = lax.cond(
        table[4, 3] == 0,
        lambda kept: kept,
        lambda kept: padded_exchange(
            source_fields, weight_blocks, pair_source, targets, pair_block
        ),
        moments,
    )
    lon_band = band_matrix(LON_DEV)
    lat_band = band_matrix(LAT_DEV)
    taller = padded(moments, (("lat", 1),), WINDOW_HALF, False)
    wider = padded(taller, (("lon", 2),), WINDOW_HALF, True).astype(F32)
    smoothed = smooth_lat(smooth_lon(wider, lon_band), lat_band)
    kernel = gaussian_taps()
    height = LAT_DEV * lax.axis_size("lat")
    rows = (
        lax.axis_index("lat") * LAT_DEV
        + jnp.arange(LAT_DEV, dtype=jnp.int32)[:, None]
        + jnp.arange(2 * WINDOW_HALF + 1, dtype=jnp.int32)[None, :]
        - WINDOW_HALF
    )
    inside = ((rows >= 0) & (rows < height)).astype(jnp.float32)
    lat_total = jnp.sum(inside * kernel[None, :], axis=1)
    weight_total = lat_total[:, None] * (jnp.sum(kernel) * days)
    mean_temper = smoothed[0] / weight_total
    mean_moist = smoothed[1] / weight_total
    var_temper = smoothed[2] / weight_total - mean_temper * mean_temper
    var_moist = smoothed[3] / weight_total - mean_moist * mean_moist
    covar = smoothed[4] / weight_total - mean_temper * mean_moist
    return covar / jnp.sqrt(var_temper * var_moist + 1e-06)


def solution(mesh):
    placed = (
        P(("lat", "lon"), None, None),
        P(("lat", "lon"), None, None),
        P(("lat", "lon")),
        P(("lat", "lon"), None),
        P(("lat", "lon")),
    )
    return jax.shard_map(
        local, mesh=mesh, in_specs=placed, out_specs=P("lat", "lon"), check_vma=False
    )
```

```python
import functools

import jax
import jax.numpy as jnp
from jax import lax
from jax.experimental import pallas as pl
from jax.experimental.pallas import tpu as pltpu
from jax.sharding import PartitionSpec as P

WINDOW_HALF = 16
LAT_DEV = 64
LON_DEV = 512
LANES = 128
GROUP = 8
CHUNK = 16
F32 = jnp.float32
BF16 = jnp.bfloat16
I32 = jnp.int32


def padded(x, sides, width, wrap):
    for axis, dim in sides:
        count, length = (lax.axis_size(axis), x.shape[dim])
        up = [(i, (i + 1) % count) for i in range(count if wrap else count - 1)]
        down = [(j, i) for i, j in up]
        last = lax.slice_in_dim(x, length - width, length, axis=dim)
        leading = lax.slice_in_dim(x, 0, width, axis=dim)
        before = lax.ppermute(last, axis, up)
        after = lax.ppermute(leading, axis, down)
        x = jnp.concatenate([before, x, after], axis=dim)
    return x


def gaussian_taps():
    offsets = jnp.arange(2 * WINDOW_HALF + 1).astype(jnp.float32) - WINDOW_HALF
    return jnp.exp(-offsets * offsets / (0.5 * WINDOW_HALF * WINDOW_HALF))


def band_matrix(length):
    outer = jnp.arange(length + 2 * WINDOW_HALF, dtype=jnp.int32)[:, None]
    inner = jnp.arange(length, dtype=jnp.int32)[None, :]
    offsets = (outer - inner - WINDOW_HALF).astype(jnp.float32)
    values = jnp.exp(-offsets * offsets / (0.5 * WINDOW_HALF * WINDOW_HALF))
    return jnp.where(jnp.abs(offsets) <= WINDOW_HALF, values, 0.0)


def smooth_lon(fields, lon_band):
    return jnp.einsum("krb,bj->krj", fields, lon_band, precision=lax.Precision.HIGHEST)


def smooth_lat(fields, lat_band):
    return jnp.einsum("ai,kaj->kij", lat_band, fields, precision=lax.Precision.HIGHEST)


def iota(shape, dim):
    return lax.broadcasted_iota(I32, shape, dim)


def dot(a, b, dims=((1,), (0,)), exact=False):
    return lax.dot_general(
        a,
        b,
        (dims, ((), ())),
        preferred_element_type=F32,
        precision=lax.Precision.HIGHEST if exact else None,
    )


def repeat(count, body, carry):
    if count <= 8:
        for step in range(count):
            carry = body(step, carry)
        return carry
    return lax.fori_loop(0, count, body, carry)


def one_hots(row, height):
    pairs = row.shape[1]
    high = (iota((height, pairs), 0) == (row >> 7)).astype(F32)
    low = (iota((LANES, pairs), 0) == (row & (LANES - 1))).astype(F32)
    return high, low


def split_dot(table, other, dims=((1,), (0,))):
    upper = jnp.floor(table * (1.0 / 256.0))
    lower = table - upper * 256.0
    other = other.astype(BF16)
    return dot(upper.astype(BF16), other, dims) * 256.0 + dot(lower.astype(BF16), other, dims)


def look_up(table, high, low):
    return jnp.sum(split_dot(table, low) * high, axis=0, keepdims=True)


def prefixes(height, tile_rows):
    ahead = (iota((LANES, LANES), 0) < iota((LANES, LANES), 1)).astype(BF16)
    ones = jnp.ones((LANES, LANES), BF16)
    ahead_total = jnp.concatenate([ahead, ones], axis=1)
    up, down = iota((height, height), 1), iota((height, height), 0)
    rows_ahead = (up < down).astype(BF16)
    same_tile = ((up < down) & (up // tile_rows == down // tile_rows)).astype(BF16)

    def prefix(mask, rows):
        both = dot(mask.astype(BF16), ahead_total)
        return both[:, :LANES] + dot(rows, both[:, LANES:].astype(BF16))

    return prefix, rows_ahead, same_tile


def as_float(d):
    return float(d) if isinstance(d, int) else lax.convert_element_type(d, F32)


def load_all(sources, targets, sem):
    copies = []
    for source, target in zip(sources, targets):
        rows = source.shape[0] // 4
        for c in range(4):
            part = pl.ds(c * rows, rows)
            copies.append(pltpu.make_async_copy(source.at[part], target.at[part], sem.at[len(copies)]))
    return copies


def plan_kernel(
    count, blocks, cap, extra, mcap, parts, me_ref, keys_ref, src_ref, fields, weights, *refs
):
    table_ref, owner_ref, pres, far_ref = refs[:4]
    near_refs = refs[4 : 4 + parts]
    tall, xs, ws, total, packed, table, load_sem, table_sem, out_sem = refs[4 + parts :]
    loading = load_all((fields, weights), (xs, ws), load_sem)
    for copy in loading:
        copy.start()
    make_table(count, blocks, cap, extra, mcap, me_ref, keys_ref, src_ref, table_ref, owner_ref, pres, tall)
    to_scalar = pltpu.make_async_copy(table_ref, table, table_sem)
    to_scalar.start()
    for copy in loading:
        copy.wait()
    to_scalar.wait()
    sends = packed.shape[0] - 1
    first = count * cap
    high = (table[4, 0] + GROUP - 1) // GROUP * GROUP
    products(table, xs, ws, 0, high, total, packed, 0, sends, sends)
    outs = [pltpu.make_async_copy(packed.at[pl.ds(0, first)], far_ref, out_sem.at[0])]
    for j in range(parts):
        rows = pl.ds(first + j * extra, extra)
        outs.append(pltpu.make_async_copy(packed.at[rows], near_refs[j], out_sem.at[1 + j]))
    for out in outs:
        out.start()
    for out in outs:
        out.wait()


def make_table(
    count, blocks, cap, extra, mcap, me_ref, keys_ref, src_ref, table_ref, owner_ref, pres, tall
):
    me = me_ref[0]
    pairs = keys_ref.shape[2]
    height = count * blocks // LANES
    tile_rows = blocks // LANES
    half = count // 2
    sends = count * cap + (half - 1) * extra

    def held(d, carry):
        high, low = one_hots(keys_ref[d], height)
        found = dot(high.astype(BF16), low.astype(BF16), ((1,), (1,)))
        found = (found > 0.5).astype(F32)
        pres[d] = found
        tall[pl.ds(d, height, stride=count), :] = found
        return carry

    repeat(count, held, 0)

    zero = jnp.zeros((height, LANES), F32)
    holders = repeat(count, lambda d, total: total + pres[d], zero)
    device = iota((count, LANES), 0)
    turn = (device + count - iota((count, LANES), 1) % count) % count
    turn = turn.astype(F32)
    others = [(device != s).astype(F32) for s in range(count)]
    near = [(device // half == s // half).astype(F32) for s in range(count)]
    weight = [1.0 - 0.8 * near[s] for s in range(count)]
    part = iota((count, LANES), 1) * 2 // LANES
    sides = [(part == h).astype(F32) for h in range(2)]

    def rows_of(r):
        return pl.ds(pl.multiple_of(r * count, count), count)

    def expect(r, sums):
        here = tall[rows_of(r), :]
        even = here / jnp.maximum(jnp.sum(here, axis=0, keepdims=True), 1.0)
        return tuple(sums[s] + even * here[s : s + 1, :] for s in range(count))

    nothing = tuple(jnp.zeros((count, LANES), F32) for _ in range(count))
    sums = lax.fori_loop(0, height, expect, nothing)
    loads = tuple(
        jnp.broadcast_to(jnp.sum(sums[s], axis=1, keepdims=True), (count, LANES)) * others[s]
        for s in range(count)
    )

    def settle(r, loads):
        here = tall[rows_of(r), :]
        even = here / jnp.maximum(jnp.sum(here, axis=0, keepdims=True), 1.0)
        picks = jnp.zeros((count, LANES), F32)
        for side in sides:
            cost = jnp.zeros((count, LANES), F32)
            for s in range(count):
                growth = loads[s] * loads[s]
                cost = cost + weight[s] * growth * growth * here[s : s + 1, :]
            cost = jnp.where(here > 0.5, cost, 1e30)
            best = jnp.min(cost, axis=0, keepdims=True)
            place_in_turn = jnp.where(cost == best, turn, 1e30)
            nearest = jnp.min(place_in_turn, axis=0, keepdims=True)
            pick = jnp.where(place_in_turn == nearest, here, 0.0) * side
            picks = picks + pick
            change = pick - even * side
            loads = tuple(
                loads[s] + others[s] * jnp.sum(change * here[s : s + 1, :], axis=1, keepdims=True)
                for s in range(count)
            )
        tall[rows_of(r), :] = picks
        return loads

    loads = lax.fori_loop(0, height, settle, loads)
    far_most, near_most = loads[0] * (1.0 - near[0]), loads[0] * near[0]
    for s in range(1, count):
        far_most = jnp.maximum(far_most, loads[s] * (1.0 - near[s]))
        near_most = jnp.maximum(near_most, loads[s] * near[s])

    def tile_most(o, most):
        sums = tall[rows_of(o * tile_rows), :]
        for i in range(1, tile_rows):
            sums = sums + tall[rows_of(o * tile_rows + i), :]
        return jnp.maximum(most, jnp.sum(sums, axis=1, keepdims=True))

    most = repeat(count, tile_most, jnp.zeros((count, 1), F32))
    fits = (far_most < cap + 0.25) & (near_most < cap + extra + 0.25) & (most < mcap + 0.5)
    fits = jnp.min(jnp.min(fits.astype(F32), axis=1, keepdims=True), axis=0, keepdims=True)
    over = 1 - fits.astype(I32)

    def own(d, owner):
        return jnp.where(tall[pl.ds(d, height, stride=count), :] > 0.5, d, owner)

    owner = repeat(count, own, jnp.full((height, LANES), -1, I32))
    owner_ref[...] = owner
    prefix, rows_ahead, _ = prefixes(height, tile_rows)
    mine = (owner == me).astype(F32)
    several = mine * (holders > 1.5).astype(F32)
    single = mine - several
    rank_several = prefix(several, rows_ahead)
    rank_single = prefix(single, rows_ahead)
    total_several = jnp.sum(several, axis=(0, 1), keepdims=True)
    total_mine = jnp.sum(mine, axis=(0, 1), keepdims=True)
    held_here = pres[me]

    def route(d, place):
        away = jnp.where(d == me, 0.0, 1.0)
        leaving = held_here * (owner == d).astype(F32) * away
        rank = prefix(leaving, rows_ahead)
        first = as_float(d) * cap + rank
        steps = ((d % half + half - me % half) % half).astype(F32)
        second = count * cap + (steps - 1.0) * extra + rank - cap
        return place + leaving * (jnp.where(rank < cap - 0.5, first, second) + 1.0)

    place = repeat(count, route, zero)
    place = place + several * (sends + rank_several + 1.0)
    place = place + single * (sends + total_several + rank_single + 1.0)
    high, low = one_hots(keys_ref[me], height)
    goes = look_up(place, high, low) - 1.0
    leaving = jnp.sum((goes < sends - 0.5).astype(F32), axis=1, keepdims=True)
    first_at, second_at = iota((pairs, pairs), 0), iota((pairs, pairs), 1)
    kind = iota((8, pairs), 0)
    same = (first_at == second_at).astype(F32)
    parts = jnp.where(kind == 0, jnp.floor(goes * (1.0 / 256.0)), 0.0)
    parts = jnp.where(kind == 1, goes - 256.0 * parts[0:1, :], parts)
    upright = dot(same.astype(BF16), parts.astype(BF16), ((1,), (1,)))
    upright = upright[:, 0:1] * 256.0 + upright[:, 1:2]
    earlier = (upright < goes - 0.5) | ((jnp.abs(upright - goes) < 0.5) & (first_at < second_at))
    position = jnp.sum(earlier.astype(F32), axis=0, keepdims=True)
    at = iota((1, pairs), 1).astype(F32)
    values = jnp.where(
        kind == 0,
        at,
        jnp.where(kind == 1, goes, jnp.where(kind == 2, src_ref[...].astype(F32), 0.0)),
    )
    order = (first_at == (position + 0.5).astype(I32)).astype(F32)
    result = (split_dot(values, order, ((1,), (1,))) + 0.5).astype(I32)
    lane = iota((8, pairs), 1)
    facts = jnp.where(lane == 0, leaving.astype(I32), over)
    facts = jnp.where(lane == 1, total_mine.astype(I32), facts)
    facts = jnp.where(lane == 2, total_several.astype(I32), facts)
    facts = jnp.where(lane == 4, me, facts)
    result = jnp.where(kind == 4, facts, result)
    table_ref[...] = jnp.where(kind == 5, (goes + 0.5).astype(I32), result)


def finish_kernel(
    count, blocks, sends, mcap, me_ref, keys_ref, owner_ref, pres, table_ref, entry_ref, spot_ref, landing_ref
):
    me = me_ref[0]
    pairs = keys_ref.shape[2]
    height = count * blocks // LANES
    tile_rows = blocks // LANES
    prefix, rows_ahead, same_tile = prefixes(height, tile_rows)
    owner = owner_ref[...]
    zero = jnp.zeros((height, LANES), F32)
    holders = repeat(count, lambda d, total: total + pres[d], zero)
    mine = (owner == me).astype(F32)
    rank_several = prefix(mine * (holders > 1.5).astype(F32), rows_ahead)
    entry_rows = entry_ref.shape[0] - 8
    lane_at = iota((entry_rows, LANES), 1)
    first_lane = iota((8, LANES), 1)

    def route(d, carry):
        finished, entries, counts = carry
        away = jnp.where(d == me, 0.0, 1.0)
        theirs = (owner == d).astype(F32)
        rank_theirs = prefix(theirs, same_tile)
        finished = finished + theirs * (as_float(d) * mcap + rank_theirs + 1.0)
        coming = pres[d] * mine * away
        rank_coming = prefix(coming, rows_ahead)
        code = coming * (rank_coming * 1024.0 + rank_several + 1.0)
        high, low = one_hots(keys_ref[d], height)
        seen = jnp.sum(dot(code, low, exact=True) * high, axis=0, keepdims=True)
        seen = (seen + 0.5).astype(I32) - 1
        rank, local = seen >> 10, seen & 1023
        hit = iota((entry_rows, pairs), 0) == rank
        column = jnp.max(jnp.where(hit, local, -1), axis=1, keepdims=True)
        entries = jnp.where(lane_at == d, column, entries)
        arrivals = jnp.sum(coming, axis=(0, 1), keepdims=True).astype(I32)
        counts = jnp.where(first_lane == d, arrivals, counts)
        return finished, entries, counts

    finished, entries, counts = repeat(
        count,
        route,
        (zero, jnp.full((entry_rows, LANES), -1, I32), jnp.zeros((8, LANES), I32)),
    )
    entry_ref[:entry_rows, :] = entries
    entry_ref[entry_rows:, :] = counts
    pick = (iota((8, height), 1) == me * tile_rows + iota((8, height), 0)).astype(F32)
    spot_ref[...] = (dot(pick, finished, exact=True) + 0.5).astype(I32) - 1
    tile_of = (iota((height, LANES), 0) // tile_rows).astype(F32)
    moment_place = mine * (tile_of * mcap + finished - 1.0 - me.astype(F32) * mcap)
    high, low = one_hots(keys_ref[me], height)
    lands = look_up(moment_place, high, low)
    goes = table_ref[5:6, :]
    slot = jnp.where(goes < sends, -1, goes - sends)
    in_slot = (iota((pairs, pairs), 0) == slot).astype(F32)
    weighed = jnp.where(iota((8, pairs), 0) == 0, lands, 1.0)
    summed = split_dot(weighed, in_slot, ((1,), (1,)))
    landing = summed[0:1, :] / jnp.maximum(summed[1:2, :], 1.0)
    over = jnp.broadcast_to(table_ref[4:5, 3:4], (8, pairs))
    landing_ref[...] = jnp.where(iota((8, pairs), 0) == 0, (landing + 0.25).astype(I32), over)


def make_plan(me, keys, pair_source, fields, weights, cap, extra, mcap):
    count, _, pairs = keys.shape
    blocks, channels, cells = fields.shape
    height = count * blocks // LANES
    parts = count // 2 - 1
    first = count * cap
    sends = first + parts * extra
    vmem = pl.BlockSpec(memory_space=pltpu.VMEM)
    hbm = pl.BlockSpec(memory_space=pl.ANY)
    table, owner, pres, *sent = pl.pallas_call(
        functools.partial(plan_kernel, count, blocks, cap, extra, mcap, parts),
        out_shape=[
            jax.ShapeDtypeStruct((8, pairs), I32),
            jax.ShapeDtypeStruct((height, LANES), I32),
            jax.ShapeDtypeStruct((count, height, LANES), F32),
            jax.ShapeDtypeStruct((first, channels, cells), BF16),
        ]
        + [jax.ShapeDtypeStruct((extra, channels, cells), BF16)] * parts,
        in_specs=[pl.BlockSpec(memory_space=pltpu.SMEM), vmem, vmem, hbm, hbm],
        out_specs=[vmem] * 3 + [hbm] * (1 + parts),
        scratch_shapes=[
            pltpu.VMEM((height * count, LANES), F32),
            pltpu.VMEM(fields.shape, BF16),
            pltpu.VMEM(weights.shape, BF16),
            pltpu.VMEM((sends + 1, channels, cells), F32),
            pltpu.VMEM((sends + 1, channels, cells), BF16),
            pltpu.SMEM((8, pairs), I32),
            pltpu.SemaphoreType.DMA((8,)),
            pltpu.SemaphoreType.DMA,
            pltpu.SemaphoreType.DMA((1 + parts,)),
        ],
        compiler_params=pltpu.CompilerParams(vmem_limit_bytes=53 << 20),
        name="leaving",
    )(me, keys, pair_source[None, :], fields, weights)
    return table, owner, pres, sent


def finish_plan(me, keys, owner, pres, table, count, blocks, cap, extra, mcap):
    pairs = keys.shape[2]
    entry_rows = -(-(cap + extra) // 8) * 8 + 8
    sends = count * cap + (count // 2 - 1) * extra
    vmem = pl.BlockSpec(memory_space=pltpu.VMEM)
    return pl.pallas_call(
        functools.partial(finish_kernel, count, blocks, sends, mcap),
        out_shape=(
            jax.ShapeDtypeStruct((entry_rows, LANES), I32),
            jax.ShapeDtypeStruct((8, LANES), I32),
            jax.ShapeDtypeStruct((8, pairs), I32),
        ),
        in_specs=[pl.BlockSpec(memory_space=pltpu.SMEM)] + [vmem] * 4,
        out_specs=(vmem, vmem, vmem),
        compiler_params=pltpu.CompilerParams(vmem_limit_bytes=8 << 20),
        name="finish",
    )(me, keys, owner, pres, table)


def products(table, xs, ws, low, high, target, packed, first, last, dummy):
    def step(g, carry):
        base = g * GROUP
        results = []
        for u in range(GROUP):
            x, w = xs[table[2, base + u]], ws[table[0, base + u]]
            results.append(dot(x, w, ((1,), (1,))))
        for u in range(GROUP):
            i = base + u
            place = table[1, i]
            again = (i > low) & (table[1, jnp.maximum(i - 1, 0)] == place)
            inside = (place >= first) & (place < last)
            where = jnp.where(inside, place - first, dummy)
            value = results[u] + jnp.where(again, target[where], 0.0)
            target[where] = value
            if packed is not None:
                packed[where] = value.astype(BF16)
        return carry

    lax.fori_loop(low // GROUP, high // GROUP, step, 0)


def moment_rows(value):
    days = value.shape[0] // 2
    temper, moist = value[:days], value[days:]
    return [
        jnp.sum(each, axis=0, keepdims=True)
        for each in (temper, moist, temper * temper, moist * moist, temper * moist)
    ]


def put_moments(landing, total, moments, spare, begin, end):
    def some(g, carry):
        for u in range(4):
            i = begin + g * 4 + u
            good = i < end
            at = jnp.where(good, i, 0)
            place = jnp.where(good, jnp.minimum(landing[0, at], spare), spare)
            for k, row in enumerate(moment_rows(total[at])):
                moments[k, pl.ds(place, 1), :] = row
        return carry

    lax.fori_loop(0, (end - begin + 3) // 4, some, 0)


def chunk_copies(source, target, sem, c):
    rows = pl.ds(c * CHUNK, CHUNK)
    return pltpu.make_async_copy(source.at[rows], target.at[rows], sem.at[c])


def local_kernel(
    sends, table, landing, fields, weights, local_ref, moments, total, xs, ws, load_sem, out_sem
):
    pairs = weights.shape[0]
    leaving, owned, several = table[4, 0], table[4, 1], table[4, 2]
    low = leaving // GROUP * GROUP
    loading = load_all((fields, weights), (xs, ws), load_sem)
    for copy in loading:
        copy.start()
    moments[...] = jnp.zeros(moments.shape, F32)
    for copy in loading:
        copy.wait()
    products(table, xs, ws, low, pairs, total, None, sends, sends + pairs, pairs)
    chunks = (several + CHUNK - 1) // CHUNK

    def begin(c, carry):
        chunk_copies(total, local_ref, out_sem, c).start()
        return carry

    lax.fori_loop(0, chunks, begin, 0)
    put_moments(landing, total, moments, moments.shape[1] - 8, several, owned)

    def end(c, carry):
        chunk_copies(total, local_ref, out_sem, c).wait()
        return carry

    lax.fori_loop(0, chunks, end, 0)


def merge_kernel(count, cap, extra, mcap, table, landing, entry, local_ref, moments_in, far_ref, *refs):
    parts = count // 2 - 1
    near_refs = refs[:parts]
    out_ref, total, near, moments, in_sem, near_sem, moment_sem = refs[parts:]
    several, me = table[4, 2], table[4, 4]
    half = count // 2
    spare = total.shape[0] - 1
    counts_row = entry.shape[0] - 8
    chunks = (several + CHUNK - 1) // CHUNK

    def begin(c, carry):
        chunk_copies(local_ref, total, in_sem, c).start()
        return carry

    near_copies = [
        pltpu.make_async_copy(near_refs[j], near.at[pl.ds(j * extra, extra)], near_sem.at[j])
        for j in range(parts)
    ]
    lax.fori_loop(0, chunks, begin, 0)
    for near_copy in near_copies:
        near_copy.start()
    moment_copy = pltpu.make_async_copy(moments_in, moments, moment_sem)
    moment_copy.start()

    def end(c, carry):
        chunk_copies(local_ref, total, in_sem, c).wait()
        return carry

    lax.fori_loop(0, chunks, end, 0)

    def add(s, low, high, came, shift):
        def some(g, inner):
            for u in range(4):
                r = low + g * 4 + u
                good = r < high
                at = jnp.where(good, r, low)
                where = jnp.where(good, jnp.maximum(entry[at, s], 0), spare)
                total[where] = total[where] + came[shift + at].astype(F32)
            return inner

        lax.fori_loop(0, (high - low + 3) // 4, some, 0)

    def from_far(s, carry):
        add(s, 0, jnp.minimum(entry[counts_row, s], cap), far_ref, s * cap)
        return carry

    lax.fori_loop(0, count, from_far, 0)
    for near_copy in near_copies:
        near_copy.wait()

    def from_near(j, carry):
        s = me // half * half + (me % half + half - j - 1) % half
        number = jnp.clip(entry[counts_row, s], cap, cap + extra)
        add(s, cap, number, near, j * extra - cap)
        return carry

    lax.fori_loop(0, parts, from_near, 0)
    moment_copy.wait()
    put_moments(landing, total, moments, moments.shape[1] - 8, 0, several)
    for o in range(count):
        for k in range(5):
            out_ref[o, k] = moments[k, o * mcap : (o + 1) * mcap, :].astype(BF16)


def spread_kernel(count, mcap, spot_ref, came, map_ref, top_ref, bottom_ref, flat):
    rows, blocks_wide = map_ref.shape[1], map_ref.shape[2] // LANES
    for a in range(count):
        for k in range(5):
            flat[a * mcap : (a + 1) * mcap, k * LANES : (k + 1) * LANES] = came[a, k]
    chosen = (iota((spot_ref.shape[0], count * mcap), 1) == spot_ref[...]).astype(F32)
    laid = dot(chosen.astype(BF16), flat[...]).astype(BF16)
    for q in range(blocks_wide):
        for k in range(5):
            tile = laid[q * rows : (q + 1) * rows, k * LANES : (k + 1) * LANES]
            lanes = slice(q * LANES, (q + 1) * LANES)
            map_ref[k, :, lanes] = tile
            top_ref[k, :, lanes] = tile[:WINDOW_HALF]
            bottom_ref[k, :, lanes] = tile[rows - WINDOW_HALF :]


def tap(offset):
    offset = offset.astype(F32)
    value = jnp.exp(-offset * offset / (0.5 * WINDOW_HALF * WINDOW_HALF))
    return jnp.where(jnp.abs(offset) <= WINDOW_HALF, value, 0.0)


def halved(value):
    upper = value.astype(BF16)
    return upper, (value - upper.astype(F32)).astype(BF16)


def bands_kernel(after_ref, upper_ref, lower_ref):
    shape = upper_ref.shape
    upper_ref[...], lower_ref[...] = halved(tap(iota(shape, 0) - iota(shape, 1)))


def across(fields, upper, lower):
    return dot(fields, upper) + dot(fields, lower)


def center_kernel(map_ref, upper, lower, out_ref):
    fields = jnp.concatenate([map_ref[k] for k in range(5)], axis=0)
    rows = map_ref.shape[1]
    smooth = across(fields, upper[...], lower[...])
    for k in range(5):
        out_ref[k] = smooth[k * rows : (k + 1) * rows]


def lat_weights(rows):
    shape = (rows, rows + 2 * WINDOW_HALF)
    return tap(iota(shape, 1) - iota(shape, 0) - WINDOW_HALF)


def rows_kernel(before, after, upper, lower, center, out_ref):
    rows = center.shape[1]
    half = WINDOW_HALF
    fields = jnp.concatenate([before[k] for k in range(5)] + [after[k] for k in range(5)], axis=0)
    smooth = across(fields, upper[...], lower[...])
    weights = lat_weights(rows)
    for k in range(5):
        first = smooth[k * half : (k + 1) * half]
        last = smooth[(5 + k) * half : (6 + k) * half]
        tall = jnp.concatenate([first, center[k], last], axis=0)
        out_ref[k] = dot(weights, tall, exact=True)


def result_kernel(height, days, lat_ref, left, right, partial, out_ref, edges):
    rows, width = out_ref.shape
    half = WINDOW_HALF
    tall = rows + 2 * half
    at, lane = iota((half, LANES), 0), iota((half, LANES), 1)
    for side, (ref, offset) in enumerate(((left, at - half - lane), (right, LANES + at - lane))):
        upper, lower = halved(tap(offset))
        fields = jnp.concatenate([ref[k] for k in range(5)], axis=0)
        smooth = across(fields, upper, lower)
        for k in range(5):
            place = (side * 5 + k) * LANES
            edges[:, place : place + LANES] = smooth[k * tall : (k + 1) * tall]
    beside = dot(lat_weights(rows), edges[...], exact=True)
    k_at = iota((rows, LANES), 1) - half
    row = lat_ref[0] * rows + iota((rows, LANES), 0) + k_at
    taps = tap(k_at)
    inside = jnp.where((row >= 0) & (row < height), taps, 0.0)
    weight = jnp.sum(inside, axis=1, keepdims=True) * (jnp.sum(taps, axis=1, keepdims=True) * days)
    scale = 1.0 / weight
    tiles = width // LANES
    for q in range(tiles):
        lanes = slice(q * LANES, (q + 1) * LANES)
        values = []
        for k in range(5):
            value = partial[k, :, lanes]
            if q == 0:
                value = value + beside[:, k * LANES : (k + 1) * LANES]
            if q == tiles - 1:
                value = value + beside[:, (5 + k) * LANES : (6 + k) * LANES]
            values.append(value * scale)
        mean_t, mean_m, square_t, square_m, cross = values
        var_t = square_t - mean_t * mean_t
        var_m = square_m - mean_m * mean_m
        covar = cross - mean_t * mean_m
        out_ref[:, lanes] = covar / jnp.sqrt(var_t * var_m + 1e-06)


def neighbours(low, high, axis, wrap):
    count = lax.axis_size(axis)
    up = [(i, (i + 1) % count) for i in range(count if wrap else count - 1)]
    down = [(j, i) for i, j in up]
    return lax.ppermute(high, axis, up), lax.ppermute(low, axis, down)


def correlate(days, moments, top, bottom, bands):
    vmem = pl.BlockSpec(memory_space=pltpu.VMEM)
    smem = pl.BlockSpec(memory_space=pltpu.SMEM)
    small = pltpu.CompilerParams(vmem_limit_bytes=16 << 20)
    _, rows, width = moments.shape
    whole = jax.ShapeDtypeStruct(moments.shape, F32)
    before, after = neighbours(top, bottom, "lat", False)
    center = pl.pallas_call(
        center_kernel,
        out_shape=whole,
        in_specs=[vmem] * 3,
        out_specs=vmem,
        compiler_params=small,
        name="center",
    )(moments, *bands)
    before, after, center = lax.optimization_barrier((before, after, center))
    tall = (before, moments, after)
    low = jnp.concatenate([each[:, :, :WINDOW_HALF] for each in tall], axis=1)
    high = jnp.concatenate([each[:, :, width - WINDOW_HALF :] for each in tall], axis=1)
    left, right = neighbours(low, high, "lon", True)
    partial = pl.pallas_call(
        rows_kernel,
        out_shape=whole,
        in_specs=[vmem] * 5,
        out_specs=vmem,
        compiler_params=small,
        name="rows",
    )(before, after, *bands, center)
    height = rows * lax.axis_size("lat")
    return pl.pallas_call(
        functools.partial(result_kernel, height, days),
        out_shape=jax.ShapeDtypeStruct((rows, width), F32),
        in_specs=[smem, vmem, vmem, vmem],
        out_specs=vmem,
        scratch_shapes=[pltpu.VMEM((rows + 2 * WINDOW_HALF, 10 * LANES), F32)],
        compiler_params=small,
        name="result",
    )(lax.axis_index("lat").astype(I32)[None], left, right, partial)


def direct(cap, extra, mcap, source_fields, weight_blocks, me, keys, table, owner, pres, sent):
    count = lax.axis_size("lon")
    half = count // 2
    blocks, channels, cells = source_fields.shape
    pairs = weight_blocks.shape[0]
    parts = half - 1
    first = count * cap
    sends = first + parts * extra
    smem = pl.BlockSpec(memory_space=pltpu.SMEM)
    vmem = pl.BlockSpec(memory_space=pltpu.VMEM)
    hbm = pl.BlockSpec(memory_space=pl.ANY)
    far = lax.all_to_all(
        sent[0].reshape(count, cap, channels, cells), "lon", split_axis=0, concat_axis=0, tiled=True
    ).reshape(first, channels, cells)
    near = []
    for j in range(parts):
        turn = [(i, i // half * half + (i % half + j + 1) % half) for i in range(count)]
        near.append(lax.ppermute(sent[1 + j], "lon", turn))
    entry, spot, landing = finish_plan(
        me, keys, owner, pres, table, count, blocks, cap, extra, mcap
    )
    lat_count = lax.axis_size("lat")
    flag = landing[1:2, :LANES]
    flags = [flag]
    for j in range(1, lat_count):
        turn = [(i, (i + j) % lat_count) for i in range(lat_count)]
        flags.append(lax.ppermute(flag, "lat", turn))
    chunk_count = -(-pairs // CHUNK)
    local, moments = pl.pallas_call(
        functools.partial(local_kernel, sends),
        out_shape=(
            jax.ShapeDtypeStruct((pairs, channels, cells), F32),
            jax.ShapeDtypeStruct((5, count * mcap + 8, cells), F32),
        ),
        in_specs=[smem, smem, hbm, hbm],
        out_specs=(hbm, vmem),
        scratch_shapes=[
            pltpu.VMEM((pairs + 1, channels, cells), F32),
            pltpu.VMEM(source_fields.shape, BF16),
            pltpu.VMEM(weight_blocks.shape, BF16),
            pltpu.SemaphoreType.DMA((8,)),
            pltpu.SemaphoreType.DMA((chunk_count,)),
        ],
        compiler_params=pltpu.CompilerParams(vmem_limit_bytes=50 << 20),
        name="staying",
    )(table, landing, source_fields, weight_blocks)
    far, near, flags = lax.optimization_barrier((far, near, flags))
    finished = pl.pallas_call(
        functools.partial(merge_kernel, count, cap, extra, mcap),
        out_shape=jax.ShapeDtypeStruct((count, 5, mcap, cells), BF16),
        in_specs=[smem, smem, smem, hbm, hbm, vmem] + [hbm] * parts,
        out_specs=vmem,
        scratch_shapes=[
            pltpu.VMEM((pairs + 1, channels, cells), F32),
            pltpu.VMEM((parts * extra, channels, cells), BF16),
            pltpu.VMEM((5, count * mcap + 8, cells), F32),
            pltpu.SemaphoreType.DMA((chunk_count,)),
            pltpu.SemaphoreType.DMA((parts,)),
            pltpu.SemaphoreType.DMA,
        ],
        compiler_params=pltpu.CompilerParams(vmem_limit_bytes=50 << 20),
        name="merge",
    )(table, landing, entry, local, moments, far, *near)
    bands = pl.pallas_call(
        bands_kernel,
        out_shape=[jax.ShapeDtypeStruct((LON_DEV, LON_DEV), BF16)] * 2,
        in_specs=[hbm],
        out_specs=[vmem] * 2,
        compiler_params=pltpu.CompilerParams(vmem_limit_bytes=50 << 20),
        name="bands",
    )(finished)
    arrived = lax.all_to_all(finished, "lon", split_axis=0, concat_axis=0, tiled=True)
    wide = LON_DEV // cells
    where = spot.reshape(-1)[:blocks].reshape(LAT_DEV, wide).T.reshape(blocks, 1)
    moments, top, bottom = pl.pallas_call(
        functools.partial(spread_kernel, count, mcap),
        out_shape=[
            jax.ShapeDtypeStruct((5, each, LON_DEV), BF16)
            for each in (LAT_DEV, WINDOW_HALF, WINDOW_HALF)
        ],
        in_specs=[vmem, vmem],
        out_specs=[vmem] * 3,
        scratch_shapes=[pltpu.VMEM((count * mcap, 5 * cells), BF16)],
        compiler_params=pltpu.CompilerParams(vmem_limit_bytes=8 << 20),
        name="spread",
    )(where, arrived)
    arrived_flags = functools.reduce(jnp.maximum, flags)
    return correlate(channels // 2, moments, top, bottom, bands), arrived_flags


def padded_exchange(source_fields, weight_blocks, pair_source, targets, pair_block):
    lon_count = lax.axis_size("lon")
    pair_count = pair_source.shape[0]
    capacity = max(2, 2 * pair_count // lon_count)
    blocks_dev, channels, cell_count = source_fields.shape
    lanes = jnp.arange(lon_count, dtype=jnp.int32)
    matches = (targets[:, None] == lanes[None, :]).astype(jnp.int32)
    earlier = jnp.cumsum(matches, axis=0) - matches
    slots = jnp.sum(earlier * matches, axis=1)
    position = targets * capacity + slots
    outgoing = jnp.zeros((lon_count * capacity,), jnp.int32).at[position].set(pair_block)
    arriving = lax.all_to_all(
        outgoing.reshape(lon_count, capacity), "lon", split_axis=0, concat_axis=0, tiled=True
    )
    picked = source_fields[pair_source]
    terms = jnp.einsum("pck,pjk->pcj", picked, weight_blocks, preferred_element_type=jnp.float32)
    packed = (
        jnp.zeros((lon_count * capacity, channels, cell_count), jnp.float32).at[position].set(terms)
    )
    received = lax.all_to_all(
        packed.reshape(lon_count, capacity, channels, cell_count).astype(jnp.bfloat16),
        "lon",
        split_axis=0,
        concat_axis=0,
        tiled=True,
    ).astype(jnp.float32)
    remapped = jax.ops.segment_sum(
        received.reshape(lon_count * capacity, channels, cell_count),
        arriving.reshape(-1),
        num_segments=blocks_dev,
    )
    days = channels // 2
    temper = remapped[:, :days]
    moist = remapped[:, days:]
    moments = jnp.stack(
        [
            temper.sum(1),
            moist.sum(1),
            (temper * temper).sum(1),
            (moist * moist).sum(1),
            (temper * moist).sum(1),
        ]
    )
    return moments.reshape(5, LAT_DEV, LON_DEV).astype(BF16)


def padded_result(source_fields, weight_blocks, pair_source, targets, pair_block):
    moments = padded_exchange(source_fields, weight_blocks, pair_source, targets, pair_block)
    days = source_fields.shape[1] // 2
    lon_band = band_matrix(LON_DEV)
    lat_band = band_matrix(LAT_DEV)
    taller = padded(moments, (("lat", 1),), WINDOW_HALF, False)
    wider = padded(taller, (("lon", 2),), WINDOW_HALF, True).astype(F32)
    smoothed = smooth_lat(smooth_lon(wider, lon_band), lat_band)
    kernel = gaussian_taps()
    height = LAT_DEV * lax.axis_size("lat")
    rows = (
        lax.axis_index("lat") * LAT_DEV
        + jnp.arange(LAT_DEV, dtype=jnp.int32)[:, None]
        + jnp.arange(2 * WINDOW_HALF + 1, dtype=jnp.int32)[None, :]
        - WINDOW_HALF
    )
    inside = ((rows >= 0) & (rows < height)).astype(jnp.float32)
    lat_total = jnp.sum(inside * kernel[None, :], axis=1)
    weight_total = lat_total[:, None] * (jnp.sum(kernel) * days)
    mean_temper = smoothed[0] / weight_total
    mean_moist = smoothed[1] / weight_total
    var_temper = smoothed[2] / weight_total - mean_temper * mean_temper
    var_moist = smoothed[3] / weight_total - mean_moist * mean_moist
    covar = smoothed[4] / weight_total - mean_temper * mean_moist
    return covar / jnp.sqrt(var_temper * var_moist + 1e-06)


def local(source_fields, weight_blocks, pair_source, pair_target, pair_block):
    count = lax.axis_size("lon")
    blocks = source_fields.shape[0]
    pairs = pair_source.shape[0]
    share = -(-pairs // count)
    cap = max(share * 7 // 16, min(share, 8))
    extra = max(share * 3 // 16, 1)
    mcap = -(-share * 3 // 2 // 16) * 16
    targets = pair_target[:, 0]
    keys = pair_target.reshape(1, 1, pairs) * blocks + pair_block[None, None, :]
    all_keys = lax.all_to_all(
        jnp.broadcast_to(keys, (count, 1, pairs)), "lon", split_axis=0, concat_axis=0, tiled=True
    )
    me = lax.axis_index("lon").astype(I32)[None]
    table, owner, pres, sent = make_plan(
        me, all_keys, pair_source, source_fields, weight_blocks, cap, extra, mcap
    )
    sent, owner = lax.optimization_barrier((sent, owner))
    result, flags = direct(
        cap, extra, mcap, source_fields, weight_blocks, me, all_keys, table, owner, pres, sent
    )
    return lax.cond(
        jnp.max(flags) == 0,
        lambda kept: kept,
        lambda kept: padded_result(
            source_fields, weight_blocks, pair_source, targets, pair_block
        ),
        result,
    )


def solution(mesh):
    placed = (
        P(("lat", "lon"), None, None),
        P(("lat", "lon"), None, None),
        P(("lat", "lon")),
        P(("lat", "lon"), None),
        P(("lat", "lon")),
    )
    return jax.shard_map(
        local, mesh=mesh, in_specs=placed, out_specs=P("lat", "lon"), check_vma=False
    )
```

```python
import functools

import jax
import jax.numpy as jnp
from jax import lax
from jax.experimental import pallas as pl
from jax.experimental.pallas import tpu as pltpu
from jax.sharding import PartitionSpec as P

WINDOW_HALF = 16
LAT_DEV = 64
LON_DEV = 512
LANES = 128
GROUP = 8
CHUNK = 16
F32 = jnp.float32
BF16 = jnp.bfloat16
I32 = jnp.int32


def padded(x, sides, width, wrap):
    for axis, dim in sides:
        count, length = (lax.axis_size(axis), x.shape[dim])
        up = [(i, (i + 1) % count) for i in range(count if wrap else count - 1)]
        down = [(j, i) for i, j in up]
        last = lax.slice_in_dim(x, length - width, length, axis=dim)
        leading = lax.slice_in_dim(x, 0, width, axis=dim)
        before = lax.ppermute(last, axis, up)
        after = lax.ppermute(leading, axis, down)
        x = jnp.concatenate([before, x, after], axis=dim)
    return x


def gaussian_taps():
    offsets = jnp.arange(2 * WINDOW_HALF + 1).astype(jnp.float32) - WINDOW_HALF
    return jnp.exp(-offsets * offsets / (0.5 * WINDOW_HALF * WINDOW_HALF))


def band_matrix(length):
    outer = jnp.arange(length + 2 * WINDOW_HALF, dtype=jnp.int32)[:, None]
    inner = jnp.arange(length, dtype=jnp.int32)[None, :]
    offsets = (outer - inner - WINDOW_HALF).astype(jnp.float32)
    values = jnp.exp(-offsets * offsets / (0.5 * WINDOW_HALF * WINDOW_HALF))
    return jnp.where(jnp.abs(offsets) <= WINDOW_HALF, values, 0.0)


def smooth_lon(fields, lon_band):
    return jnp.einsum("krb,bj->krj", fields, lon_band, precision=lax.Precision.HIGHEST)


def smooth_lat(fields, lat_band):
    return jnp.einsum("ai,kaj->kij", lat_band, fields, precision=lax.Precision.HIGHEST)


def iota(shape, dim):
    return lax.broadcasted_iota(I32, shape, dim)


def dot(a, b, dims=((1,), (0,)), exact=False):
    return lax.dot_general(
        a,
        b,
        (dims, ((), ())),
        preferred_element_type=F32,
        precision=lax.Precision.HIGHEST if exact else None,
    )


def repeat(count, body, carry):
    if count <= 8:
        for step in range(count):
            carry = body(step, carry)
        return carry
    return lax.fori_loop(0, count, body, carry)


def one_hots(row, height):
    pairs = row.shape[1]
    high = (iota((height, pairs), 0) == (row >> 7)).astype(F32)
    low = (iota((LANES, pairs), 0) == (row & (LANES - 1))).astype(F32)
    return high, low


def split_dot(table, other, dims=((1,), (0,))):
    upper = jnp.floor(table * (1.0 / 256.0))
    lower = table - upper * 256.0
    other = other.astype(BF16)
    return dot(upper.astype(BF16), other, dims) * 256.0 + dot(lower.astype(BF16), other, dims)


def look_up(table, high, low):
    return jnp.sum(split_dot(table, low) * high, axis=0, keepdims=True)


def prefixes(height, tile_rows):
    ahead = (iota((LANES, LANES), 0) < iota((LANES, LANES), 1)).astype(BF16)
    ones = jnp.ones((LANES, LANES), BF16)
    ahead_total = jnp.concatenate([ahead, ones], axis=1)
    up, down = iota((height, height), 1), iota((height, height), 0)
    rows_ahead = (up < down).astype(BF16)
    same_tile = ((up < down) & (up // tile_rows == down // tile_rows)).astype(BF16)

    def prefix(mask, rows):
        both = dot(mask.astype(BF16), ahead_total)
        return both[:, :LANES] + dot(rows, both[:, LANES:].astype(BF16))

    return prefix, rows_ahead, same_tile


def as_float(d):
    return float(d) if isinstance(d, int) else lax.convert_element_type(d, F32)


def load_all(sources, targets, sem):
    copies = []
    for source, target in zip(sources, targets):
        rows = source.shape[0] // 4
        for c in range(4):
            part = pl.ds(c * rows, rows)
            copies.append(pltpu.make_async_copy(source.at[part], target.at[part], sem.at[len(copies)]))
    return copies


def plan_kernel(
    count, blocks, cap, extra, mcap, parts, me_ref, keys_ref, src_ref, fields, weights, *refs
):
    table_ref, owner_ref, pres, far_ref = refs[:4]
    near_refs = refs[4 : 4 + parts]
    tall, xs, ws, total, packed, table, load_sem, table_sem, out_sem = refs[4 + parts :]
    loading = load_all((fields, weights), (xs, ws), load_sem)
    for copy in loading:
        copy.start()
    make_table(count, blocks, cap, extra, mcap, me_ref, keys_ref, src_ref, table_ref, owner_ref, pres, tall)
    to_scalar = pltpu.make_async_copy(table_ref, table, table_sem)
    to_scalar.start()
    for copy in loading:
        copy.wait()
    to_scalar.wait()
    sends = packed.shape[0] - 1
    first = count * cap
    high = (table[4, 0] + GROUP - 1) // GROUP * GROUP
    products(table, xs, ws, 0, high, total, packed, 0, sends, sends)
    outs = [pltpu.make_async_copy(packed.at[pl.ds(0, first)], far_ref, out_sem.at[0])]
    for j in range(parts):
        rows = pl.ds(first + j * extra, extra)
        outs.append(pltpu.make_async_copy(packed.at[rows], near_refs[j], out_sem.at[1 + j]))
    for out in outs:
        out.start()
    for out in outs:
        out.wait()


def make_table(
    count, blocks, cap, extra, mcap, me_ref, keys_ref, src_ref, table_ref, owner_ref, pres, tall
):
    me = me_ref[0]
    pairs = keys_ref.shape[2]
    height = count * blocks // LANES
    tile_rows = blocks // LANES
    half = count // 2
    sends = count * cap + (half - 1) * extra

    def held(d, carry):
        high, low = one_hots(keys_ref[d], height)
        found = dot(high.astype(BF16), low.astype(BF16), ((1,), (1,)))
        found = (found > 0.5).astype(F32)
        pres[d] = found
        tall[pl.ds(d, height, stride=count), :] = found
        return carry

    repeat(count, held, 0)

    zero = jnp.zeros((height, LANES), F32)
    holders = repeat(count, lambda d, total: total + pres[d], zero)
    device = iota((count, LANES), 0)
    turn = (device + count - iota((count, LANES), 1) % count) % count
    turn = turn.astype(F32)
    others = [(device != s).astype(F32) for s in range(count)]
    near = [(device // half == s // half).astype(F32) for s in range(count)]
    weight = [1.0 - 0.8 * near[s] for s in range(count)]
    part = iota((count, LANES), 1) * 2 // LANES
    sides = [(part == h).astype(F32) for h in range(2)]

    def rows_of(r):
        return pl.ds(pl.multiple_of(r * count, count), count)

    def expect(r, sums):
        here = tall[rows_of(r), :]
        even = here / jnp.maximum(jnp.sum(here, axis=0, keepdims=True), 1.0)
        return tuple(sums[s] + even * here[s : s + 1, :] for s in range(count))

    nothing = tuple(jnp.zeros((count, LANES), F32) for _ in range(count))
    sums = lax.fori_loop(0, height, expect, nothing)
    loads = tuple(
        jnp.broadcast_to(jnp.sum(sums[s], axis=1, keepdims=True), (count, LANES)) * others[s]
        for s in range(count)
    )

    def settle(r, loads):
        here = tall[rows_of(r), :]
        even = here / jnp.maximum(jnp.sum(here, axis=0, keepdims=True), 1.0)
        picks = jnp.zeros((count, LANES), F32)
        *loads, filled = loads
        begins = r % tile_rows == 0
        expected = jnp.zeros((count, LANES), F32)
        for i in range(tile_rows):
            ahead = tall[rows_of(jnp.minimum(r + i, height - 1)), :]
            expected = expected + ahead / jnp.maximum(jnp.sum(ahead, axis=0, keepdims=True), 1.0)
        filled = jnp.where(begins, jnp.sum(expected, axis=1, keepdims=True), filled)
        for side in sides:
            excess = jnp.maximum(filled - 2.0 * mcap / 3.0 + 4.0, 0.0)
            cost = 324.0 * excess * excess
            for s in range(count):
                growth = loads[s] * loads[s]
                cost = cost + weight[s] * growth * growth * here[s : s + 1, :]
            cost = jnp.where(here > 0.5, cost, 1e30)
            best = jnp.min(cost, axis=0, keepdims=True)
            place_in_turn = jnp.where(cost == best, turn, 1e30)
            nearest = jnp.min(place_in_turn, axis=0, keepdims=True)
            pick = jnp.where(place_in_turn == nearest, here, 0.0) * side
            picks = picks + pick
            change = pick - even * side
            loads = tuple(
                loads[s] + others[s] * jnp.sum(change * here[s : s + 1, :], axis=1, keepdims=True)
                for s in range(count)
            )
            filled = filled + jnp.sum(change, axis=1, keepdims=True)
        tall[rows_of(r), :] = picks
        return loads + (filled,)

    loads = lax.fori_loop(0, height, settle, loads + (jnp.zeros((count, LANES), F32),))
    far_most, near_most = loads[0] * (1.0 - near[0]), loads[0] * near[0]
    for s in range(1, count):
        far_most = jnp.maximum(far_most, loads[s] * (1.0 - near[s]))
        near_most = jnp.maximum(near_most, loads[s] * near[s])

    fits = (far_most < cap + 0.25) & (near_most < cap + extra + 0.25)
    fits = jnp.min(jnp.min(fits.astype(F32), axis=1, keepdims=True), axis=0, keepdims=True)
    over = 1 - fits.astype(I32)

    def own(d, owner):
        return jnp.where(tall[pl.ds(d, height, stride=count), :] > 0.5, d, owner)

    owner = repeat(count, own, jnp.full((height, LANES), -1, I32))
    owner_ref[...] = owner
    prefix, rows_ahead, _ = prefixes(height, tile_rows)
    mine = (owner == me).astype(F32)
    several = mine * (holders > 1.5).astype(F32)
    single = mine - several
    rank_several = prefix(several, rows_ahead)
    rank_single = prefix(single, rows_ahead)
    total_several = jnp.sum(several, axis=(0, 1), keepdims=True)
    total_mine = jnp.sum(mine, axis=(0, 1), keepdims=True)
    held_here = pres[me]

    def route(d, place):
        away = jnp.where(d == me, 0.0, 1.0)
        leaving = held_here * (owner == d).astype(F32) * away
        rank = prefix(leaving, rows_ahead)
        first = as_float(d) * cap + rank
        steps = ((d % half + half - me % half) % half).astype(F32)
        second = count * cap + (steps - 1.0) * extra + rank - cap
        return place + leaving * (jnp.where(rank < cap - 0.5, first, second) + 1.0)

    place = repeat(count, route, zero)
    place = place + several * (sends + rank_several + 1.0)
    place = place + single * (sends + total_several + rank_single + 1.0)
    high, low = one_hots(keys_ref[me], height)
    goes = look_up(place, high, low) - 1.0
    leaving = jnp.sum((goes < sends - 0.5).astype(F32), axis=1, keepdims=True)
    first_at, second_at = iota((pairs, pairs), 0), iota((pairs, pairs), 1)
    kind = iota((8, pairs), 0)
    same = (first_at == second_at).astype(F32)
    parts = jnp.where(kind == 0, jnp.floor(goes * (1.0 / 256.0)), 0.0)
    parts = jnp.where(kind == 1, goes - 256.0 * parts[0:1, :], parts)
    upright = dot(same.astype(BF16), parts.astype(BF16), ((1,), (1,)))
    upright = upright[:, 0:1] * 256.0 + upright[:, 1:2]
    earlier = (upright < goes - 0.5) | ((jnp.abs(upright - goes) < 0.5) & (first_at < second_at))
    position = jnp.sum(earlier.astype(F32), axis=0, keepdims=True)
    at = iota((1, pairs), 1).astype(F32)
    values = jnp.where(
        kind == 0,
        at,
        jnp.where(kind == 1, goes, jnp.where(kind == 2, src_ref[...].astype(F32), 0.0)),
    )
    order = (first_at == (position + 0.5).astype(I32)).astype(F32)
    result = (split_dot(values, order, ((1,), (1,))) + 0.5).astype(I32)
    lane = iota((8, pairs), 1)
    facts = jnp.where(lane == 0, leaving.astype(I32), over)
    facts = jnp.where(lane == 1, total_mine.astype(I32), facts)
    facts = jnp.where(lane == 2, total_several.astype(I32), facts)
    facts = jnp.where(lane == 4, me, facts)
    result = jnp.where(kind == 4, facts, result)
    table_ref[...] = jnp.where(kind == 5, (goes + 0.5).astype(I32), result)


def finish_kernel(
    count,
    blocks,
    sends,
    mcap,
    rim,
    me_ref,
    keys_ref,
    owner_ref,
    pres,
    table_ref,
    entry_ref,
    spot_ref,
    landing_ref,
):
    me = me_ref[0]
    pairs = keys_ref.shape[2]
    height = count * blocks // LANES
    tile_rows = blocks // LANES
    prefix, rows_ahead, same_tile = prefixes(height, tile_rows)
    owner = owner_ref[...]
    zero = jnp.zeros((height, LANES), F32)
    holders = repeat(count, lambda d, total: total + pres[d], zero)
    mine = (owner == me).astype(F32)
    rank_several = prefix(mine * (holders > 1.5).astype(F32), rows_ahead)
    entry_rows = entry_ref.shape[0] - 8
    lane_at = iota((entry_rows, LANES), 1)
    first_lane = iota((8, LANES), 1)
    wide = LON_DEV // LANES
    column_at = iota((height, LANES), 1) % wide
    rims = [(column_at == c).astype(F32) for c in (wide - 1, 0)]
    main = mcap - 2 * rim

    def route(d, carry):
        finished, codes, most, entries, counts = carry
        away = jnp.where(d == me, 0.0, 1.0)
        theirs = (owner == d).astype(F32)
        rank_theirs = prefix(theirs, same_tile)
        finished = finished + theirs * (as_float(d) * mcap + rank_theirs + 1.0)
        most = jnp.maximum(most, theirs * (rank_theirs + 1.0) - main)
        places = []
        for i in range(2):
            edge = theirs * rims[i]
            rank_edge = prefix(edge, same_tile)
            place = (as_float(d) * mcap + main + i * rim) * 8.0 + rank_edge + 1.0
            places.append(codes[i] + edge * place)
            most = jnp.maximum(most, edge * (rank_edge + 1.0) - 8.0 * rim)
        codes = tuple(places)
        coming = pres[d] * mine * away
        rank_coming = prefix(coming, rows_ahead)
        code = coming * (rank_coming * 1024.0 + rank_several + 1.0)
        high, low = one_hots(keys_ref[d], height)
        seen = jnp.sum(dot(code, low, exact=True) * high, axis=0, keepdims=True)
        seen = (seen + 0.5).astype(I32) - 1
        rank, local = seen >> 10, seen & 1023
        hit = iota((entry_rows, pairs), 0) == rank
        column = jnp.max(jnp.where(hit, local, -1), axis=1, keepdims=True)
        entries = jnp.where(lane_at == d, column, entries)
        arrivals = jnp.sum(coming, axis=(0, 1), keepdims=True).astype(I32)
        counts = jnp.where(first_lane == d, arrivals, counts)
        return finished, codes, most, entries, counts

    finished, codes, most, entries, counts = repeat(
        count,
        route,
        (zero, (zero, zero), zero, jnp.full((entry_rows, LANES), -1, I32), jnp.zeros((8, LANES), I32)),
    )
    entry_ref[:entry_rows, :] = entries
    entry_ref[entry_rows:, :] = counts
    for i, (tile, codes_of) in enumerate(
        ((me, finished), ((me + count - 1) % count, codes[0]), ((me + 1) % count, codes[1]))
    ):
        pick = (iota((8, height), 1) == tile * tile_rows + iota((8, height), 0)).astype(F32)
        spot_ref[i * 8 : i * 8 + 8, :] = (dot(pick, codes_of, exact=True) + 0.5).astype(I32) - 1
    tile_of = iota((height, LANES), 0) // tile_rows
    base = me.astype(F32) * mcap
    moment_place = mine * (tile_of.astype(F32) * mcap + finished - 1.0 - base)
    after = ((tile_of + 1) % count).astype(F32) * mcap - base
    ahead = ((tile_of + count - 1) % count).astype(F32) * mcap - base
    edge_place = rims[0] * 2.0 * (codes[0] - 1.0 + after * 8.0)
    edge_place = edge_place + rims[1] * (2.0 * (codes[1] - 1.0 + ahead * 8.0) + 1.0)
    edge_place = mine * (rims[0] + rims[1]) * (edge_place + 1.0)
    high, low = one_hots(keys_ref[me], height)
    lands = look_up(moment_place, high, low)
    edges = look_up(edge_place, high, low)
    goes = table_ref[5:6, :]
    slot = jnp.where(goes < sends, -1, goes - sends)
    in_slot = (iota((pairs, pairs), 0) == slot).astype(F32)
    kind = iota((8, pairs), 0)
    weighed = jnp.where(kind == 0, lands, jnp.where(kind == 2, edges, 1.0))
    summed = split_dot(weighed, in_slot, ((1,), (1,)))
    landing = summed / jnp.maximum(summed[1:2, :], 1.0)
    crowded = jnp.max(jnp.max(most, axis=1, keepdims=True), axis=0, keepdims=True) > 0.5
    over = jnp.maximum(table_ref[4:5, 3:4], crowded.astype(I32))
    found = (landing + 0.25).astype(I32) - jnp.where(kind == 2, 1, 0)
    landing_ref[...] = jnp.where(kind == 1, over, found)


def make_plan(me, keys, pair_source, fields, weights, cap, extra, mcap):
    count, _, pairs = keys.shape
    blocks, channels, cells = fields.shape
    height = count * blocks // LANES
    parts = count // 2 - 1
    first = count * cap
    sends = first + parts * extra
    vmem = pl.BlockSpec(memory_space=pltpu.VMEM)
    hbm = pl.BlockSpec(memory_space=pl.ANY)
    table, owner, pres, *sent = pl.pallas_call(
        functools.partial(plan_kernel, count, blocks, cap, extra, mcap, parts),
        out_shape=[
            jax.ShapeDtypeStruct((8, pairs), I32),
            jax.ShapeDtypeStruct((height, LANES), I32),
            jax.ShapeDtypeStruct((count, height, LANES), F32),
            jax.ShapeDtypeStruct((first, channels, cells), BF16),
        ]
        + [jax.ShapeDtypeStruct((extra, channels, cells), BF16)] * parts,
        in_specs=[pl.BlockSpec(memory_space=pltpu.SMEM), vmem, vmem, hbm, hbm],
        out_specs=[vmem] * 3 + [hbm] * (1 + parts),
        scratch_shapes=[
            pltpu.VMEM((height * count, LANES), F32),
            pltpu.VMEM(fields.shape, BF16),
            pltpu.VMEM(weights.shape, BF16),
            pltpu.VMEM((sends + 1, channels, cells), F32),
            pltpu.VMEM((sends + 1, channels, cells), BF16),
            pltpu.SMEM((8, pairs), I32),
            pltpu.SemaphoreType.DMA((8,)),
            pltpu.SemaphoreType.DMA,
            pltpu.SemaphoreType.DMA((1 + parts,)),
        ],
        compiler_params=pltpu.CompilerParams(vmem_limit_bytes=53 << 20),
        name="leaving",
    )(me, keys, pair_source[None, :], fields, weights)
    return table, owner, pres, sent


def finish_plan(me, keys, owner, pres, table, count, blocks, cap, extra, mcap, rim):
    pairs = keys.shape[2]
    entry_rows = -(-(cap + extra) // 8) * 8 + 8
    sends = count * cap + (count // 2 - 1) * extra
    vmem = pl.BlockSpec(memory_space=pltpu.VMEM)
    return pl.pallas_call(
        functools.partial(finish_kernel, count, blocks, sends, mcap, rim),
        out_shape=(
            jax.ShapeDtypeStruct((entry_rows, LANES), I32),
            jax.ShapeDtypeStruct((24, LANES), I32),
            jax.ShapeDtypeStruct((8, pairs), I32),
        ),
        in_specs=[pl.BlockSpec(memory_space=pltpu.SMEM)] + [vmem] * 4,
        out_specs=(vmem, vmem, vmem),
        compiler_params=pltpu.CompilerParams(vmem_limit_bytes=8 << 20),
        name="finish",
    )(me, keys, owner, pres, table)


def products(table, xs, ws, low, high, target, packed, first, last, dummy):
    def step(g, carry):
        base = g * GROUP
        results = []
        for u in range(GROUP):
            x, w = xs[table[2, base + u]], ws[table[0, base + u]]
            results.append(dot(x, w, ((1,), (1,))))
        for u in range(GROUP):
            i = base + u
            place = table[1, i]
            again = (i > low) & (table[1, jnp.maximum(i - 1, 0)] == place)
            inside = (place >= first) & (place < last)
            where = jnp.where(inside, place - first, dummy)
            value = results[u] + jnp.where(again, target[where], 0.0)
            target[where] = value
            if packed is not None:
                packed[where] = value.astype(BF16)
        return carry

    lax.fori_loop(low // GROUP, high // GROUP, step, 0)


def moment_rows(value):
    days = value.shape[0] // 2
    temper, moist = value[:days], value[days:]
    return [
        jnp.sum(each, axis=0, keepdims=True)
        for each in (temper, moist, temper * temper, moist * moist, temper * moist)
    ]


def put_moments(landing, total, moments, begin, end):
    spare = moments.shape[0] // 8 - 1
    row_at, group_at = iota((8, LANES), 0), iota((8, LANES), 1) // WINDOW_HALF

    def tile(place):
        return pl.ds(pl.multiple_of(place * 8, 8), 8)

    def some(g, carry):
        for u in range(4):
            i = begin + g * 4 + u
            good = i < end
            at = jnp.where(good, i, 0)
            place = jnp.where(good, jnp.clip(landing[0, at], 0, spare), spare)
            value = jnp.zeros((8, LANES), F32)
            for k, row in enumerate(moment_rows(total[at])):
                value = jnp.where(row_at == k, row, value)
            moments[tile(place), :] = value
            code = landing[2, at]
            edge = jnp.where(good & (code >= 0), jnp.minimum(code >> 4, spare), spare)
            group = (code >> 1) & 7
            shift = (group * WINDOW_HALF + (code & 1) * (LANES - WINDOW_HALF) + WINDOW_HALF) % LANES
            moved = pltpu.roll(value, shift, 1)
            moments[tile(edge), :] = jnp.where(group_at == group, moved, moments[tile(edge), :])
        return carry

    lax.fori_loop(0, (end - begin + 3) // 4, some, 0)


def chunk_copies(source, target, sem, c):
    rows = pl.ds(c * CHUNK, CHUNK)
    return pltpu.make_async_copy(source.at[rows], target.at[rows], sem.at[c])


def local_kernel(
    sends, table, landing, fields, weights, local_ref, moments, total, xs, ws, load_sem, out_sem
):
    pairs = weights.shape[0]
    leaving, owned, several = table[4, 0], table[4, 1], table[4, 2]
    low = leaving // GROUP * GROUP
    loading = load_all((fields, weights), (xs, ws), load_sem)
    for copy in loading:
        copy.start()
    moments[...] = jnp.zeros(moments.shape, F32)
    for copy in loading:
        copy.wait()
    products(table, xs, ws, low, pairs, total, None, sends, sends + pairs, pairs)
    chunks = (several + CHUNK - 1) // CHUNK

    def begin(c, carry):
        chunk_copies(total, local_ref, out_sem, c).start()
        return carry

    lax.fori_loop(0, chunks, begin, 0)
    put_moments(landing, total, moments, several, owned)

    def end(c, carry):
        chunk_copies(total, local_ref, out_sem, c).wait()
        return carry

    lax.fori_loop(0, chunks, end, 0)


def merge_kernel(count, cap, extra, mcap, table, landing, entry, local_ref, moments_in, far_ref, *refs):
    parts = count // 2 - 1
    near_refs = refs[:parts]
    out_ref, total, near, moments, in_sem, near_sem, moment_sem = refs[parts:]
    several, me = table[4, 2], table[4, 4]
    half = count // 2
    spare = total.shape[0] - 1
    counts_row = entry.shape[0] - 8
    chunks = (several + CHUNK - 1) // CHUNK

    def begin(c, carry):
        chunk_copies(local_ref, total, in_sem, c).start()
        return carry

    near_copies = [
        pltpu.make_async_copy(near_refs[j], near.at[pl.ds(j * extra, extra)], near_sem.at[j])
        for j in range(parts)
    ]
    lax.fori_loop(0, chunks, begin, 0)
    for near_copy in near_copies:
        near_copy.start()
    moment_copy = pltpu.make_async_copy(moments_in, moments, moment_sem)
    moment_copy.start()

    def end(c, carry):
        chunk_copies(local_ref, total, in_sem, c).wait()
        return carry

    lax.fori_loop(0, chunks, end, 0)

    def add(s, low, high, came, shift):
        def some(g, inner):
            for u in range(4):
                r = low + g * 4 + u
                good = r < high
                at = jnp.where(good, r, low)
                where = jnp.where(good, jnp.maximum(entry[at, s], 0), spare)
                total[where] = total[where] + came[shift + at].astype(F32)
            return inner

        lax.fori_loop(0, (high - low + 3) // 4, some, 0)

    def from_far(s, carry):
        add(s, 0, jnp.minimum(entry[counts_row, s], cap), far_ref, s * cap)
        return carry

    lax.fori_loop(0, count, from_far, 0)
    for near_copy in near_copies:
        near_copy.wait()

    def from_near(j, carry):
        s = me // half * half + (me % half + half - j - 1) % half
        number = jnp.clip(entry[counts_row, s], cap, cap + extra)
        add(s, cap, number, near, j * extra - cap)
        return carry

    lax.fori_loop(0, parts, from_near, 0)
    moment_copy.wait()
    put_moments(landing, total, moments, 0, several)
    for o in range(count):
        for k in range(5):
            out_ref[o, k] = moments[pl.ds(o * mcap * 8 + k, mcap, stride=8), :].astype(BF16)


def spread_kernel(count, mcap, spot_ref, rim_ref, came, map_ref, top_ref, bottom_ref, flat):
    rows, blocks_wide = map_ref.shape[1], map_ref.shape[2] // LANES - 1
    for a in range(count):
        for k in range(5):
            flat[a * mcap : (a + 1) * mcap, k * LANES : (k + 1) * LANES] = came[a, k]
    slots = count * mcap

    def gather(row):
        chosen = (iota((row.shape[0], slots), 1) == row).astype(F32)
        return dot(chosen.astype(BF16), flat[...])

    laid = gather(spot_ref[...]).astype(BF16)
    code = rim_ref[...]
    rims = gather(code >> 3)
    kept = iota((2 * rows, LANES), 1) // WINDOW_HALF == (code & 7)
    source, target = iota((LANES, LANES), 0) % WINDOW_HALF, iota((LANES, LANES), 1)
    folds = [(source == target - i * WINDOW_HALF).astype(F32).astype(BF16) for i in range(2)]

    def put(k, lanes, tile):
        map_ref[k, :, lanes] = tile
        top_ref[k, :, lanes] = tile[:WINDOW_HALF]
        bottom_ref[k, :, lanes] = tile[rows - WINDOW_HALF :]

    for k in range(5):
        of_k = slice(k * LANES, (k + 1) * LANES)
        for q in range(blocks_wide):
            put(k, slice(q * LANES, (q + 1) * LANES), laid[q * rows : (q + 1) * rows, of_k])
        piece = jnp.where(kept, rims[:, of_k], 0.0).astype(BF16)
        side = dot(piece[:rows], folds[0]) + dot(piece[rows:], folds[1])
        put(k, slice(blocks_wide * LANES, (blocks_wide + 1) * LANES), side.astype(BF16))


def tap(offset):
    offset = offset.astype(F32)
    value = jnp.exp(-offset * offset / (0.5 * WINDOW_HALF * WINDOW_HALF))
    return jnp.where(jnp.abs(offset) <= WINDOW_HALF, value, 0.0)


def halved(value):
    upper = value.astype(BF16)
    return upper, (value - upper.astype(F32)).astype(BF16)


def bands_kernel(after_ref, upper_ref, lower_ref):
    shape = upper_ref.shape
    width = shape[1]
    at, inner = iota(shape, 0), iota(shape, 1)
    beyond = at - width
    beside = jnp.where(beyond < WINDOW_HALF, beyond - WINDOW_HALF, at - WINDOW_HALF)
    outer = jnp.where(beyond < 0, at, beside)
    used = beyond < 2 * WINDOW_HALF
    upper_ref[...], lower_ref[...] = halved(jnp.where(used, tap(outer - inner), 0.0))


def across(fields, upper, lower):
    return dot(fields, upper) + dot(fields, lower)


def center_kernel(map_ref, upper, lower, out_ref):
    fields = jnp.concatenate([map_ref[k] for k in range(5)], axis=0)
    rows = map_ref.shape[1]
    smooth = across(fields, upper[...], lower[...])
    shape = (rows, rows)
    weights = tap(iota(shape, 1) - iota(shape, 0))
    for k in range(5):
        out_ref[k] = dot(weights, smooth[k * rows : (k + 1) * rows], exact=True)


def result_kernel(height, days, lat_ref, before, after, upper, lower, partial, out_ref):
    rows, width = out_ref.shape
    half = WINDOW_HALF
    fields = jnp.concatenate([ref[k] for k in range(5) for ref in (before, after)], axis=0)
    smooth = across(fields, upper[...], lower[...])
    at = iota((rows, 2 * half), 1)
    weights = tap(jnp.where(at < half, at - half, rows + at - half) - iota((rows, 2 * half), 0))
    k_at = iota((rows, LANES), 1) - half
    row = lat_ref[0] * rows + iota((rows, LANES), 0) + k_at
    taps = tap(k_at)
    inside = jnp.where((row >= 0) & (row < height), taps, 0.0)
    weight = jnp.sum(inside, axis=1, keepdims=True) * (jnp.sum(taps, axis=1, keepdims=True) * days)
    scale = 1.0 / weight
    values = []
    for k in range(5):
        beside = dot(weights, smooth[2 * k * half : 2 * (k + 1) * half], exact=True)
        values.append((partial[k] + beside) * scale)
    mean_t, mean_m, square_t, square_m, cross = values
    var_t = square_t - mean_t * mean_t
    var_m = square_m - mean_m * mean_m
    covar = cross - mean_t * mean_m
    out_ref[...] = covar / jnp.sqrt(var_t * var_m + 1e-06)


def neighbours(low, high, axis, wrap):
    count = lax.axis_size(axis)
    up = [(i, (i + 1) % count) for i in range(count if wrap else count - 1)]
    down = [(j, i) for i, j in up]
    return lax.ppermute(high, axis, up), lax.ppermute(low, axis, down)


def correlate(days, moments, top, bottom, bands):
    vmem = pl.BlockSpec(memory_space=pltpu.VMEM)
    smem = pl.BlockSpec(memory_space=pltpu.SMEM)
    small = pltpu.CompilerParams(vmem_limit_bytes=16 << 20)
    rows, width = moments.shape[1], bands[0].shape[1]
    before, after = neighbours(top, bottom, "lat", False)
    partial = pl.pallas_call(
        center_kernel,
        out_shape=jax.ShapeDtypeStruct((5, rows, width), F32),
        in_specs=[vmem] * 3,
        out_specs=vmem,
        compiler_params=small,
        name="center",
    )(moments, *bands)
    before, after, partial = lax.optimization_barrier((before, after, partial))
    height = rows * lax.axis_size("lat")
    return pl.pallas_call(
        functools.partial(result_kernel, height, days),
        out_shape=jax.ShapeDtypeStruct((rows, width), F32),
        in_specs=[smem] + [vmem] * 5,
        out_specs=vmem,
        compiler_params=small,
        name="result",
    )(lax.axis_index("lat").astype(I32)[None], before, after, *bands, partial)


def direct(cap, extra, mcap, rim, source_fields, weight_blocks, me, keys, table, owner, pres, sent):
    count = lax.axis_size("lon")
    half = count // 2
    blocks, channels, cells = source_fields.shape
    pairs = weight_blocks.shape[0]
    parts = half - 1
    first = count * cap
    sends = first + parts * extra
    smem = pl.BlockSpec(memory_space=pltpu.SMEM)
    vmem = pl.BlockSpec(memory_space=pltpu.VMEM)
    hbm = pl.BlockSpec(memory_space=pl.ANY)
    far = lax.all_to_all(
        sent[0].reshape(count, cap, channels, cells), "lon", split_axis=0, concat_axis=0, tiled=True
    ).reshape(first, channels, cells)
    near = []
    for j in range(parts):
        turn = [(i, i // half * half + (i % half + j + 1) % half) for i in range(count)]
        near.append(lax.ppermute(sent[1 + j], "lon", turn))
    entry, spot, landing = finish_plan(
        me, keys, owner, pres, table, count, blocks, cap, extra, mcap, rim
    )
    lat_count = lax.axis_size("lat")
    flag = landing[1:2, :LANES]
    flags = [flag]
    for j in range(1, lat_count):
        turn = [(i, (i + j) % lat_count) for i in range(lat_count)]
        flags.append(lax.ppermute(flag, "lat", turn))
    chunk_count = -(-pairs // CHUNK)
    local, moments = pl.pallas_call(
        functools.partial(local_kernel, sends),
        out_shape=(
            jax.ShapeDtypeStruct((pairs, channels, cells), F32),
            jax.ShapeDtypeStruct(((count * mcap + 1) * 8, cells), F32),
        ),
        in_specs=[smem, smem, hbm, hbm],
        out_specs=(hbm, vmem),
        scratch_shapes=[
            pltpu.VMEM((pairs + 1, channels, cells), F32),
            pltpu.VMEM(source_fields.shape, BF16),
            pltpu.VMEM(weight_blocks.shape, BF16),
            pltpu.SemaphoreType.DMA((8,)),
            pltpu.SemaphoreType.DMA((chunk_count,)),
        ],
        compiler_params=pltpu.CompilerParams(vmem_limit_bytes=50 << 20),
        name="staying",
    )(table, landing, source_fields, weight_blocks)
    far, near, flags = lax.optimization_barrier((far, near, flags))
    finished = pl.pallas_call(
        functools.partial(merge_kernel, count, cap, extra, mcap),
        out_shape=jax.ShapeDtypeStruct((count, 5, mcap, cells), BF16),
        in_specs=[smem, smem, smem, hbm, hbm, vmem] + [hbm] * parts,
        out_specs=vmem,
        scratch_shapes=[
            pltpu.VMEM((pairs + 1, channels, cells), F32),
            pltpu.VMEM((parts * extra, channels, cells), BF16),
            pltpu.VMEM(((count * mcap + 1) * 8, cells), F32),
            pltpu.SemaphoreType.DMA((chunk_count,)),
            pltpu.SemaphoreType.DMA((parts,)),
            pltpu.SemaphoreType.DMA,
        ],
        compiler_params=pltpu.CompilerParams(vmem_limit_bytes=50 << 20),
        name="merge",
    )(table, landing, entry, local, moments, far, *near)
    bands = pl.pallas_call(
        bands_kernel,
        out_shape=[jax.ShapeDtypeStruct((LON_DEV + LANES, LON_DEV), BF16)] * 2,
        in_specs=[hbm],
        out_specs=[vmem] * 2,
        compiler_params=pltpu.CompilerParams(vmem_limit_bytes=50 << 20),
        name="bands",
    )(finished)
    arrived = lax.all_to_all(finished, "lon", split_axis=0, concat_axis=0, tiled=True)
    wide = LON_DEV // cells
    tables = spot.reshape(3, 8 * LANES)[:, :blocks].reshape(3, LAT_DEV, wide)
    where = tables[0].T.reshape(blocks, 1)
    rims = jnp.concatenate([tables[1, :, wide - 1], tables[2, :, 0]])[:, None]
    moments, top, bottom = pl.pallas_call(
        functools.partial(spread_kernel, count, mcap),
        out_shape=[
            jax.ShapeDtypeStruct((5, each, LON_DEV + LANES), BF16)
            for each in (LAT_DEV, WINDOW_HALF, WINDOW_HALF)
        ],
        in_specs=[vmem] * 3,
        out_specs=[vmem] * 3,
        scratch_shapes=[pltpu.VMEM((count * mcap, 5 * cells), BF16)],
        compiler_params=pltpu.CompilerParams(vmem_limit_bytes=8 << 20),
        name="spread",
    )(where, rims, arrived)
    arrived_flags = functools.reduce(jnp.maximum, flags)
    return correlate(channels // 2, moments, top, bottom, bands), arrived_flags


def padded_exchange(source_fields, weight_blocks, pair_source, targets, pair_block):
    lon_count = lax.axis_size("lon")
    pair_count = pair_source.shape[0]
    capacity = max(2, 2 * pair_count // lon_count)
    blocks_dev, channels, cell_count = source_fields.shape
    lanes = jnp.arange(lon_count, dtype=jnp.int32)
    matches = (targets[:, None] == lanes[None, :]).astype(jnp.int32)
    earlier = jnp.cumsum(matches, axis=0) - matches
    slots = jnp.sum(earlier * matches, axis=1)
    position = targets * capacity + slots
    outgoing = jnp.zeros((lon_count * capacity,), jnp.int32).at[position].set(pair_block)
    arriving = lax.all_to_all(
        outgoing.reshape(lon_count, capacity), "lon", split_axis=0, concat_axis=0, tiled=True
    )
    picked = source_fields[pair_source]
    terms = jnp.einsum("pck,pjk->pcj", picked, weight_blocks, preferred_element_type=jnp.float32)
    packed = (
        jnp.zeros((lon_count * capacity, channels, cell_count), jnp.float32).at[position].set(terms)
    )
    received = lax.all_to_all(
        packed.reshape(lon_count, capacity, channels, cell_count).astype(jnp.bfloat16),
        "lon",
        split_axis=0,
        concat_axis=0,
        tiled=True,
    ).astype(jnp.float32)
    remapped = jax.ops.segment_sum(
        received.reshape(lon_count * capacity, channels, cell_count),
        arriving.reshape(-1),
        num_segments=blocks_dev,
    )
    days = channels // 2
    temper = remapped[:, :days]
    moist = remapped[:, days:]
    moments = jnp.stack(
        [
            temper.sum(1),
            moist.sum(1),
            (temper * temper).sum(1),
            (moist * moist).sum(1),
            (temper * moist).sum(1),
        ]
    )
    return moments.reshape(5, LAT_DEV, LON_DEV).astype(BF16)


def padded_result(source_fields, weight_blocks, pair_source, targets, pair_block):
    moments = padded_exchange(source_fields, weight_blocks, pair_source, targets, pair_block)
    days = source_fields.shape[1] // 2
    lon_band = band_matrix(LON_DEV)
    lat_band = band_matrix(LAT_DEV)
    taller = padded(moments, (("lat", 1),), WINDOW_HALF, False)
    wider = padded(taller, (("lon", 2),), WINDOW_HALF, True).astype(F32)
    smoothed = smooth_lat(smooth_lon(wider, lon_band), lat_band)
    kernel = gaussian_taps()
    height = LAT_DEV * lax.axis_size("lat")
    rows = (
        lax.axis_index("lat") * LAT_DEV
        + jnp.arange(LAT_DEV, dtype=jnp.int32)[:, None]
        + jnp.arange(2 * WINDOW_HALF + 1, dtype=jnp.int32)[None, :]
        - WINDOW_HALF
    )
    inside = ((rows >= 0) & (rows < height)).astype(jnp.float32)
    lat_total = jnp.sum(inside * kernel[None, :], axis=1)
    weight_total = lat_total[:, None] * (jnp.sum(kernel) * days)
    mean_temper = smoothed[0] / weight_total
    mean_moist = smoothed[1] / weight_total
    var_temper = smoothed[2] / weight_total - mean_temper * mean_temper
    var_moist = smoothed[3] / weight_total - mean_moist * mean_moist
    covar = smoothed[4] / weight_total - mean_temper * mean_moist
    return covar / jnp.sqrt(var_temper * var_moist + 1e-06)


def local(source_fields, weight_blocks, pair_source, pair_target, pair_block):
    count = lax.axis_size("lon")
    blocks = source_fields.shape[0]
    pairs = pair_source.shape[0]
    share = -(-pairs // count)
    cap = max(share * 7 // 16, min(share, 8))
    extra = max(share * 3 // 16, 1)
    mcap = -(-share * 3 // 2 // 16) * 16
    rim = max(mcap // 16, 1)
    targets = pair_target[:, 0]
    keys = pair_target.reshape(1, 1, pairs) * blocks + pair_block[None, None, :]
    all_keys = lax.all_to_all(
        jnp.broadcast_to(keys, (count, 1, pairs)), "lon", split_axis=0, concat_axis=0, tiled=True
    )
    me = lax.axis_index("lon").astype(I32)[None]
    table, owner, pres, sent = make_plan(
        me, all_keys, pair_source, source_fields, weight_blocks, cap, extra, mcap
    )
    sent, owner = lax.optimization_barrier((sent, owner))
    result, flags = direct(
        cap, extra, mcap, rim, source_fields, weight_blocks, me, all_keys, table, owner, pres, sent
    )
    return lax.cond(
        jnp.max(flags) == 0,
        lambda kept: kept,
        lambda kept: padded_result(
            source_fields, weight_blocks, pair_source, targets, pair_block
        ),
        result,
    )


def solution(mesh):
    placed = (
        P(("lat", "lon"), None, None),
        P(("lat", "lon"), None, None),
        P(("lat", "lon")),
        P(("lat", "lon"), None),
        P(("lat", "lon")),
    )
    return jax.shard_map(
        local, mesh=mesh, in_specs=placed, out_specs=P("lat", "lon"), check_vma=False
    )
```

```python
import functools

import jax
import jax.numpy as jnp
from jax import lax
from jax.experimental import pallas as pl
from jax.experimental.pallas import tpu as pltpu
from jax.sharding import PartitionSpec as P

WINDOW_HALF = 16
LAT_DEV = 64
LON_DEV = 512
LANES = 128
GROUP = 16
CHUNK = 16
F32 = jnp.float32
BF16 = jnp.bfloat16
I32 = jnp.int32


def padded(x, sides, width, wrap):
    for axis, dim in sides:
        count, length = (lax.axis_size(axis), x.shape[dim])
        up = [(i, (i + 1) % count) for i in range(count if wrap else count - 1)]
        down = [(j, i) for i, j in up]
        last = lax.slice_in_dim(x, length - width, length, axis=dim)
        leading = lax.slice_in_dim(x, 0, width, axis=dim)
        before = lax.ppermute(last, axis, up)
        after = lax.ppermute(leading, axis, down)
        x = jnp.concatenate([before, x, after], axis=dim)
    return x


def gaussian_taps():
    offsets = jnp.arange(2 * WINDOW_HALF + 1).astype(jnp.float32) - WINDOW_HALF
    return jnp.exp(-offsets * offsets / (0.5 * WINDOW_HALF * WINDOW_HALF))


def band_matrix(length):
    outer = jnp.arange(length + 2 * WINDOW_HALF, dtype=jnp.int32)[:, None]
    inner = jnp.arange(length, dtype=jnp.int32)[None, :]
    offsets = (outer - inner - WINDOW_HALF).astype(jnp.float32)
    values = jnp.exp(-offsets * offsets / (0.5 * WINDOW_HALF * WINDOW_HALF))
    return jnp.where(jnp.abs(offsets) <= WINDOW_HALF, values, 0.0)


def smooth_lon(fields, lon_band):
    return jnp.einsum("krb,bj->krj", fields, lon_band, precision=lax.Precision.HIGHEST)


def smooth_lat(fields, lat_band):
    return jnp.einsum("ai,kaj->kij", lat_band, fields, precision=lax.Precision.HIGHEST)


def iota(shape, dim):
    return lax.broadcasted_iota(I32, shape, dim)


def dot(a, b, dims=((1,), (0,)), exact=False):
    return lax.dot_general(
        a,
        b,
        (dims, ((), ())),
        preferred_element_type=F32,
        precision=lax.Precision.HIGHEST if exact else None,
    )


def repeat(count, body, carry):
    if count <= 8:
        for step in range(count):
            carry = body(step, carry)
        return carry
    return lax.fori_loop(0, count, body, carry)


def one_hots(row, height):
    pairs = row.shape[1]
    high = (iota((height, pairs), 0) == (row >> 7)).astype(F32)
    low = (iota((LANES, pairs), 0) == (row & (LANES - 1))).astype(F32)
    return high, low


def split_dot(table, other, dims=((1,), (0,))):
    upper = jnp.floor(table * (1.0 / 256.0))
    lower = table - upper * 256.0
    other = other.astype(BF16)
    return dot(upper.astype(BF16), other, dims) * 256.0 + dot(lower.astype(BF16), other, dims)


def look_up(table, high, low):
    return jnp.sum(split_dot(table, low) * high, axis=0, keepdims=True)


def prefixes(height, tile_rows):
    ahead = (iota((LANES, LANES), 0) < iota((LANES, LANES), 1)).astype(BF16)
    ones = jnp.ones((LANES, LANES), BF16)
    ahead_total = jnp.concatenate([ahead, ones], axis=1)
    up, down = iota((height, height), 1), iota((height, height), 0)
    rows_ahead = (up < down).astype(BF16)
    same_tile = ((up < down) & (up // tile_rows == down // tile_rows)).astype(BF16)

    def prefix(mask, rows):
        both = dot(mask.astype(BF16), ahead_total)
        return both[:, :LANES] + dot(rows, both[:, LANES:].astype(BF16))

    return prefix, rows_ahead, same_tile


def prefix_each(masks, height):
    group = max(1, LANES // height)
    ahead = (iota((LANES, LANES), 0) < iota((LANES, LANES), 1)).astype(BF16)
    ahead_total = jnp.concatenate([ahead, jnp.ones((LANES, LANES), BF16)], axis=1)
    ranks = []
    for begin in range(0, len(masks), group):
        part = masks[begin : begin + group]
        rows = height * len(part)
        up, down = iota((rows, rows), 1), iota((rows, rows), 0)
        rows_ahead = ((up < down) & (up // height == down // height)).astype(BF16)
        both = dot(jnp.concatenate(part, axis=0).astype(BF16), ahead_total)
        rank = both[:, :LANES] + dot(rows_ahead, both[:, LANES:].astype(BF16))
        ranks += [rank[i * height : (i + 1) * height] for i in range(len(part))]
    return ranks


def as_float(d):
    return float(d) if isinstance(d, int) else lax.convert_element_type(d, F32)


def load_all(sources, targets, sem):
    copies = []
    for source, target in zip(sources, targets):
        rows = source.shape[0] // 4
        for c in range(4):
            part = pl.ds(c * rows, rows)
            copies.append(pltpu.make_async_copy(source.at[part], target.at[part], sem.at[len(copies)]))
    return copies


def plan_kernel(
    count, blocks, cap, extra, mcap, parts, me_ref, keys_ref, src_ref, fields, weights, *refs
):
    table_ref, owner_ref, pres, far_ref = refs[:4]
    near_refs = refs[4 : 4 + parts]
    tall, xs, ws, total, packed, table, load_sem, table_sem, out_sem = refs[4 + parts :]
    loading = load_all((fields, weights), (xs, ws), load_sem)
    for copy in loading:
        copy.start()
    make_table(count, blocks, cap, extra, mcap, me_ref, keys_ref, src_ref, table_ref, owner_ref, pres, tall)
    to_scalar = pltpu.make_async_copy(table_ref, table, table_sem)
    to_scalar.start()
    for copy in loading:
        copy.wait()
    to_scalar.wait()
    sends = packed.shape[0] - 1
    first = count * cap
    high = (table[4, 0] + GROUP - 1) // GROUP * GROUP

    def far_copy(d):
        rows = pl.ds(d * cap, cap)
        return pltpu.make_async_copy(packed.at[rows], far_ref.at[rows], out_sem.at[d])

    def start_far(begin, end):
        def one(d, carry):
            far_copy(d).start()
            return carry

        lax.fori_loop(begin, end, one, 0)

    def after(started, place):
        done = jnp.maximum(started, jnp.minimum(place // cap, count))
        start_far(started, done)
        return done

    started = products(table, xs, ws, 0, high, total, packed, 0, sends, sends, after)
    start_far(started, count)
    outs = []
    for j in range(parts):
        rows = pl.ds(first + j * extra, extra)
        outs.append(pltpu.make_async_copy(packed.at[rows], near_refs[j], out_sem.at[count + j]))
    for out in outs:
        out.start()
    for d in range(count):
        far_copy(d).wait()
    for out in outs:
        out.wait()


def make_table(
    count, blocks, cap, extra, mcap, me_ref, keys_ref, src_ref, table_ref, owner_ref, pres, tall
):
    me = me_ref[0]
    pairs = keys_ref.shape[2]
    height = count * blocks // LANES
    tile_rows = blocks // LANES
    half = count // 2
    sends = count * cap + (half - 1) * extra

    def held(d, carry):
        high, low = one_hots(keys_ref[d], height)
        found = dot(high.astype(BF16), low.astype(BF16), ((1,), (1,)))
        found = (found > 0.5).astype(F32)
        pres[d] = found
        tall[pl.ds(d, height, stride=count), :] = found
        return carry

    repeat(count, held, 0)

    zero = jnp.zeros((height, LANES), F32)
    holders = repeat(count, lambda d, total: total + pres[d], zero)
    device = iota((count, LANES), 0)
    turn = (device + count - iota((count, LANES), 1) % count) % count
    turn = turn.astype(F32)
    others = [(device != s).astype(F32) for s in range(count)]
    near = [(device // half == s // half).astype(F32) for s in range(count)]
    weight = [1.0 - 0.8 * near[s] for s in range(count)]
    def rows_of(r):
        return pl.ds(pl.multiple_of(r * count, count), count)

    def expect(r, sums):
        here = tall[rows_of(r), :]
        even = here / jnp.maximum(jnp.sum(here, axis=0, keepdims=True), 1.0)
        return tuple(sums[s] + even * here[s : s + 1, :] for s in range(count))

    nothing = tuple(jnp.zeros((count, LANES), F32) for _ in range(count))
    sums = lax.fori_loop(0, height, expect, nothing)
    loads = tuple(
        jnp.broadcast_to(jnp.sum(sums[s], axis=1, keepdims=True), (count, LANES)) * others[s]
        for s in range(count)
    )

    def settle(pieces, o, loads):
        part = iota((count, LANES), 1) * pieces // LANES
        sides = [(part == h).astype(F32) for h in range(pieces)]
        places = [rows_of(o * tile_rows + i) for i in range(tile_rows)]
        fields = [tall[rows, :] for rows in places]
        evens = [here / jnp.maximum(jnp.sum(here, axis=0, keepdims=True), 1.0) for here in fields]
        filled = jnp.sum(sum(evens), axis=1, keepdims=True)
        for rows, here, even in zip(places, fields, evens):
            picks = jnp.zeros((count, LANES), F32)
            for side in sides:
                excess = jnp.maximum(filled - 2.0 * mcap / 3.0 + 5.0, 0.0)
                cost = 648.0 * excess * excess
                for s in range(count):
                    growth = loads[s] * loads[s]
                    cost = cost + weight[s] * growth * growth * here[s : s + 1, :]
                cost = jnp.where(here > 0.5, cost, 1e30)
                best = jnp.min(cost, axis=0, keepdims=True)
                place_in_turn = jnp.where(cost == best, turn, 1e30)
                nearest = jnp.min(place_in_turn, axis=0, keepdims=True)
                pick = jnp.where(place_in_turn == nearest, here, 0.0) * side
                picks = picks + pick
                change = pick - even * side
                loads = tuple(
                    loads[s]
                    + others[s] * jnp.sum(change * here[s : s + 1, :], axis=1, keepdims=True)
                    for s in range(count)
                )
                filled = filled + jnp.sum(change, axis=1, keepdims=True)
            tall[rows, :] = picks
        return loads

    bounds = (0, count // 4, count * 3 // 4, count)
    for i in range(3):
        step = functools.partial(settle, 1 << i)
        loads = lax.fori_loop(bounds[i], bounds[i + 1], step, loads)
    far_most, near_most = loads[0] * (1.0 - near[0]), loads[0] * near[0]
    for s in range(1, count):
        far_most = jnp.maximum(far_most, loads[s] * (1.0 - near[s]))
        near_most = jnp.maximum(near_most, loads[s] * near[s])

    fits = (far_most < cap + 0.25) & (near_most < cap + extra + 0.25)
    fits = jnp.min(jnp.min(fits.astype(F32), axis=1, keepdims=True), axis=0, keepdims=True)
    over = 1 - fits.astype(I32)

    def own(d, owner):
        return jnp.where(tall[pl.ds(d, height, stride=count), :] > 0.5, d, owner)

    owner = repeat(count, own, jnp.full((height, LANES), -1, I32))
    owner_ref[...] = owner
    mine = (owner == me).astype(F32)
    several = mine * (holders > 1.5).astype(F32)
    single = mine - several
    held_here = pres[me] * (1.0 - mine)
    departing = [held_here * (owner == d).astype(F32) for d in range(count)]
    *ranks, rank_several, rank_single = prefix_each(departing + [several, single], height)
    total_several = jnp.sum(several, axis=(0, 1), keepdims=True)
    total_mine = jnp.sum(mine, axis=(0, 1), keepdims=True)
    place = zero
    for d in range(count):
        first = d * cap + ranks[d]
        steps = ((d % half + half - me % half) % half).astype(F32)
        second = count * cap + (steps - 1.0) * extra + ranks[d] - cap
        place = place + departing[d] * (jnp.where(ranks[d] < cap - 0.5, first, second) + 1.0)

    place = place + several * (sends + rank_several + 1.0)
    place = place + single * (sends + total_several + rank_single + 1.0)
    high, low = one_hots(keys_ref[me], height)
    goes = look_up(place, high, low) - 1.0
    leaving = jnp.sum((goes < sends - 0.5).astype(F32), axis=1, keepdims=True)
    first_at, second_at = iota((pairs, pairs), 0), iota((pairs, pairs), 1)
    kind = iota((8, pairs), 0)
    same = (first_at == second_at).astype(F32)
    parts = jnp.where(kind == 0, jnp.floor(goes * (1.0 / 256.0)), 0.0)
    parts = jnp.where(kind == 1, goes - 256.0 * parts[0:1, :], parts)
    upright = dot(same.astype(BF16), parts.astype(BF16), ((1,), (1,)))
    upright = upright[:, 0:1] * 256.0 + upright[:, 1:2]
    earlier = (upright < goes - 0.5) | ((jnp.abs(upright - goes) < 0.5) & (first_at < second_at))
    position = jnp.sum(earlier.astype(F32), axis=0, keepdims=True)
    at = iota((1, pairs), 1).astype(F32)
    values = jnp.where(
        kind == 0,
        at,
        jnp.where(kind == 1, goes, jnp.where(kind == 2, src_ref[...].astype(F32), 0.0)),
    )
    order = (first_at == (position + 0.5).astype(I32)).astype(F32)
    result = (split_dot(values, order, ((1,), (1,))) + 0.5).astype(I32)
    lane = iota((8, pairs), 1)
    facts = jnp.where(lane == 0, leaving.astype(I32), over)
    facts = jnp.where(lane == 1, total_mine.astype(I32), facts)
    facts = jnp.where(lane == 2, total_several.astype(I32), facts)
    facts = jnp.where(lane == 4, me, facts)
    result = jnp.where(kind == 4, facts, result)
    table_ref[...] = jnp.where(kind == 5, (goes + 0.5).astype(I32), result)


def finish_kernel(
    count,
    blocks,
    sends,
    mcap,
    rim,
    me_ref,
    keys_ref,
    owner_ref,
    pres,
    table_ref,
    entry_ref,
    spot_ref,
    landing_ref,
):
    me = me_ref[0]
    pairs = keys_ref.shape[2]
    height = count * blocks // LANES
    tile_rows = blocks // LANES
    prefix, rows_ahead, same_tile = prefixes(height, tile_rows)
    owner = owner_ref[...]
    zero = jnp.zeros((height, LANES), F32)
    holders = repeat(count, lambda d, total: total + pres[d], zero)
    mine = (owner == me).astype(F32)
    rank_several = prefix(mine * (holders > 1.5).astype(F32), rows_ahead)
    entry_rows = entry_ref.shape[0] - 8
    lane_at = iota((entry_rows, LANES), 1)
    first_lane = iota((8, LANES), 1)
    wide = LON_DEV // LANES
    column_at = iota((height, LANES), 1) % wide
    rims = [(column_at == c).astype(F32) for c in (wide - 1, 0)]
    main = mcap - 2 * rim

    def route(d, carry):
        finished, codes, most, entries, counts = carry
        away = jnp.where(d == me, 0.0, 1.0)
        theirs = (owner == d).astype(F32)
        rank_theirs = prefix(theirs, same_tile)
        finished = finished + theirs * (as_float(d) * mcap + rank_theirs + 1.0)
        most = jnp.maximum(most, theirs * (rank_theirs + 1.0) - main)
        places = []
        for i in range(2):
            edge = theirs * rims[i]
            rank_edge = prefix(edge, same_tile)
            place = (as_float(d) * mcap + main + i * rim) * 8.0 + rank_edge + 1.0
            places.append(codes[i] + edge * place)
            most = jnp.maximum(most, edge * (rank_edge + 1.0) - 8.0 * rim)
        codes = tuple(places)
        coming = pres[d] * mine * away
        rank_coming = prefix(coming, rows_ahead)
        code = coming * (rank_coming * 1024.0 + rank_several + 1.0)
        high, low = one_hots(keys_ref[d], height)
        seen = jnp.sum(dot(code, low, exact=True) * high, axis=0, keepdims=True)
        seen = (seen + 0.5).astype(I32) - 1
        rank, local = seen >> 10, seen & 1023
        hit = iota((entry_rows, pairs), 0) == rank
        column = jnp.max(jnp.where(hit, local, -1), axis=1, keepdims=True)
        entries = jnp.where(lane_at == d, column, entries)
        arrivals = jnp.sum(coming, axis=(0, 1), keepdims=True).astype(I32)
        counts = jnp.where(first_lane == d, arrivals, counts)
        return finished, codes, most, entries, counts

    finished, codes, most, entries, counts = repeat(
        count,
        route,
        (zero, (zero, zero), zero, jnp.full((entry_rows, LANES), -1, I32), jnp.zeros((8, LANES), I32)),
    )
    entry_ref[:entry_rows, :] = entries
    entry_ref[entry_rows:, :] = counts
    for i, (tile, codes_of) in enumerate(
        ((me, finished), ((me + count - 1) % count, codes[0]), ((me + 1) % count, codes[1]))
    ):
        pick = (iota((8, height), 1) == tile * tile_rows + iota((8, height), 0)).astype(F32)
        spot_ref[i * 8 : i * 8 + 8, :] = (dot(pick, codes_of, exact=True) + 0.5).astype(I32) - 1
    tile_of = iota((height, LANES), 0) // tile_rows
    base = me.astype(F32) * mcap
    moment_place = mine * (tile_of.astype(F32) * mcap + finished - 1.0 - base)
    after = ((tile_of + 1) % count).astype(F32) * mcap - base
    ahead = ((tile_of + count - 1) % count).astype(F32) * mcap - base
    edge_place = rims[0] * 2.0 * (codes[0] - 1.0 + after * 8.0)
    edge_place = edge_place + rims[1] * (2.0 * (codes[1] - 1.0 + ahead * 8.0) + 1.0)
    edge_place = mine * (rims[0] + rims[1]) * (edge_place + 1.0)
    high, low = one_hots(keys_ref[me], height)
    lands = look_up(moment_place, high, low)
    edges = look_up(edge_place, high, low)
    goes = table_ref[5:6, :]
    slot = jnp.where(goes < sends, -1, goes - sends)
    in_slot = (iota((pairs, pairs), 0) == slot).astype(F32)
    kind = iota((8, pairs), 0)
    weighed = jnp.where(kind == 0, lands, jnp.where(kind == 2, edges, 1.0))
    summed = split_dot(weighed, in_slot, ((1,), (1,)))
    landing = summed / jnp.maximum(summed[1:2, :], 1.0)
    crowded = jnp.max(jnp.max(most, axis=1, keepdims=True), axis=0, keepdims=True) > 0.5
    over = jnp.maximum(table_ref[4:5, 3:4], crowded.astype(I32))
    found = (landing + 0.25).astype(I32) - jnp.where(kind == 2, 1, 0)
    landing_ref[...] = jnp.where(kind == 1, over, found)


def make_plan(me, keys, pair_source, fields, weights, cap, extra, mcap):
    count, _, pairs = keys.shape
    blocks, channels, cells = fields.shape
    height = count * blocks // LANES
    parts = count // 2 - 1
    first = count * cap
    sends = first + parts * extra
    vmem = pl.BlockSpec(memory_space=pltpu.VMEM)
    hbm = pl.BlockSpec(memory_space=pl.ANY)
    table, owner, pres, *sent = pl.pallas_call(
        functools.partial(plan_kernel, count, blocks, cap, extra, mcap, parts),
        out_shape=[
            jax.ShapeDtypeStruct((8, pairs), I32),
            jax.ShapeDtypeStruct((height, LANES), I32),
            jax.ShapeDtypeStruct((count, height, LANES), F32),
            jax.ShapeDtypeStruct((first, channels, cells), BF16),
        ]
        + [jax.ShapeDtypeStruct((extra, channels, cells), BF16)] * parts,
        in_specs=[pl.BlockSpec(memory_space=pltpu.SMEM), vmem, vmem, hbm, hbm],
        out_specs=[vmem] * 3 + [hbm] * (1 + parts),
        scratch_shapes=[
            pltpu.VMEM((height * count, LANES), F32),
            pltpu.VMEM(fields.shape, BF16),
            pltpu.VMEM(weights.shape, BF16),
            pltpu.VMEM((sends + 1, channels, cells), F32),
            pltpu.VMEM((sends + 1, channels, cells), BF16),
            pltpu.SMEM((8, pairs), I32),
            pltpu.SemaphoreType.DMA((8,)),
            pltpu.SemaphoreType.DMA,
            pltpu.SemaphoreType.DMA((count + parts,)),
        ],
        compiler_params=pltpu.CompilerParams(vmem_limit_bytes=53 << 20),
        name="leaving",
    )(me, keys, pair_source[None, :], fields, weights)
    return table, owner, pres, sent


def finish_plan(me, keys, owner, pres, table, count, blocks, cap, extra, mcap, rim):
    pairs = keys.shape[2]
    entry_rows = -(-(cap + extra) // 8) * 8 + 8
    sends = count * cap + (count // 2 - 1) * extra
    vmem = pl.BlockSpec(memory_space=pltpu.VMEM)
    return pl.pallas_call(
        functools.partial(finish_kernel, count, blocks, sends, mcap, rim),
        out_shape=(
            jax.ShapeDtypeStruct((entry_rows, LANES), I32),
            jax.ShapeDtypeStruct((24, LANES), I32),
            jax.ShapeDtypeStruct((8, pairs), I32),
        ),
        in_specs=[pl.BlockSpec(memory_space=pltpu.SMEM)] + [vmem] * 4,
        out_specs=(vmem, vmem, vmem),
        compiler_params=pltpu.CompilerParams(vmem_limit_bytes=8 << 20),
        name="finish",
    )(me, keys, owner, pres, table)


def products(table, xs, ws, low, high, target, packed, first, last, dummy, after=None):
    def step(g, carry):
        base = g * GROUP
        results = []
        for u in range(GROUP):
            x, w = xs[table[2, base + u]], ws[table[0, base + u]]
            results.append(dot(x, w, ((1,), (1,))))
        for u in range(GROUP):
            i = base + u
            place = table[1, i]
            again = (i > low) & (table[1, jnp.maximum(i - 1, 0)] == place)
            inside = (place >= first) & (place < last)
            where = jnp.where(inside, place - first, dummy)
            value = results[u] + jnp.where(again, target[where], 0.0)
            target[where] = value
            if packed is not None:
                packed[where] = value.astype(BF16)
        return carry if after is None else after(carry, table[1, base + GROUP - 1])

    return lax.fori_loop(low // GROUP, high // GROUP, step, 0)


def moment_rows(value):
    days = value.shape[0] // 2
    temper, moist = value[:days], value[days:]
    return [
        jnp.sum(each, axis=0, keepdims=True)
        for each in (temper, moist, temper * temper, moist * moist, temper * moist)
    ]


def put_moments(landing, total, moments, begin, end):
    spare = moments.shape[0] // 8 - 1
    row_at, group_at = iota((8, LANES), 0), iota((8, LANES), 1) // WINDOW_HALF

    def tile(place):
        return pl.ds(pl.multiple_of(place * 8, 8), 8)

    def some(g, carry):
        for u in range(4):
            i = begin + g * 4 + u
            good = i < end
            at = jnp.where(good, i, 0)
            place = jnp.where(good, jnp.clip(landing[0, at], 0, spare), spare)
            value = jnp.zeros((8, LANES), F32)
            for k, row in enumerate(moment_rows(total[at])):
                value = jnp.where(row_at == k, row, value)
            moments[tile(place), :] = value
            code = landing[2, at]
            edge = jnp.where(good & (code >= 0), jnp.minimum(code >> 4, spare), spare)
            group = (code >> 1) & 7
            shift = (group * WINDOW_HALF + (code & 1) * (LANES - WINDOW_HALF) + WINDOW_HALF) % LANES
            moved = pltpu.roll(value, shift, 1)
            moments[tile(edge), :] = jnp.where(group_at == group, moved, moments[tile(edge), :])
        return carry

    lax.fori_loop(0, (end - begin + 3) // 4, some, 0)


def chunk_copies(source, target, sem, c):
    rows = pl.ds(c * CHUNK, CHUNK)
    return pltpu.make_async_copy(source.at[rows], target.at[rows], sem.at[c])


def local_kernel(
    sends, table, landing, fields, weights, local_ref, moments, total, xs, ws, load_sem, out_sem
):
    pairs = weights.shape[0]
    leaving, owned, several = table[4, 0], table[4, 1], table[4, 2]
    low = leaving // GROUP * GROUP
    loading = load_all((fields, weights), (xs, ws), load_sem)
    for copy in loading:
        copy.start()
    moments[...] = jnp.zeros(moments.shape, F32)
    for copy in loading:
        copy.wait()
    products(table, xs, ws, low, pairs, total, None, sends, sends + pairs, pairs)
    chunks = (several + CHUNK - 1) // CHUNK

    def begin(c, carry):
        chunk_copies(total, local_ref, out_sem, c).start()
        return carry

    lax.fori_loop(0, chunks, begin, 0)
    put_moments(landing, total, moments, several, owned)

    def end(c, carry):
        chunk_copies(total, local_ref, out_sem, c).wait()
        return carry

    lax.fori_loop(0, chunks, end, 0)


def merge_kernel(count, cap, extra, mcap, table, landing, entry, local_ref, moments_in, far_ref, *refs):
    parts = count // 2 - 1
    near_refs = refs[:parts]
    out_ref, total, far, near, moments, in_sem, far_sem, near_sem, moment_sem = refs[parts:]
    several, me = table[4, 2], table[4, 4]
    half = count // 2
    spare = total.shape[0] - 1
    counts_row = entry.shape[0] - 8
    chunks = (several + CHUNK - 1) // CHUNK

    def begin(c, carry):
        chunk_copies(local_ref, total, in_sem, c).start()
        return carry

    def far_copy(s):
        rows = pl.ds(s * cap, cap)
        return pltpu.make_async_copy(far_ref.at[rows], far.at[rows], far_sem.at[s])

    near_copies = [
        pltpu.make_async_copy(near_refs[j], near.at[pl.ds(j * extra, extra)], near_sem.at[j])
        for j in range(parts)
    ]
    lax.fori_loop(0, chunks, begin, 0)
    for s in range(count):
        far_copy(s).start()
    for near_copy in near_copies:
        near_copy.start()
    moment_copy = pltpu.make_async_copy(moments_in, moments, moment_sem)
    moment_copy.start()

    def end(c, carry):
        chunk_copies(local_ref, total, in_sem, c).wait()
        return carry

    lax.fori_loop(0, chunks, end, 0)

    def add(s, low, high, came, shift):
        def some(g, inner):
            for u in range(4):
                r = low + g * 4 + u
                good = r < high
                at = jnp.where(good, r, low)
                where = jnp.where(good, jnp.maximum(entry[at, s], 0), spare)
                total[where] = total[where] + came[shift + at].astype(F32)
            return inner

        lax.fori_loop(0, (high - low + 3) // 4, some, 0)

    def from_far(s, carry):
        far_copy(s).wait()
        add(s, 0, jnp.minimum(entry[counts_row, s], cap), far, s * cap)
        return carry

    lax.fori_loop(0, count, from_far, 0)
    for near_copy in near_copies:
        near_copy.wait()

    def from_near(j, carry):
        s = me // half * half + (me % half + half - j - 1) % half
        number = jnp.clip(entry[counts_row, s], cap, cap + extra)
        add(s, cap, number, near, j * extra - cap)
        return carry

    lax.fori_loop(0, parts, from_near, 0)
    moment_copy.wait()
    put_moments(landing, total, moments, 0, several)
    for o in range(count):
        for k in range(5):
            out_ref[o, k] = moments[pl.ds(o * mcap * 8 + k, mcap, stride=8), :].astype(BF16)


def spread_kernel(count, mcap, spot_ref, rim_ref, came, map_ref, top_ref, bottom_ref, flat):
    rows, blocks_wide = map_ref.shape[1], map_ref.shape[2] // LANES - 1
    for a in range(count):
        for k in range(5):
            flat[a * mcap : (a + 1) * mcap, k * LANES : (k + 1) * LANES] = came[a, k]
    slots = count * mcap

    def gather(row):
        chosen = (iota((row.shape[0], slots), 1) == row).astype(F32)
        return dot(chosen.astype(BF16), flat[...])

    laid = gather(spot_ref[...]).astype(BF16)
    code = rim_ref[...]
    rims = gather(code >> 3)
    kept = iota((2 * rows, LANES), 1) // WINDOW_HALF == (code & 7)
    source, target = iota((LANES, LANES), 0) % WINDOW_HALF, iota((LANES, LANES), 1)
    folds = [(source == target - i * WINDOW_HALF).astype(F32).astype(BF16) for i in range(2)]

    def put(k, lanes, tile):
        map_ref[k, :, lanes] = tile
        top_ref[k, :, lanes] = tile[:WINDOW_HALF]
        bottom_ref[k, :, lanes] = tile[rows - WINDOW_HALF :]

    for k in range(5):
        of_k = slice(k * LANES, (k + 1) * LANES)
        for q in range(blocks_wide):
            put(k, slice(q * LANES, (q + 1) * LANES), laid[q * rows : (q + 1) * rows, of_k])
        piece = jnp.where(kept, rims[:, of_k], 0.0).astype(BF16)
        side = dot(piece[:rows], folds[0]) + dot(piece[rows:], folds[1])
        put(k, slice(blocks_wide * LANES, (blocks_wide + 1) * LANES), side.astype(BF16))


def tap(offset):
    offset = offset.astype(F32)
    value = jnp.exp(-offset * offset / (0.5 * WINDOW_HALF * WINDOW_HALF))
    return jnp.where(jnp.abs(offset) <= WINDOW_HALF, value, 0.0)


def halved(value):
    upper = value.astype(BF16)
    return upper, (value - upper.astype(F32)).astype(BF16)


def bands_kernel(after_ref, upper_ref, lower_ref):
    shape = upper_ref.shape
    width = shape[1]
    at, inner = iota(shape, 0), iota(shape, 1)
    beyond = at - width
    beside = jnp.where(beyond < WINDOW_HALF, beyond - WINDOW_HALF, at - WINDOW_HALF)
    outer = jnp.where(beyond < 0, at, beside)
    used = beyond < 2 * WINDOW_HALF
    upper_ref[...], lower_ref[...] = halved(jnp.where(used, tap(outer - inner), 0.0))


def across(fields, upper, lower):
    return dot(fields, upper) + dot(fields, lower)


def center_kernel(map_ref, upper, lower, out_ref):
    fields = jnp.concatenate([map_ref[k] for k in range(5)], axis=0)
    rows = map_ref.shape[1]
    smooth = across(fields, upper[...], lower[...])
    shape = (rows, rows)
    weights = tap(iota(shape, 1) - iota(shape, 0))
    for k in range(5):
        out_ref[k] = dot(weights, smooth[k * rows : (k + 1) * rows], exact=True)


def result_kernel(height, days, lat_ref, before, after, upper, lower, partial, out_ref):
    rows, width = out_ref.shape
    half = WINDOW_HALF
    fields = jnp.concatenate([ref[k] for k in range(5) for ref in (before, after)], axis=0)
    smooth = across(fields, upper[...], lower[...])
    at = iota((rows, 2 * half), 1)
    weights = tap(jnp.where(at < half, at - half, rows + at - half) - iota((rows, 2 * half), 0))
    k_at = iota((rows, LANES), 1) - half
    row = lat_ref[0] * rows + iota((rows, LANES), 0) + k_at
    taps = tap(k_at)
    inside = jnp.where((row >= 0) & (row < height), taps, 0.0)
    weight = jnp.sum(inside, axis=1, keepdims=True) * (jnp.sum(taps, axis=1, keepdims=True) * days)
    scale = 1.0 / weight
    values = []
    for k in range(5):
        beside = dot(weights, smooth[2 * k * half : 2 * (k + 1) * half], exact=True)
        values.append((partial[k] + beside) * scale)
    mean_t, mean_m, square_t, square_m, cross = values
    var_t = square_t - mean_t * mean_t
    var_m = square_m - mean_m * mean_m
    covar = cross - mean_t * mean_m
    out_ref[...] = covar / jnp.sqrt(var_t * var_m + 1e-06)


def neighbours(low, high, axis, wrap):
    count = lax.axis_size(axis)
    up = [(i, (i + 1) % count) for i in range(count if wrap else count - 1)]
    down = [(j, i) for i, j in up]
    return lax.ppermute(high, axis, up), lax.ppermute(low, axis, down)


def correlate(days, moments, top, bottom, bands):
    vmem = pl.BlockSpec(memory_space=pltpu.VMEM)
    smem = pl.BlockSpec(memory_space=pltpu.SMEM)
    small = pltpu.CompilerParams(vmem_limit_bytes=16 << 20)
    rows, width = moments.shape[1], bands[0].shape[1]
    before, after = neighbours(top, bottom, "lat", False)
    partial = pl.pallas_call(
        center_kernel,
        out_shape=jax.ShapeDtypeStruct((5, rows, width), F32),
        in_specs=[vmem] * 3,
        out_specs=vmem,
        compiler_params=small,
        name="center",
    )(moments, *bands)
    before, after, partial = lax.optimization_barrier((before, after, partial))
    height = rows * lax.axis_size("lat")
    return pl.pallas_call(
        functools.partial(result_kernel, height, days),
        out_shape=jax.ShapeDtypeStruct((rows, width), F32),
        in_specs=[smem] + [vmem] * 5,
        out_specs=vmem,
        compiler_params=small,
        name="result",
    )(lax.axis_index("lat").astype(I32)[None], before, after, *bands, partial)


def direct(cap, extra, mcap, rim, source_fields, weight_blocks, me, keys, table, owner, pres, sent):
    count = lax.axis_size("lon")
    half = count // 2
    blocks, channels, cells = source_fields.shape
    pairs = weight_blocks.shape[0]
    parts = half - 1
    first = count * cap
    sends = first + parts * extra
    smem = pl.BlockSpec(memory_space=pltpu.SMEM)
    vmem = pl.BlockSpec(memory_space=pltpu.VMEM)
    hbm = pl.BlockSpec(memory_space=pl.ANY)
    far = lax.all_to_all(
        sent[0].reshape(count, cap, channels, cells), "lon", split_axis=0, concat_axis=0, tiled=True
    ).reshape(first, channels, cells)
    near = []
    for j in range(parts):
        turn = [(i, i // half * half + (i % half + j + 1) % half) for i in range(count)]
        near.append(lax.ppermute(sent[1 + j], "lon", turn))
    entry, spot, landing = finish_plan(
        me, keys, owner, pres, table, count, blocks, cap, extra, mcap, rim
    )
    lat_count = lax.axis_size("lat")
    flag = landing[1:2, :LANES]
    flags = [flag]
    for j in range(1, lat_count):
        turn = [(i, (i + j) % lat_count) for i in range(lat_count)]
        flags.append(lax.ppermute(flag, "lat", turn))
    chunk_count = -(-pairs // CHUNK)
    local, moments = pl.pallas_call(
        functools.partial(local_kernel, sends),
        out_shape=(
            jax.ShapeDtypeStruct((pairs, channels, cells), F32),
            jax.ShapeDtypeStruct(((count * mcap + 1) * 8, cells), F32),
        ),
        in_specs=[smem, smem, hbm, hbm],
        out_specs=(hbm, vmem),
        scratch_shapes=[
            pltpu.VMEM((pairs + 1, channels, cells), F32),
            pltpu.VMEM(source_fields.shape, BF16),
            pltpu.VMEM(weight_blocks.shape, BF16),
            pltpu.SemaphoreType.DMA((8,)),
            pltpu.SemaphoreType.DMA((chunk_count,)),
        ],
        compiler_params=pltpu.CompilerParams(vmem_limit_bytes=50 << 20),
        name="staying",
    )(table, landing, source_fields, weight_blocks)
    far, near, flags = lax.optimization_barrier((far, near, flags))
    finished = pl.pallas_call(
        functools.partial(merge_kernel, count, cap, extra, mcap),
        out_shape=jax.ShapeDtypeStruct((count, 5, mcap, cells), BF16),
        in_specs=[smem, smem, smem, hbm, hbm, hbm] + [hbm] * parts,
        out_specs=vmem,
        scratch_shapes=[
            pltpu.VMEM((pairs + 1, channels, cells), F32),
            pltpu.VMEM((first, channels, cells), BF16),
            pltpu.VMEM((parts * extra, channels, cells), BF16),
            pltpu.VMEM(((count * mcap + 1) * 8, cells), F32),
            pltpu.SemaphoreType.DMA((chunk_count,)),
            pltpu.SemaphoreType.DMA((count,)),
            pltpu.SemaphoreType.DMA((parts,)),
            pltpu.SemaphoreType.DMA,
        ],
        compiler_params=pltpu.CompilerParams(vmem_limit_bytes=50 << 20),
        name="merge",
    )(table, landing, entry, local, moments, far, *near)
    bands = pl.pallas_call(
        bands_kernel,
        out_shape=[jax.ShapeDtypeStruct((LON_DEV + LANES, LON_DEV), BF16)] * 2,
        in_specs=[hbm],
        out_specs=[vmem] * 2,
        compiler_params=pltpu.CompilerParams(vmem_limit_bytes=50 << 20),
        name="bands",
    )(finished)
    arrived = lax.all_to_all(finished, "lon", split_axis=0, concat_axis=0, tiled=True)
    wide = LON_DEV // cells
    tables = spot.reshape(3, 8 * LANES)[:, :blocks].reshape(3, LAT_DEV, wide)
    where = tables[0].T.reshape(blocks, 1)
    rims = jnp.concatenate([tables[1, :, wide - 1], tables[2, :, 0]])[:, None]
    moments, top, bottom = pl.pallas_call(
        functools.partial(spread_kernel, count, mcap),
        out_shape=[
            jax.ShapeDtypeStruct((5, each, LON_DEV + LANES), BF16)
            for each in (LAT_DEV, WINDOW_HALF, WINDOW_HALF)
        ],
        in_specs=[vmem] * 3,
        out_specs=[vmem] * 3,
        scratch_shapes=[pltpu.VMEM((count * mcap, 5 * cells), BF16)],
        compiler_params=pltpu.CompilerParams(vmem_limit_bytes=8 << 20),
        name="spread",
    )(where, rims, arrived)
    arrived_flags = functools.reduce(jnp.maximum, flags)
    return correlate(channels // 2, moments, top, bottom, bands), arrived_flags


def padded_exchange(source_fields, weight_blocks, pair_source, targets, pair_block):
    lon_count = lax.axis_size("lon")
    pair_count = pair_source.shape[0]
    capacity = max(2, 2 * pair_count // lon_count)
    blocks_dev, channels, cell_count = source_fields.shape
    lanes = jnp.arange(lon_count, dtype=jnp.int32)
    matches = (targets[:, None] == lanes[None, :]).astype(jnp.int32)
    earlier = jnp.cumsum(matches, axis=0) - matches
    slots = jnp.sum(earlier * matches, axis=1)
    position = targets * capacity + slots
    outgoing = jnp.zeros((lon_count * capacity,), jnp.int32).at[position].set(pair_block)
    arriving = lax.all_to_all(
        outgoing.reshape(lon_count, capacity), "lon", split_axis=0, concat_axis=0, tiled=True
    )
    picked = source_fields[pair_source]
    terms = jnp.einsum("pck,pjk->pcj", picked, weight_blocks, preferred_element_type=jnp.float32)
    packed = (
        jnp.zeros((lon_count * capacity, channels, cell_count), jnp.float32).at[position].set(terms)
    )
    received = lax.all_to_all(
        packed.reshape(lon_count, capacity, channels, cell_count).astype(jnp.bfloat16),
        "lon",
        split_axis=0,
        concat_axis=0,
        tiled=True,
    ).astype(jnp.float32)
    remapped = jax.ops.segment_sum(
        received.reshape(lon_count * capacity, channels, cell_count),
        arriving.reshape(-1),
        num_segments=blocks_dev,
    )
    days = channels // 2
    temper = remapped[:, :days]
    moist = remapped[:, days:]
    moments = jnp.stack(
        [
            temper.sum(1),
            moist.sum(1),
            (temper * temper).sum(1),
            (moist * moist).sum(1),
            (temper * moist).sum(1),
        ]
    )
    return moments.reshape(5, LAT_DEV, LON_DEV).astype(BF16)


def padded_result(source_fields, weight_blocks, pair_source, targets, pair_block):
    moments = padded_exchange(source_fields, weight_blocks, pair_source, targets, pair_block)
    days = source_fields.shape[1] // 2
    lon_band = band_matrix(LON_DEV)
    lat_band = band_matrix(LAT_DEV)
    taller = padded(moments, (("lat", 1),), WINDOW_HALF, False)
    wider = padded(taller, (("lon", 2),), WINDOW_HALF, True).astype(F32)
    smoothed = smooth_lat(smooth_lon(wider, lon_band), lat_band)
    kernel = gaussian_taps()
    height = LAT_DEV * lax.axis_size("lat")
    rows = (
        lax.axis_index("lat") * LAT_DEV
        + jnp.arange(LAT_DEV, dtype=jnp.int32)[:, None]
        + jnp.arange(2 * WINDOW_HALF + 1, dtype=jnp.int32)[None, :]
        - WINDOW_HALF
    )
    inside = ((rows >= 0) & (rows < height)).astype(jnp.float32)
    lat_total = jnp.sum(inside * kernel[None, :], axis=1)
    weight_total = lat_total[:, None] * (jnp.sum(kernel) * days)
    mean_temper = smoothed[0] / weight_total
    mean_moist = smoothed[1] / weight_total
    var_temper = smoothed[2] / weight_total - mean_temper * mean_temper
    var_moist = smoothed[3] / weight_total - mean_moist * mean_moist
    covar = smoothed[4] / weight_total - mean_temper * mean_moist
    return covar / jnp.sqrt(var_temper * var_moist + 1e-06)


def local(source_fields, weight_blocks, pair_source, pair_target, pair_block):
    count = lax.axis_size("lon")
    blocks = source_fields.shape[0]
    pairs = pair_source.shape[0]
    share = -(-pairs // count)
    cap = max(share * 7 // 16, min(share, 8))
    extra = max(share * 3 // 16, 1)
    mcap = -(-share * 3 // 2 // 16) * 16
    rim = max(mcap // 16, 1)
    targets = pair_target[:, 0]
    keys = pair_target.reshape(1, 1, pairs) * blocks + pair_block[None, None, :]
    all_keys = lax.all_to_all(
        jnp.broadcast_to(keys, (count, 1, pairs)), "lon", split_axis=0, concat_axis=0, tiled=True
    )
    me = lax.axis_index("lon").astype(I32)[None]
    table, owner, pres, sent = make_plan(
        me, all_keys, pair_source, source_fields, weight_blocks, cap, extra, mcap
    )
    sent, owner = lax.optimization_barrier((sent, owner))
    result, flags = direct(
        cap, extra, mcap, rim, source_fields, weight_blocks, me, all_keys, table, owner, pres, sent
    )
    return lax.cond(
        jnp.max(flags) == 0,
        lambda kept: kept,
        lambda kept: padded_result(
            source_fields, weight_blocks, pair_source, targets, pair_block
        ),
        result,
    )


def solution(mesh):
    placed = (
        P(("lat", "lon"), None, None),
        P(("lat", "lon"), None, None),
        P(("lat", "lon")),
        P(("lat", "lon"), None),
        P(("lat", "lon")),
    )
    return jax.shard_map(
        local, mesh=mesh, in_specs=placed, out_specs=P("lat", "lon"), check_vma=False
    )
```

```python
import functools

import jax
import jax.numpy as jnp
from jax import lax
from jax.experimental import pallas as pl
from jax.experimental.pallas import tpu as pltpu
from jax.sharding import PartitionSpec as P

WINDOW_HALF = 16
LAT_DEV = 64
LON_DEV = 512
LANES = 128
GROUP = 16
CHUNK = 16
F32 = jnp.float32
BF16 = jnp.bfloat16
I32 = jnp.int32


def padded(x, sides, width, wrap):
    for axis, dim in sides:
        count, length = (lax.axis_size(axis), x.shape[dim])
        up = [(i, (i + 1) % count) for i in range(count if wrap else count - 1)]
        down = [(j, i) for i, j in up]
        last = lax.slice_in_dim(x, length - width, length, axis=dim)
        leading = lax.slice_in_dim(x, 0, width, axis=dim)
        before = lax.ppermute(last, axis, up)
        after = lax.ppermute(leading, axis, down)
        x = jnp.concatenate([before, x, after], axis=dim)
    return x


def gaussian_taps():
    offsets = jnp.arange(2 * WINDOW_HALF + 1).astype(jnp.float32) - WINDOW_HALF
    return jnp.exp(-offsets * offsets / (0.5 * WINDOW_HALF * WINDOW_HALF))


def band_matrix(length):
    outer = jnp.arange(length + 2 * WINDOW_HALF, dtype=jnp.int32)[:, None]
    inner = jnp.arange(length, dtype=jnp.int32)[None, :]
    offsets = (outer - inner - WINDOW_HALF).astype(jnp.float32)
    values = jnp.exp(-offsets * offsets / (0.5 * WINDOW_HALF * WINDOW_HALF))
    return jnp.where(jnp.abs(offsets) <= WINDOW_HALF, values, 0.0)


def smooth_lon(fields, lon_band):
    return jnp.einsum("krb,bj->krj", fields, lon_band, precision=lax.Precision.HIGHEST)


def smooth_lat(fields, lat_band):
    return jnp.einsum("ai,kaj->kij", lat_band, fields, precision=lax.Precision.HIGHEST)


def iota(shape, dim):
    return lax.broadcasted_iota(I32, shape, dim)


def dot(a, b, dims=((1,), (0,)), exact=False):
    return lax.dot_general(
        a,
        b,
        (dims, ((), ())),
        preferred_element_type=F32,
        precision=lax.Precision.HIGHEST if exact else None,
    )


def repeat(count, body, carry):
    if count <= 8:
        for step in range(count):
            carry = body(step, carry)
        return carry
    return lax.fori_loop(0, count, body, carry)


def one_hots(row, height):
    pairs = row.shape[1]
    high = (iota((height, pairs), 0) == (row >> 7)).astype(F32)
    low = (iota((LANES, pairs), 0) == (row & (LANES - 1))).astype(F32)
    return high, low


def split_dot(table, other, dims=((1,), (0,))):
    upper = jnp.floor(table * (1.0 / 256.0))
    lower = table - upper * 256.0
    other = other.astype(BF16)
    return dot(upper.astype(BF16), other, dims) * 256.0 + dot(lower.astype(BF16), other, dims)


def look_up(table, high, low):
    return jnp.sum(split_dot(table, low) * high, axis=0, keepdims=True)


def prefixes(height, tile_rows):
    ahead = (iota((LANES, LANES), 0) < iota((LANES, LANES), 1)).astype(BF16)
    ones = jnp.ones((LANES, LANES), BF16)
    ahead_total = jnp.concatenate([ahead, ones], axis=1)
    up, down = iota((height, height), 1), iota((height, height), 0)
    rows_ahead = (up < down).astype(BF16)
    same_tile = ((up < down) & (up // tile_rows == down // tile_rows)).astype(BF16)

    def prefix(mask, rows):
        both = dot(mask.astype(BF16), ahead_total)
        return both[:, :LANES] + dot(rows, both[:, LANES:].astype(BF16))

    return prefix, rows_ahead, same_tile


def prefix_each(masks, height):
    group = max(1, LANES // height)
    ahead = (iota((LANES, LANES), 0) < iota((LANES, LANES), 1)).astype(BF16)
    ahead_total = jnp.concatenate([ahead, jnp.ones((LANES, LANES), BF16)], axis=1)
    ranks = []
    for begin in range(0, len(masks), group):
        part = masks[begin : begin + group]
        rows = height * len(part)
        up, down = iota((rows, rows), 1), iota((rows, rows), 0)
        rows_ahead = ((up < down) & (up // height == down // height)).astype(BF16)
        both = dot(jnp.concatenate(part, axis=0).astype(BF16), ahead_total)
        rank = both[:, :LANES] + dot(rows_ahead, both[:, LANES:].astype(BF16))
        ranks += [rank[i * height : (i + 1) * height] for i in range(len(part))]
    return ranks


def as_float(d):
    return float(d) if isinstance(d, int) else lax.convert_element_type(d, F32)


def load_all(sources, targets, sem):
    copies = []
    for source, target in zip(sources, targets):
        rows = source.shape[0] // 4
        for c in range(4):
            part = pl.ds(c * rows, rows)
            copies.append(pltpu.make_async_copy(source.at[part], target.at[part], sem.at[len(copies)]))
    return copies


def plan_kernel(
    count, blocks, cap, extra, mcap, parts, me_ref, src_ref, fields, weights, *refs
):
    rings, refs = refs[:count], refs[count:]
    keys_ref, refs = refs[0], refs[1:]
    me = me_ref[0]
    for j in range(count):
        keys_ref[(me + count - j) % count] = rings[j][...]
    table_ref, owner_ref, pres, far_ref = refs[:4]
    near_refs = refs[4 : 4 + parts]
    tall, xs, ws, total, packed, guide, table, load_sem, table_sem, out_sem = refs[4 + parts :]
    loading = load_all((fields, weights), (xs, ws), load_sem)
    for copy in loading:
        copy.start()
    make_table(count, blocks, cap, extra, mcap, me_ref, keys_ref, src_ref, table_ref, owner_ref, pres, tall)
    guide[...] = table_ref[0:4, :]
    to_scalar = pltpu.make_async_copy(guide, table, table_sem)
    to_scalar.start()
    for copy in loading:
        copy.wait()
    to_scalar.wait()
    sends = packed.shape[0] - 1
    first = count * cap
    high = (table[3, 0] + GROUP - 1) // GROUP * GROUP

    def far_copy(d):
        rows = pl.ds(d * cap, cap)
        return pltpu.make_async_copy(packed.at[rows], far_ref.at[rows], out_sem.at[d])

    def start_far(begin, end):
        def one(d, carry):
            far_copy(d).start()
            return carry

        lax.fori_loop(begin, end, one, 0)

    def after(started, place):
        done = jnp.maximum(started, jnp.minimum(place // cap, count))
        start_far(started, done)
        return done

    started = products(table, xs, ws, 0, high, total, packed, 0, sends, sends, after)
    start_far(started, count)
    outs = []
    for j in range(parts):
        rows = pl.ds(first + j * extra, extra)
        outs.append(pltpu.make_async_copy(packed.at[rows], near_refs[j], out_sem.at[count + j]))
    for out in outs:
        out.start()
    for d in range(count):
        far_copy(d).wait()
    for out in outs:
        out.wait()


def make_table(
    count, blocks, cap, extra, mcap, me_ref, keys_ref, src_ref, table_ref, owner_ref, pres, tall
):
    me = me_ref[0]
    pairs = keys_ref.shape[2]
    height = count * blocks // LANES
    tile_rows = blocks // LANES
    half = count // 2
    sends = count * cap + (half - 1) * extra

    def held(d, carry):
        high, low = one_hots(keys_ref[d], height)
        found = dot(high.astype(BF16), low.astype(BF16), ((1,), (1,)))
        found = (found > 0.5).astype(F32)
        pres[d] = found
        tall[pl.ds(d, height, stride=count), :] = found
        return carry

    repeat(count, held, 0)

    zero = jnp.zeros((height, LANES), F32)
    holders = repeat(count, lambda d, total: total + pres[d], zero)
    device = iota((count, LANES), 0)
    turn = (device + count - iota((count, LANES), 1) % count) % count
    turn = turn.astype(F32)
    others = [(device != s).astype(F32) for s in range(count)]
    near = [(device // half == s // half).astype(F32) for s in range(count)]
    weight = [1.0 - 0.8 * near[s] for s in range(count)]
    def rows_of(r):
        return pl.ds(pl.multiple_of(r * count, count), count)

    def expect(r, sums):
        here = tall[rows_of(r), :]
        even = here / jnp.maximum(jnp.sum(here, axis=0, keepdims=True), 1.0)
        return tuple(sums[s] + even * here[s : s + 1, :] for s in range(count))

    nothing = tuple(jnp.zeros((count, LANES), F32) for _ in range(count))
    sums = lax.fori_loop(0, height, expect, nothing)
    loads = tuple(
        jnp.broadcast_to(jnp.sum(sums[s], axis=1, keepdims=True), (count, LANES)) * others[s]
        for s in range(count)
    )

    def settle(pieces, o, loads):
        part = iota((count, LANES), 1) * pieces // LANES
        sides = [(part == h).astype(F32) for h in range(pieces)]
        places = [rows_of(o * tile_rows + i) for i in range(tile_rows)]
        fields = [tall[rows, :] for rows in places]
        evens = [here / jnp.maximum(jnp.sum(here, axis=0, keepdims=True), 1.0) for here in fields]
        filled = jnp.sum(sum(evens), axis=1, keepdims=True)
        for rows, here, even in zip(places, fields, evens):
            picks = jnp.zeros((count, LANES), F32)
            for side in sides:
                excess = jnp.maximum(filled - 2.0 * mcap / 3.0 + 5.0, 0.0)
                cost = 648.0 * excess * excess
                for s in range(count):
                    growth = loads[s] * loads[s]
                    cost = cost + weight[s] * growth * growth * here[s : s + 1, :]
                cost = jnp.where(here > 0.5, cost, 1e30)
                best = jnp.min(cost, axis=0, keepdims=True)
                place_in_turn = jnp.where(cost == best, turn, 1e30)
                nearest = jnp.min(place_in_turn, axis=0, keepdims=True)
                pick = jnp.where(place_in_turn == nearest, here, 0.0) * side
                picks = picks + pick
                change = pick - even * side
                loads = tuple(
                    loads[s]
                    + others[s] * jnp.sum(change * here[s : s + 1, :], axis=1, keepdims=True)
                    for s in range(count)
                )
                filled = filled + jnp.sum(change, axis=1, keepdims=True)
            tall[rows, :] = picks
        return loads

    bounds = (0, count // 4, count * 3 // 4, count)
    for i in range(3):
        step = functools.partial(settle, 1 << i)
        loads = lax.fori_loop(bounds[i], bounds[i + 1], step, loads)
    far_most, near_most = loads[0] * (1.0 - near[0]), loads[0] * near[0]
    for s in range(1, count):
        far_most = jnp.maximum(far_most, loads[s] * (1.0 - near[s]))
        near_most = jnp.maximum(near_most, loads[s] * near[s])

    fits = (far_most < cap + 0.25) & (near_most < cap + extra + 0.25)
    fits = jnp.min(jnp.min(fits.astype(F32), axis=1, keepdims=True), axis=0, keepdims=True)
    over = 1 - fits.astype(I32)

    def own(d, owner):
        return jnp.where(tall[pl.ds(d, height, stride=count), :] > 0.5, d, owner)

    owner = repeat(count, own, jnp.full((height, LANES), -1, I32))
    owner_ref[...] = owner
    mine = (owner == me).astype(F32)
    several = mine * (holders > 1.5).astype(F32)
    single = mine - several
    held_here = pres[me] * (1.0 - mine)
    departing = [held_here * (owner == d).astype(F32) for d in range(count)]
    *ranks, rank_several, rank_single = prefix_each(departing + [several, single], height)
    total_several = jnp.sum(several, axis=(0, 1), keepdims=True)
    total_mine = jnp.sum(mine, axis=(0, 1), keepdims=True)
    place = zero
    for d in range(count):
        first = d * cap + ranks[d]
        steps = ((d % half + half - me % half) % half).astype(F32)
        second = count * cap + (steps - 1.0) * extra + ranks[d] - cap
        place = place + departing[d] * (jnp.where(ranks[d] < cap - 0.5, first, second) + 1.0)

    place = place + several * (sends + rank_several + 1.0)
    place = place + single * (sends + total_several + rank_single + 1.0)
    high, low = one_hots(keys_ref[me], height)
    goes = look_up(place, high, low) - 1.0
    leaving = jnp.sum((goes < sends - 0.5).astype(F32), axis=1, keepdims=True)
    first_at, second_at = iota((pairs, pairs), 0), iota((pairs, pairs), 1)
    kind = iota((8, pairs), 0)
    same = (first_at == second_at).astype(F32)
    parts = jnp.where(kind == 0, jnp.floor(goes * (1.0 / 256.0)), 0.0)
    parts = jnp.where(kind == 1, goes - 256.0 * parts[0:1, :], parts)
    upright = dot(same.astype(BF16), parts.astype(BF16), ((1,), (1,)))
    upright = upright[:, 0:1] * 256.0 + upright[:, 1:2]
    earlier = (upright < goes - 0.5) | ((jnp.abs(upright - goes) < 0.5) & (first_at < second_at))
    position = jnp.sum(earlier.astype(F32), axis=0, keepdims=True)
    at = iota((1, pairs), 1).astype(F32)
    values = jnp.where(
        kind == 0,
        at,
        jnp.where(kind == 1, goes, jnp.where(kind == 2, src_ref[...].astype(F32), 0.0)),
    )
    order = (first_at == (position + 0.5).astype(I32)).astype(F32)
    result = (split_dot(values, order, ((1,), (1,))) + 0.5).astype(I32)
    lane = iota((8, pairs), 1)
    facts = jnp.where(lane == 0, leaving.astype(I32), over)
    facts = jnp.where(lane == 1, total_mine.astype(I32), facts)
    facts = jnp.where(lane == 2, total_several.astype(I32), facts)
    facts = jnp.where(lane == 4, me, facts)
    result = jnp.where(kind == 3, facts, result)
    table_ref[...] = jnp.where(kind == 5, (goes + 0.5).astype(I32), result)


def finish_kernel(
    count,
    blocks,
    sends,
    mcap,
    rim,
    entry_rows,
    me_ref,
    keys_ref,
    owner_ref,
    pres,
    table_ref,
    entry_ref,
    spot_ref,
    landing_ref,
):
    me = me_ref[0]
    pairs = keys_ref.shape[2]
    height = count * blocks // LANES
    tile_rows = blocks // LANES
    prefix, rows_ahead, same_tile = prefixes(height, tile_rows)
    owner = owner_ref[...]
    zero = jnp.zeros((height, LANES), F32)
    holders = repeat(count, lambda d, total: total + pres[d], zero)
    mine = (owner == me).astype(F32)
    rank_several = prefix(mine * (holders > 1.5).astype(F32), rows_ahead)
    lane_at = iota((entry_rows, LANES), 1)
    first_lane = iota((8, LANES), 1)
    wide = LON_DEV // LANES
    column_at = iota((height, LANES), 1) % wide
    rims = [(column_at == c).astype(F32) for c in (wide - 1, 0)]
    main = mcap - 2 * rim

    def route(d, carry):
        finished, codes, most, entries, counts = carry
        away = jnp.where(d == me, 0.0, 1.0)
        theirs = (owner == d).astype(F32)
        rank_theirs = prefix(theirs, same_tile)
        finished = finished + theirs * (as_float(d) * mcap + rank_theirs + 1.0)
        most = jnp.maximum(most, theirs * (rank_theirs + 1.0) - main)
        places = []
        for i in range(2):
            edge = theirs * rims[i]
            rank_edge = prefix(edge, same_tile)
            place = (as_float(d) * mcap + main + i * rim) * 8.0 + rank_edge + 1.0
            places.append(codes[i] + edge * place)
            most = jnp.maximum(most, edge * (rank_edge + 1.0) - 8.0 * rim)
        codes = tuple(places)
        coming = pres[d] * mine * away
        rank_coming = prefix(coming, rows_ahead)
        code = coming * (rank_coming * 1024.0 + rank_several + 1.0)
        high, low = one_hots(keys_ref[d], height)
        seen = jnp.sum(dot(code, low, exact=True) * high, axis=0, keepdims=True)
        seen = (seen + 0.5).astype(I32) - 1
        rank, local = seen >> 10, seen & 1023
        hit = iota((entry_rows, pairs), 0) == rank
        column = jnp.max(jnp.where(hit, local, -1), axis=1, keepdims=True)
        entries = jnp.where(lane_at == d, column, entries)
        arrivals = jnp.sum(coming, axis=(0, 1), keepdims=True).astype(I32)
        counts = jnp.where(first_lane == d, arrivals, counts)
        return finished, codes, most, entries, counts

    finished, codes, most, entries, counts = repeat(
        count,
        route,
        (zero, (zero, zero), zero, jnp.full((entry_rows, LANES), -1, I32), jnp.zeros((8, LANES), I32)),
    )
    picked = (iota((entry_ref.shape[0], LANES), 0) == iota((entry_ref.shape[0], LANES), 1)).astype(F32)
    turned = dot(picked, entries.astype(F32) + 1.0, ((1,), (1,)), exact=True)
    arrivals = dot(picked, counts.astype(F32), ((1,), (1,)), exact=True)
    entry_ref[:, :entry_rows] = (turned + 0.5).astype(I32) - 1
    entry_ref[:, LANES - 1 :] = (arrivals[:, 0:1] + 0.5).astype(I32)
    for i, (tile, codes_of) in enumerate(
        ((me, finished), ((me + count - 1) % count, codes[0]), ((me + 1) % count, codes[1]))
    ):
        pick = (iota((8, height), 1) == tile * tile_rows + iota((8, height), 0)).astype(F32)
        spot_ref[i * 8 : i * 8 + 8, :] = (dot(pick, codes_of, exact=True) + 0.5).astype(I32) - 1
    tile_of = iota((height, LANES), 0) // tile_rows
    base = me.astype(F32) * mcap
    moment_place = mine * (tile_of.astype(F32) * mcap + finished - 1.0 - base)
    after = ((tile_of + 1) % count).astype(F32) * mcap - base
    ahead = ((tile_of + count - 1) % count).astype(F32) * mcap - base
    edge_place = rims[0] * 2.0 * (codes[0] - 1.0 + after * 8.0)
    edge_place = edge_place + rims[1] * (2.0 * (codes[1] - 1.0 + ahead * 8.0) + 1.0)
    edge_place = mine * (rims[0] + rims[1]) * (edge_place + 1.0)
    high, low = one_hots(keys_ref[me], height)
    lands = look_up(moment_place, high, low)
    edges = look_up(edge_place, high, low)
    goes = table_ref[5:6, :]
    slot = jnp.where(goes < sends, -1, goes - sends)
    in_slot = (iota((pairs, pairs), 0) == slot).astype(F32)
    kind = iota((8, pairs), 0)
    weighed = jnp.where(kind == 0, lands, jnp.where(kind == 2, edges, 1.0))
    summed = split_dot(weighed, in_slot, ((1,), (1,)))
    landing = summed / jnp.maximum(summed[1:2, :], 1.0)
    crowded = jnp.max(jnp.max(most, axis=1, keepdims=True), axis=0, keepdims=True) > 0.5
    over = jnp.maximum(table_ref[3:4, 3:4], crowded.astype(I32))
    found = (landing + 0.25).astype(I32) - jnp.where(kind == 2, 1, 0)
    found = jnp.where(kind == 1, over, found)
    found = jnp.where(kind == 3, table_ref[3:4, :], found)
    landing_ref[...] = found[0:4, :]


def make_plan(me, rings, pair_source, fields, weights, cap, extra, mcap):
    count, pairs = len(rings), rings[0].shape[1]
    blocks, channels, cells = fields.shape
    height = count * blocks // LANES
    parts = count // 2 - 1
    first = count * cap
    sends = first + parts * extra
    vmem = pl.BlockSpec(memory_space=pltpu.VMEM)
    hbm = pl.BlockSpec(memory_space=pl.ANY)
    keys, table, owner, pres, *sent = pl.pallas_call(
        functools.partial(plan_kernel, count, blocks, cap, extra, mcap, parts),
        out_shape=[
            jax.ShapeDtypeStruct((count, 1, pairs), I32),
            jax.ShapeDtypeStruct((8, pairs), I32),
            jax.ShapeDtypeStruct((height, LANES), I32),
            jax.ShapeDtypeStruct((count, height, LANES), F32),
            jax.ShapeDtypeStruct((first, channels, cells), BF16),
        ]
        + [jax.ShapeDtypeStruct((extra, channels, cells), BF16)] * parts,
        in_specs=[pl.BlockSpec(memory_space=pltpu.SMEM), vmem, hbm, hbm] + [vmem] * count,
        out_specs=[vmem] * 4 + [hbm] * (1 + parts),
        scratch_shapes=[
            pltpu.VMEM((height * count, LANES), F32),
            pltpu.VMEM(fields.shape, BF16),
            pltpu.VMEM(weights.shape, BF16),
            pltpu.VMEM((sends + 1, channels, cells), F32),
            pltpu.VMEM((sends + 1, channels, cells), BF16),
            pltpu.VMEM((4, pairs), I32),
            pltpu.SMEM((4, pairs), I32),
            pltpu.SemaphoreType.DMA((8,)),
            pltpu.SemaphoreType.DMA,
            pltpu.SemaphoreType.DMA((count + parts,)),
        ],
        compiler_params=pltpu.CompilerParams(vmem_limit_bytes=53 << 20),
        name="leaving",
    )(me, pair_source[None, :], fields, weights, *rings)
    return keys, table, owner, pres, sent


def finish_plan(me, keys, owner, pres, table, count, blocks, cap, extra, mcap, rim):
    pairs = keys.shape[2]
    entry_rows = -(-(cap + extra) // 8) * 8
    sends = count * cap + (count // 2 - 1) * extra
    vmem = pl.BlockSpec(memory_space=pltpu.VMEM)
    return pl.pallas_call(
        functools.partial(finish_kernel, count, blocks, sends, mcap, rim, entry_rows),
        out_shape=(
            jax.ShapeDtypeStruct((-(-count // 8) * 8, LANES), I32),
            jax.ShapeDtypeStruct((24, LANES), I32),
            jax.ShapeDtypeStruct((4, pairs), I32),
        ),
        in_specs=[pl.BlockSpec(memory_space=pltpu.SMEM)] + [vmem] * 4,
        out_specs=(vmem, vmem, vmem),
        compiler_params=pltpu.CompilerParams(vmem_limit_bytes=8 << 20),
        name="finish",
    )(me, keys, owner, pres, table)


def products(table, xs, ws, low, high, target, packed, first, last, dummy, after=None):
    def step(g, carry):
        base = g * GROUP
        results = []
        for u in range(GROUP):
            x, w = xs[table[2, base + u]], ws[table[0, base + u]]
            results.append(dot(x, w, ((1,), (1,))))
        for u in range(GROUP):
            i = base + u
            place = table[1, i]
            again = (i > low) & (table[1, jnp.maximum(i - 1, 0)] == place)
            inside = (place >= first) & (place < last)
            where = jnp.where(inside, place - first, dummy)
            value = results[u] + jnp.where(again, target[where], 0.0)
            target[where] = value
            if packed is not None:
                packed[where] = value.astype(BF16)
        return carry if after is None else after(carry, table[1, base + GROUP - 1])

    return lax.fori_loop(low // GROUP, high // GROUP, step, 0)


def moment_rows(value):
    days = value.shape[0] // 2
    temper, moist = value[:days], value[days:]
    return [
        jnp.sum(each, axis=0, keepdims=True)
        for each in (temper, moist, temper * temper, moist * moist, temper * moist)
    ]


def put_moments(landing, total, moments, begin, end):
    spare = moments.shape[0] // 8 - 1
    row_at, group_at = iota((8, LANES), 0), iota((8, LANES), 1) // WINDOW_HALF

    def tile(place):
        return pl.ds(pl.multiple_of(place * 8, 8), 8)

    def some(g, carry):
        for u in range(4):
            i = begin + g * 4 + u
            good = i < end
            at = jnp.where(good, i, 0)
            place = jnp.where(good, jnp.clip(landing[0, at], 0, spare), spare)
            value = jnp.zeros((8, LANES), F32)
            for k, row in enumerate(moment_rows(total[at])):
                value = jnp.where(row_at == k, row, value)
            moments[tile(place), :] = value
            code = landing[2, at]
            edge = jnp.where(good & (code >= 0), jnp.minimum(code >> 4, spare), spare)
            group = (code >> 1) & 7
            shift = (group * WINDOW_HALF + (code & 1) * (LANES - WINDOW_HALF) + WINDOW_HALF) % LANES
            moved = pltpu.roll(value, shift, 1)
            moments[tile(edge), :] = jnp.where(group_at == group, moved, moments[tile(edge), :])
        return carry

    lax.fori_loop(0, (end - begin + 3) // 4, some, 0)


def chunk_copies(source, target, sem, c):
    rows = pl.ds(c * CHUNK, CHUNK)
    return pltpu.make_async_copy(source.at[rows], target.at[rows], sem.at[c])


def local_kernel(
    sends, table, landing, fields, weights, local_ref, moments, total, xs, ws, load_sem, out_sem
):
    pairs = weights.shape[0]
    leaving, owned, several = table[3, 0], table[3, 1], table[3, 2]
    low = leaving // GROUP * GROUP
    loading = load_all((fields, weights), (xs, ws), load_sem)
    for copy in loading:
        copy.start()
    moments[...] = jnp.zeros(moments.shape, F32)
    for copy in loading:
        copy.wait()
    products(table, xs, ws, low, pairs, total, None, sends, sends + pairs, pairs)
    chunks = (several + CHUNK - 1) // CHUNK

    def begin(c, carry):
        chunk_copies(total, local_ref, out_sem, c).start()
        return carry

    lax.fori_loop(0, chunks, begin, 0)
    put_moments(landing, total, moments, several, owned)

    def end(c, carry):
        chunk_copies(total, local_ref, out_sem, c).wait()
        return carry

    lax.fori_loop(0, chunks, end, 0)


def merge_kernel(count, cap, extra, mcap, landing, entry, local_ref, moments_in, far_ref, *refs):
    parts = count // 2 - 1
    near_refs = refs[:parts]
    out_refs, refs = refs[parts : parts + count], refs[parts + count :]
    total, far, near, moments, in_sem, far_sem, near_sem, moment_sem = refs
    several, me = landing[3, 2], landing[3, 4]
    half = count // 2
    spare = total.shape[0] - 1
    last = entry.shape[1] - 1
    chunks = (several + CHUNK - 1) // CHUNK

    def begin(c, carry):
        chunk_copies(local_ref, total, in_sem, c).start()
        return carry

    def far_copy(s):
        rows = pl.ds(s * cap, cap)
        return pltpu.make_async_copy(far_ref.at[rows], far.at[rows], far_sem.at[s])

    near_copies = [
        pltpu.make_async_copy(near_refs[j], near.at[pl.ds(j * extra, extra)], near_sem.at[j])
        for j in range(parts)
    ]
    lax.fori_loop(0, chunks, begin, 0)
    for s in range(count):
        far_copy(s).start()
    for near_copy in near_copies:
        near_copy.start()
    moment_copy = pltpu.make_async_copy(moments_in, moments, moment_sem)
    moment_copy.start()

    def end(c, carry):
        chunk_copies(local_ref, total, in_sem, c).wait()
        return carry

    lax.fori_loop(0, chunks, end, 0)

    def add(s, low, high, came, shift):
        def some(g, inner):
            for u in range(4):
                r = low + g * 4 + u
                good = r < high
                at = jnp.where(good, r, low)
                where = jnp.where(good, jnp.maximum(entry[s, at], 0), spare)
                total[where] = total[where] + came[shift + at].astype(F32)
            return inner

        lax.fori_loop(0, (high - low + 3) // 4, some, 0)

    def from_far(s, carry):
        far_copy(s).wait()
        add(s, 0, jnp.minimum(entry[s, last], cap), far, s * cap)
        return carry

    lax.fori_loop(0, count, from_far, 0)
    for near_copy in near_copies:
        near_copy.wait()

    def from_near(j, carry):
        s = me // half * half + (me % half + half - j - 1) % half
        number = jnp.clip(entry[s, last], cap, cap + extra)
        add(s, cap, number, near, j * extra - cap)
        return carry

    lax.fori_loop(0, parts, from_near, 0)
    moment_copy.wait()
    put_moments(landing, total, moments, 0, several)
    for j in range(count):
        base = pl.multiple_of((me + j) % count * (mcap * 8), 8)
        for k in range(5):
            out_refs[j][k] = moments[pl.ds(base + k, mcap, stride=8), :].astype(BF16)


def spread_kernel(count, mcap, me_ref, spot_ref, rim_ref, *refs):
    came, (map_ref, top_ref, bottom_ref, flat) = refs[:count], refs[count:]
    rows, blocks_wide = map_ref.shape[1], map_ref.shape[2] // LANES - 1
    for j in range(count):
        a = (me_ref[0] + count - j) % count
        place = pl.ds(pl.multiple_of(a * mcap, 16), mcap)
        for k in range(5):
            flat[place, k * LANES : (k + 1) * LANES] = came[j][k]
    slots = count * mcap

    def gather(row):
        chosen = (iota((row.shape[0], slots), 1) == row).astype(F32)
        return dot(chosen.astype(BF16), flat[...])

    laid = gather(spot_ref[...]).astype(BF16)
    code = rim_ref[...]
    rims = gather(code >> 3)
    kept = iota((2 * rows, LANES), 1) // WINDOW_HALF == (code & 7)
    source, target = iota((LANES, LANES), 0) % WINDOW_HALF, iota((LANES, LANES), 1)
    folds = [(source == target - i * WINDOW_HALF).astype(F32).astype(BF16) for i in range(2)]

    def put(k, lanes, tile):
        map_ref[k, :, lanes] = tile
        top_ref[k, :, lanes] = tile[:WINDOW_HALF]
        bottom_ref[k, :, lanes] = tile[rows - WINDOW_HALF :]

    for k in range(5):
        of_k = slice(k * LANES, (k + 1) * LANES)
        for q in range(blocks_wide):
            put(k, slice(q * LANES, (q + 1) * LANES), laid[q * rows : (q + 1) * rows, of_k])
        piece = jnp.where(kept, rims[:, of_k], 0.0).astype(BF16)
        side = dot(piece[:rows], folds[0]) + dot(piece[rows:], folds[1])
        put(k, slice(blocks_wide * LANES, (blocks_wide + 1) * LANES), side.astype(BF16))


def tap(offset):
    offset = offset.astype(F32)
    value = jnp.exp(-offset * offset / (0.5 * WINDOW_HALF * WINDOW_HALF))
    return jnp.where(jnp.abs(offset) <= WINDOW_HALF, value, 0.0)


def halved(value):
    upper = value.astype(BF16)
    return upper, (value - upper.astype(F32)).astype(BF16)


def bands_kernel(after_ref, upper_ref, lower_ref):
    shape = upper_ref.shape
    width = shape[1]
    at, inner = iota(shape, 0), iota(shape, 1)
    beyond = at - width
    beside = jnp.where(beyond < WINDOW_HALF, beyond - WINDOW_HALF, at - WINDOW_HALF)
    outer = jnp.where(beyond < 0, at, beside)
    used = beyond < 2 * WINDOW_HALF
    upper_ref[...], lower_ref[...] = halved(jnp.where(used, tap(outer - inner), 0.0))


def across(fields, upper, lower):
    return dot(fields, upper) + dot(fields, lower)


def center_kernel(map_ref, upper, lower, out_ref):
    fields = jnp.concatenate([map_ref[k] for k in range(5)], axis=0)
    rows = map_ref.shape[1]
    smooth = across(fields, upper[...], lower[...])
    shape = (rows, rows)
    weights = tap(iota(shape, 1) - iota(shape, 0))
    for k in range(5):
        out_ref[k] = dot(weights, smooth[k * rows : (k + 1) * rows], exact=True)


def result_kernel(height, days, lat_ref, before, after, upper, lower, partial, out_ref):
    rows, width = out_ref.shape
    half = WINDOW_HALF
    fields = jnp.concatenate([ref[k] for k in range(5) for ref in (before, after)], axis=0)
    smooth = across(fields, upper[...], lower[...])
    at = iota((rows, 2 * half), 1)
    weights = tap(jnp.where(at < half, at - half, rows + at - half) - iota((rows, 2 * half), 0))
    k_at = iota((rows, LANES), 1) - half
    row = lat_ref[0] * rows + iota((rows, LANES), 0) + k_at
    taps = tap(k_at)
    inside = jnp.where((row >= 0) & (row < height), taps, 0.0)
    weight = jnp.sum(inside, axis=1, keepdims=True) * (jnp.sum(taps, axis=1, keepdims=True) * days)
    scale = 1.0 / weight
    values = []
    for k in range(5):
        beside = dot(weights, smooth[2 * k * half : 2 * (k + 1) * half], exact=True)
        values.append((partial[k] + beside) * scale)
    mean_t, mean_m, square_t, square_m, cross = values
    var_t = square_t - mean_t * mean_t
    var_m = square_m - mean_m * mean_m
    covar = cross - mean_t * mean_m
    out_ref[...] = covar / jnp.sqrt(var_t * var_m + 1e-06)


def neighbours(low, high, axis, wrap):
    count = lax.axis_size(axis)
    up = [(i, (i + 1) % count) for i in range(count if wrap else count - 1)]
    down = [(j, i) for i, j in up]
    return lax.ppermute(high, axis, up), lax.ppermute(low, axis, down)


def correlate(days, moments, top, bottom, bands):
    vmem = pl.BlockSpec(memory_space=pltpu.VMEM)
    smem = pl.BlockSpec(memory_space=pltpu.SMEM)
    small = pltpu.CompilerParams(vmem_limit_bytes=16 << 20)
    rows, width = moments.shape[1], bands[0].shape[1]
    before, after = neighbours(top, bottom, "lat", False)
    partial = pl.pallas_call(
        center_kernel,
        out_shape=jax.ShapeDtypeStruct((5, rows, width), F32),
        in_specs=[vmem] * 3,
        out_specs=vmem,
        compiler_params=small,
        name="center",
    )(moments, *bands)
    before, after, partial = lax.optimization_barrier((before, after, partial))
    height = rows * lax.axis_size("lat")
    return pl.pallas_call(
        functools.partial(result_kernel, height, days),
        out_shape=jax.ShapeDtypeStruct((rows, width), F32),
        in_specs=[smem] + [vmem] * 5,
        out_specs=vmem,
        compiler_params=small,
        name="result",
    )(lax.axis_index("lat").astype(I32)[None], before, after, *bands, partial)


def direct(cap, extra, mcap, rim, source_fields, weight_blocks, me, keys, table, owner, pres, sent):
    count = lax.axis_size("lon")
    half = count // 2
    blocks, channels, cells = source_fields.shape
    pairs = weight_blocks.shape[0]
    parts = half - 1
    first = count * cap
    sends = first + parts * extra
    smem = pl.BlockSpec(memory_space=pltpu.SMEM)
    vmem = pl.BlockSpec(memory_space=pltpu.VMEM)
    hbm = pl.BlockSpec(memory_space=pl.ANY)
    far = lax.all_to_all(
        sent[0].reshape(count, cap, channels, cells), "lon", split_axis=0, concat_axis=0, tiled=True
    ).reshape(first, channels, cells)
    near = []
    for j in range(parts):
        turn = [(i, i // half * half + (i % half + j + 1) % half) for i in range(count)]
        near.append(lax.ppermute(sent[1 + j], "lon", turn))
    entry, spot, landing = finish_plan(
        me, keys, owner, pres, table, count, blocks, cap, extra, mcap, rim
    )
    lat_count = lax.axis_size("lat")
    flag = landing[1:2, :LANES]
    flags = [flag]
    for j in range(1, lat_count):
        turn = [(i, (i + j) % lat_count) for i in range(lat_count)]
        flags.append(lax.ppermute(flag, "lat", turn))
    chunk_count = -(-pairs // CHUNK)
    local, moments = pl.pallas_call(
        functools.partial(local_kernel, sends),
        out_shape=(
            jax.ShapeDtypeStruct((pairs, channels, cells), F32),
            jax.ShapeDtypeStruct(((count * mcap + 1) * 8, cells), F32),
        ),
        in_specs=[smem, smem, hbm, hbm],
        out_specs=(hbm, vmem),
        scratch_shapes=[
            pltpu.VMEM((pairs + 1, channels, cells), F32),
            pltpu.VMEM(source_fields.shape, BF16),
            pltpu.VMEM(weight_blocks.shape, BF16),
            pltpu.SemaphoreType.DMA((8,)),
            pltpu.SemaphoreType.DMA((chunk_count,)),
        ],
        compiler_params=pltpu.CompilerParams(vmem_limit_bytes=50 << 20),
        name="staying",
    )(table, landing, source_fields, weight_blocks)
    far, near, flags = lax.optimization_barrier((far, near, flags))
    finished = pl.pallas_call(
        functools.partial(merge_kernel, count, cap, extra, mcap),
        out_shape=[jax.ShapeDtypeStruct((5, mcap, cells), BF16)] * count,
        in_specs=[smem, smem, hbm, hbm, hbm] + [hbm] * parts,
        out_specs=[vmem] * count,
        scratch_shapes=[
            pltpu.VMEM((pairs + 1, channels, cells), F32),
            pltpu.VMEM((first, channels, cells), BF16),
            pltpu.VMEM((parts * extra, channels, cells), BF16),
            pltpu.VMEM(((count * mcap + 1) * 8, cells), F32),
            pltpu.SemaphoreType.DMA((chunk_count,)),
            pltpu.SemaphoreType.DMA((count,)),
            pltpu.SemaphoreType.DMA((parts,)),
            pltpu.SemaphoreType.DMA,
        ],
        compiler_params=pltpu.CompilerParams(vmem_limit_bytes=50 << 20),
        name="merge",
    )(landing, entry, local, moments, far, *near)
    bands = pl.pallas_call(
        bands_kernel,
        out_shape=[jax.ShapeDtypeStruct((LON_DEV + LANES, LON_DEV), BF16)] * 2,
        in_specs=[hbm],
        out_specs=[vmem] * 2,
        compiler_params=pltpu.CompilerParams(vmem_limit_bytes=50 << 20),
        name="bands",
    )(finished[0])
    arrived = [finished[0]]
    for j in range(1, count):
        turn = [(i, (i + j) % count) for i in range(count)]
        arrived.append(lax.ppermute(finished[j], "lon", turn))
    wide = LON_DEV // cells
    tables = spot.reshape(3, 8 * LANES)[:, :blocks].reshape(3, LAT_DEV, wide)
    where = tables[0].T.reshape(blocks, 1)
    rims = jnp.concatenate([tables[1, :, wide - 1], tables[2, :, 0]])[:, None]
    moments, top, bottom = pl.pallas_call(
        functools.partial(spread_kernel, count, mcap),
        out_shape=[
            jax.ShapeDtypeStruct((5, each, LON_DEV + LANES), BF16)
            for each in (LAT_DEV, WINDOW_HALF, WINDOW_HALF)
        ],
        in_specs=[smem] + [vmem] * (2 + count),
        out_specs=[vmem] * 3,
        scratch_shapes=[pltpu.VMEM((count * mcap, 5 * cells), BF16)],
        compiler_params=pltpu.CompilerParams(vmem_limit_bytes=8 << 20),
        name="spread",
    )(me, where, rims, *arrived)
    arrived_flags = functools.reduce(jnp.maximum, flags)
    return correlate(channels // 2, moments, top, bottom, bands), arrived_flags


def padded_exchange(source_fields, weight_blocks, pair_source, targets, pair_block):
    lon_count = lax.axis_size("lon")
    pair_count = pair_source.shape[0]
    capacity = max(2, 2 * pair_count // lon_count)
    blocks_dev, channels, cell_count = source_fields.shape
    lanes = jnp.arange(lon_count, dtype=jnp.int32)
    matches = (targets[:, None] == lanes[None, :]).astype(jnp.int32)
    earlier = jnp.cumsum(matches, axis=0) - matches
    slots = jnp.sum(earlier * matches, axis=1)
    position = targets * capacity + slots
    outgoing = jnp.zeros((lon_count * capacity,), jnp.int32).at[position].set(pair_block)
    arriving = lax.all_to_all(
        outgoing.reshape(lon_count, capacity), "lon", split_axis=0, concat_axis=0, tiled=True
    )
    picked = source_fields[pair_source]
    terms = jnp.einsum("pck,pjk->pcj", picked, weight_blocks, preferred_element_type=jnp.float32)
    packed = (
        jnp.zeros((lon_count * capacity, channels, cell_count), jnp.float32).at[position].set(terms)
    )
    received = lax.all_to_all(
        packed.reshape(lon_count, capacity, channels, cell_count).astype(jnp.bfloat16),
        "lon",
        split_axis=0,
        concat_axis=0,
        tiled=True,
    ).astype(jnp.float32)
    remapped = jax.ops.segment_sum(
        received.reshape(lon_count * capacity, channels, cell_count),
        arriving.reshape(-1),
        num_segments=blocks_dev,
    )
    days = channels // 2
    temper = remapped[:, :days]
    moist = remapped[:, days:]
    moments = jnp.stack(
        [
            temper.sum(1),
            moist.sum(1),
            (temper * temper).sum(1),
            (moist * moist).sum(1),
            (temper * moist).sum(1),
        ]
    )
    return moments.reshape(5, LAT_DEV, LON_DEV).astype(BF16)


def padded_result(source_fields, weight_blocks, pair_source, targets, pair_block):
    moments = padded_exchange(source_fields, weight_blocks, pair_source, targets, pair_block)
    days = source_fields.shape[1] // 2
    lon_band = band_matrix(LON_DEV)
    lat_band = band_matrix(LAT_DEV)
    taller = padded(moments, (("lat", 1),), WINDOW_HALF, False)
    wider = padded(taller, (("lon", 2),), WINDOW_HALF, True).astype(F32)
    smoothed = smooth_lat(smooth_lon(wider, lon_band), lat_band)
    kernel = gaussian_taps()
    height = LAT_DEV * lax.axis_size("lat")
    rows = (
        lax.axis_index("lat") * LAT_DEV
        + jnp.arange(LAT_DEV, dtype=jnp.int32)[:, None]
        + jnp.arange(2 * WINDOW_HALF + 1, dtype=jnp.int32)[None, :]
        - WINDOW_HALF
    )
    inside = ((rows >= 0) & (rows < height)).astype(jnp.float32)
    lat_total = jnp.sum(inside * kernel[None, :], axis=1)
    weight_total = lat_total[:, None] * (jnp.sum(kernel) * days)
    mean_temper = smoothed[0] / weight_total
    mean_moist = smoothed[1] / weight_total
    var_temper = smoothed[2] / weight_total - mean_temper * mean_temper
    var_moist = smoothed[3] / weight_total - mean_moist * mean_moist
    covar = smoothed[4] / weight_total - mean_temper * mean_moist
    return covar / jnp.sqrt(var_temper * var_moist + 1e-06)


def local(source_fields, weight_blocks, pair_source, pair_target, pair_block):
    count = lax.axis_size("lon")
    blocks = source_fields.shape[0]
    pairs = pair_source.shape[0]
    share = -(-pairs // count)
    cap = max(share * 7 // 16, min(share, 8))
    extra = max(share * 3 // 16, 1)
    mcap = -(-share * 3 // 2 // 16) * 16
    rim = max(mcap // 16, 1)
    targets = pair_target[:, 0]
    keys = pair_target.reshape(1, pairs) * blocks + pair_block[None, :]
    rings = [keys]
    for j in range(1, count):
        rings.append(lax.ppermute(keys, "lon", [(i, (i + j) % count) for i in range(count)]))
    me = lax.axis_index("lon").astype(I32)[None]
    all_keys, table, owner, pres, sent = make_plan(
        me, rings, pair_source, source_fields, weight_blocks, cap, extra, mcap
    )
    sent, owner = lax.optimization_barrier((sent, owner))
    result, flags = direct(
        cap, extra, mcap, rim, source_fields, weight_blocks, me, all_keys, table, owner, pres, sent
    )
    return lax.cond(
        jnp.max(flags) == 0,
        lambda kept: kept,
        lambda kept: padded_result(
            source_fields, weight_blocks, pair_source, targets, pair_block
        ),
        result,
    )


def solution(mesh):
    placed = (
        P(("lat", "lon"), None, None),
        P(("lat", "lon"), None, None),
        P(("lat", "lon")),
        P(("lat", "lon"), None),
        P(("lat", "lon")),
    )
    return jax.shard_map(
        local, mesh=mesh, in_specs=placed, out_specs=P("lat", "lon"), check_vma=False
    )
```

```python
import functools

import jax
import jax.numpy as jnp
from jax import lax
from jax.experimental import pallas as pl
from jax.experimental.pallas import tpu as pltpu
from jax.sharding import PartitionSpec as P

WINDOW_HALF = 16
LAT_DEV = 64
LON_DEV = 512
LANES = 128
GROUP = 16
CHUNK = 16
F32 = jnp.float32
BF16 = jnp.bfloat16
I32 = jnp.int32


def padded(x, sides, width, wrap):
    for axis, dim in sides:
        count, length = (lax.axis_size(axis), x.shape[dim])
        up = [(i, (i + 1) % count) for i in range(count if wrap else count - 1)]
        down = [(j, i) for i, j in up]
        last = lax.slice_in_dim(x, length - width, length, axis=dim)
        leading = lax.slice_in_dim(x, 0, width, axis=dim)
        before = lax.ppermute(last, axis, up)
        after = lax.ppermute(leading, axis, down)
        x = jnp.concatenate([before, x, after], axis=dim)
    return x


def gaussian_taps():
    offsets = jnp.arange(2 * WINDOW_HALF + 1).astype(jnp.float32) - WINDOW_HALF
    return jnp.exp(-offsets * offsets / (0.5 * WINDOW_HALF * WINDOW_HALF))


def band_matrix(length):
    outer = jnp.arange(length + 2 * WINDOW_HALF, dtype=jnp.int32)[:, None]
    inner = jnp.arange(length, dtype=jnp.int32)[None, :]
    offsets = (outer - inner - WINDOW_HALF).astype(jnp.float32)
    values = jnp.exp(-offsets * offsets / (0.5 * WINDOW_HALF * WINDOW_HALF))
    return jnp.where(jnp.abs(offsets) <= WINDOW_HALF, values, 0.0)


def smooth_lon(fields, lon_band):
    return jnp.einsum("krb,bj->krj", fields, lon_band, precision=lax.Precision.HIGHEST)


def smooth_lat(fields, lat_band):
    return jnp.einsum("ai,kaj->kij", lat_band, fields, precision=lax.Precision.HIGHEST)


def iota(shape, dim):
    return lax.broadcasted_iota(I32, shape, dim)


def dot(a, b, dims=((1,), (0,)), exact=False):
    return lax.dot_general(
        a,
        b,
        (dims, ((), ())),
        preferred_element_type=F32,
        precision=lax.Precision.HIGHEST if exact else None,
    )


def repeat(count, body, carry):
    if count <= 8:
        for step in range(count):
            carry = body(step, carry)
        return carry
    return lax.fori_loop(0, count, body, carry)


def one_hots(row, height):
    pairs = row.shape[1]
    high = (iota((height, pairs), 0) == (row >> 7)).astype(F32)
    low = (iota((LANES, pairs), 0) == (row & (LANES - 1))).astype(F32)
    return high, low


def split_dot(table, other, dims=((1,), (0,))):
    upper = jnp.floor(table * (1.0 / 256.0))
    lower = table - upper * 256.0
    other = other.astype(BF16)
    return dot(upper.astype(BF16), other, dims) * 256.0 + dot(lower.astype(BF16), other, dims)


def look_up(table, high, low):
    return jnp.sum(split_dot(table, low) * high, axis=0, keepdims=True)


def prefixes(height, tile_rows):
    ahead = (iota((LANES, LANES), 0) < iota((LANES, LANES), 1)).astype(BF16)
    ones = jnp.ones((LANES, LANES), BF16)
    ahead_total = jnp.concatenate([ahead, ones], axis=1)
    up, down = iota((height, height), 1), iota((height, height), 0)
    rows_ahead = (up < down).astype(BF16)
    same_tile = ((up < down) & (up // tile_rows == down // tile_rows)).astype(BF16)

    def prefix(mask, rows):
        both = dot(mask.astype(BF16), ahead_total)
        return both[:, :LANES] + dot(rows, both[:, LANES:].astype(BF16))

    return prefix, rows_ahead, same_tile


def prefix_each(masks, height):
    group = max(1, LANES // height)
    ahead = (iota((LANES, LANES), 0) < iota((LANES, LANES), 1)).astype(BF16)
    ahead_total = jnp.concatenate([ahead, jnp.ones((LANES, LANES), BF16)], axis=1)
    ranks = []
    for begin in range(0, len(masks), group):
        part = masks[begin : begin + group]
        rows = height * len(part)
        up, down = iota((rows, rows), 1), iota((rows, rows), 0)
        rows_ahead = ((up < down) & (up // height == down // height)).astype(BF16)
        both = dot(jnp.concatenate(part, axis=0).astype(BF16), ahead_total)
        rank = both[:, :LANES] + dot(rows_ahead, both[:, LANES:].astype(BF16))
        ranks += [rank[i * height : (i + 1) * height] for i in range(len(part))]
    return ranks


def messages(count, cap, extra):
    half = count // 2
    sizes = [cap] * half + [cap + extra] * (half - 1)
    return [(sum(sizes[:m]), size) for m, size in enumerate(sizes)], sum(sizes)


def as_float(d):
    return float(d) if isinstance(d, int) else lax.convert_element_type(d, F32)


def load_all(sources, targets, sem):
    copies = []
    for source, target in zip(sources, targets):
        rows = source.shape[0] // 4
        for c in range(4):
            part = pl.ds(c * rows, rows)
            copies.append(pltpu.make_async_copy(source.at[part], target.at[part], sem.at[len(copies)]))
    return copies


def plan_kernel(
    count, blocks, cap, extra, mcap, me_ref, src_ref, fields, weights, *refs
):
    rings, refs = refs[:count], refs[count:]
    keys_ref, refs = refs[0], refs[1:]
    me = me_ref[0]
    for j in range(count):
        keys_ref[(me + count - j) % count] = rings[j][...]
    table_ref, owner_ref, pres = refs[:3]
    sent_refs = refs[3 : 2 + count]
    tall, xs, ws, total, packed, guide, table, load_sem, table_sem, out_sem = refs[2 + count :]
    loading = load_all((fields, weights), (xs, ws), load_sem)
    for copy in loading:
        copy.start()
    make_table(count, blocks, cap, extra, mcap, me_ref, keys_ref, src_ref, table_ref, owner_ref, pres, tall)
    guide[...] = table_ref[0:4, :]
    to_scalar = pltpu.make_async_copy(guide, table, table_sem)
    to_scalar.start()
    for copy in loading:
        copy.wait()
    to_scalar.wait()
    sends = packed.shape[0] - 1
    high = (table[3, 0] + GROUP - 1) // GROUP * GROUP
    spans, _ = messages(count, cap, extra)
    outs = [
        pltpu.make_async_copy(packed.at[pl.ds(begin, size)], sent_refs[m], out_sem.at[m])
        for m, (begin, size) in enumerate(spans)
    ]

    def after(started, place):
        done = 0
        for m, (begin, size) in enumerate(spans):
            whole = place >= begin + size
            done = done + whole.astype(I32)

            @pl.when((started <= m) & whole)
            def _():
                outs[m].start()

        return jnp.maximum(started, done)

    started = products(table, xs, ws, 0, high, total, packed, 0, sends, sends, after)
    after(started, jnp.int32(sends))
    for out in outs:
        out.wait()


def make_table(
    count, blocks, cap, extra, mcap, me_ref, keys_ref, src_ref, table_ref, owner_ref, pres, tall
):
    me = me_ref[0]
    pairs = keys_ref.shape[2]
    height = count * blocks // LANES
    tile_rows = blocks // LANES
    half = count // 2
    sends = messages(count, cap, extra)[1]

    def held(d, carry):
        high, low = one_hots(keys_ref[d], height)
        found = dot(high.astype(BF16), low.astype(BF16), ((1,), (1,)))
        found = (found > 0.5).astype(F32)
        pres[d] = found
        tall[pl.ds(d, height, stride=count), :] = found
        return carry

    repeat(count, held, 0)

    zero = jnp.zeros((height, LANES), F32)
    holders = repeat(count, lambda d, total: total + pres[d], zero)
    device = iota((count, LANES), 0)
    turn = (device + count - iota((count, LANES), 1) % count) % count
    turn = turn.astype(F32)
    others = [(device != s).astype(F32) for s in range(count)]
    near = [(device // half == s // half).astype(F32) for s in range(count)]
    weight = [1.0 - 0.8 * near[s] for s in range(count)]
    def rows_of(r):
        return pl.ds(pl.multiple_of(r * count, count), count)

    def expect(r, sums):
        here = tall[rows_of(r), :]
        even = here / jnp.maximum(jnp.sum(here, axis=0, keepdims=True), 1.0)
        return tuple(sums[s] + even * here[s : s + 1, :] for s in range(count))

    nothing = tuple(jnp.zeros((count, LANES), F32) for _ in range(count))
    sums = lax.fori_loop(0, height, expect, nothing)
    loads = tuple(
        jnp.broadcast_to(jnp.sum(sums[s], axis=1, keepdims=True), (count, LANES)) * others[s]
        for s in range(count)
    )

    def settle(pieces, o, loads):
        part = iota((count, LANES), 1) * pieces // LANES
        sides = [(part == h).astype(F32) for h in range(pieces)]
        places = [rows_of(o * tile_rows + i) for i in range(tile_rows)]
        fields = [tall[rows, :] for rows in places]
        evens = [here / jnp.maximum(jnp.sum(here, axis=0, keepdims=True), 1.0) for here in fields]
        filled = jnp.sum(sum(evens), axis=1, keepdims=True)
        for rows, here, even in zip(places, fields, evens):
            picks = jnp.zeros((count, LANES), F32)
            for side in sides:
                excess = jnp.maximum(filled - 2.0 * mcap / 3.0 + 5.0, 0.0)
                cost = 648.0 * excess * excess
                for s in range(count):
                    growth = loads[s] * loads[s]
                    cost = cost + weight[s] * growth * growth * here[s : s + 1, :]
                cost = jnp.where(here > 0.5, cost, 1e30)
                best = jnp.min(cost, axis=0, keepdims=True)
                place_in_turn = jnp.where(cost == best, turn, 1e30)
                nearest = jnp.min(place_in_turn, axis=0, keepdims=True)
                pick = jnp.where(place_in_turn == nearest, here, 0.0) * side
                picks = picks + pick
                change = pick - even * side
                loads = tuple(
                    loads[s]
                    + others[s] * jnp.sum(change * here[s : s + 1, :], axis=1, keepdims=True)
                    for s in range(count)
                )
                filled = filled + jnp.sum(change, axis=1, keepdims=True)
            tall[rows, :] = picks
        return loads

    bounds = (0, count // 4, count * 3 // 4, count)
    for i in range(3):
        step = functools.partial(settle, 1 << i)
        loads = lax.fori_loop(bounds[i], bounds[i + 1], step, loads)
    far_most, near_most = loads[0] * (1.0 - near[0]), loads[0] * near[0]
    for s in range(1, count):
        far_most = jnp.maximum(far_most, loads[s] * (1.0 - near[s]))
        near_most = jnp.maximum(near_most, loads[s] * near[s])

    fits = (far_most < cap + 0.25) & (near_most < cap + extra + 0.25)
    fits = jnp.min(jnp.min(fits.astype(F32), axis=1, keepdims=True), axis=0, keepdims=True)
    over = 1 - fits.astype(I32)

    def own(d, owner):
        return jnp.where(tall[pl.ds(d, height, stride=count), :] > 0.5, d, owner)

    owner = repeat(count, own, jnp.full((height, LANES), -1, I32))
    owner_ref[...] = owner
    mine = (owner == me).astype(F32)
    several = mine * (holders > 1.5).astype(F32)
    single = mine - several
    held_here = pres[me] * (1.0 - mine)
    departing = [held_here * (owner == d).astype(F32) for d in range(count)]
    *ranks, rank_several, rank_single = prefix_each(departing + [several, single], height)
    total_several = jnp.sum(several, axis=(0, 1), keepdims=True)
    total_mine = jnp.sum(mine, axis=(0, 1), keepdims=True)
    place = zero
    for d in range(count):
        steps = ((d % half + half - me % half) % half).astype(F32)
        close = half * cap + (steps - 1.0) * (cap + extra)
        begin = jnp.where(me // half == d // half, close, steps * cap)
        place = place + departing[d] * (begin + ranks[d] + 1.0)

    place = place + several * (sends + rank_several + 1.0)
    place = place + single * (sends + total_several + rank_single + 1.0)
    high, low = one_hots(keys_ref[me], height)
    goes = look_up(place, high, low) - 1.0
    leaving = jnp.sum((goes < sends - 0.5).astype(F32), axis=1, keepdims=True)
    first_at, second_at = iota((pairs, pairs), 0), iota((pairs, pairs), 1)
    kind = iota((8, pairs), 0)
    same = (first_at == second_at).astype(F32)
    parts = jnp.where(kind == 0, jnp.floor(goes * (1.0 / 256.0)), 0.0)
    parts = jnp.where(kind == 1, goes - 256.0 * parts[0:1, :], parts)
    upright = dot(same.astype(BF16), parts.astype(BF16), ((1,), (1,)))
    upright = upright[:, 0:1] * 256.0 + upright[:, 1:2]
    earlier = (upright < goes - 0.5) | ((jnp.abs(upright - goes) < 0.5) & (first_at < second_at))
    position = jnp.sum(earlier.astype(F32), axis=0, keepdims=True)
    at = iota((1, pairs), 1).astype(F32)
    values = jnp.where(
        kind == 0,
        at,
        jnp.where(kind == 1, goes, jnp.where(kind == 2, src_ref[...].astype(F32), 0.0)),
    )
    order = (first_at == (position + 0.5).astype(I32)).astype(F32)
    result = (split_dot(values, order, ((1,), (1,))) + 0.5).astype(I32)
    lane = iota((8, pairs), 1)
    facts = jnp.where(lane == 0, leaving.astype(I32), over)
    facts = jnp.where(lane == 1, total_mine.astype(I32), facts)
    facts = jnp.where(lane == 2, total_several.astype(I32), facts)
    facts = jnp.where(lane == 4, me, facts)
    result = jnp.where(kind == 3, facts, result)
    table_ref[...] = jnp.where(kind == 5, (goes + 0.5).astype(I32), result)


def finish_kernel(
    count,
    blocks,
    sends,
    mcap,
    rim,
    entry_rows,
    me_ref,
    keys_ref,
    owner_ref,
    pres,
    table_ref,
    entry_ref,
    spot_ref,
    landing_ref,
):
    me = me_ref[0]
    pairs = keys_ref.shape[2]
    height = count * blocks // LANES
    tile_rows = blocks // LANES
    prefix, rows_ahead, same_tile = prefixes(height, tile_rows)
    owner = owner_ref[...]
    zero = jnp.zeros((height, LANES), F32)
    holders = repeat(count, lambda d, total: total + pres[d], zero)
    mine = (owner == me).astype(F32)
    rank_several = prefix(mine * (holders > 1.5).astype(F32), rows_ahead)
    lane_at = iota((entry_rows, LANES), 1)
    first_lane = iota((8, LANES), 1)
    wide = LON_DEV // LANES
    column_at = iota((height, LANES), 1) % wide
    rims = [(column_at == c).astype(F32) for c in (wide - 1, 0)]
    main = mcap - 2 * rim

    def route(d, carry):
        finished, codes, most, entries, counts = carry
        away = jnp.where(d == me, 0.0, 1.0)
        theirs = (owner == d).astype(F32)
        rank_theirs = prefix(theirs, same_tile)
        finished = finished + theirs * (as_float(d) * mcap + rank_theirs + 1.0)
        most = jnp.maximum(most, theirs * (rank_theirs + 1.0) - main)
        places = []
        for i in range(2):
            edge = theirs * rims[i]
            rank_edge = prefix(edge, same_tile)
            place = (as_float(d) * mcap + main + i * rim) * 8.0 + rank_edge + 1.0
            places.append(codes[i] + edge * place)
            most = jnp.maximum(most, edge * (rank_edge + 1.0) - 8.0 * rim)
        codes = tuple(places)
        coming = pres[d] * mine * away
        rank_coming = prefix(coming, rows_ahead)
        code = coming * (rank_coming * 1024.0 + rank_several + 1.0)
        high, low = one_hots(keys_ref[d], height)
        seen = jnp.sum(dot(code, low, exact=True) * high, axis=0, keepdims=True)
        seen = (seen + 0.5).astype(I32) - 1
        rank, local = seen >> 10, seen & 1023
        hit = iota((entry_rows, pairs), 0) == rank
        column = jnp.max(jnp.where(hit, local, -1), axis=1, keepdims=True)
        entries = jnp.where(lane_at == d, column, entries)
        arrivals = jnp.sum(coming, axis=(0, 1), keepdims=True).astype(I32)
        counts = jnp.where(first_lane == d, arrivals, counts)
        return finished, codes, most, entries, counts

    finished, codes, most, entries, counts = repeat(
        count,
        route,
        (zero, (zero, zero), zero, jnp.full((entry_rows, LANES), -1, I32), jnp.zeros((8, LANES), I32)),
    )
    picked = (iota((entry_ref.shape[0], LANES), 0) == iota((entry_ref.shape[0], LANES), 1)).astype(F32)
    turned = dot(picked, entries.astype(F32) + 1.0, ((1,), (1,)), exact=True)
    arrivals = dot(picked, counts.astype(F32), ((1,), (1,)), exact=True)
    entry_ref[:, :entry_rows] = (turned + 0.5).astype(I32) - 1
    entry_ref[:, LANES - 1 :] = (arrivals[:, 0:1] + 0.5).astype(I32)
    for i, (tile, codes_of) in enumerate(
        ((me, finished), ((me + count - 1) % count, codes[0]), ((me + 1) % count, codes[1]))
    ):
        pick = (iota((8, height), 1) == tile * tile_rows + iota((8, height), 0)).astype(F32)
        spot_ref[i * 8 : i * 8 + 8, :] = (dot(pick, codes_of, exact=True) + 0.5).astype(I32) - 1
    tile_of = iota((height, LANES), 0) // tile_rows
    base = me.astype(F32) * mcap
    moment_place = mine * (tile_of.astype(F32) * mcap + finished - 1.0 - base)
    after = ((tile_of + 1) % count).astype(F32) * mcap - base
    ahead = ((tile_of + count - 1) % count).astype(F32) * mcap - base
    edge_place = rims[0] * 2.0 * (codes[0] - 1.0 + after * 8.0)
    edge_place = edge_place + rims[1] * (2.0 * (codes[1] - 1.0 + ahead * 8.0) + 1.0)
    edge_place = mine * (rims[0] + rims[1]) * (edge_place + 1.0)
    high, low = one_hots(keys_ref[me], height)
    lands = look_up(moment_place, high, low)
    edges = look_up(edge_place, high, low)
    goes = table_ref[5:6, :]
    slot = jnp.where(goes < sends, -1, goes - sends)
    in_slot = (iota((pairs, pairs), 0) == slot).astype(F32)
    kind = iota((8, pairs), 0)
    weighed = jnp.where(kind == 0, lands, jnp.where(kind == 2, edges, 1.0))
    summed = split_dot(weighed, in_slot, ((1,), (1,)))
    landing = summed / jnp.maximum(summed[1:2, :], 1.0)
    crowded = jnp.max(jnp.max(most, axis=1, keepdims=True), axis=0, keepdims=True) > 0.5
    over = jnp.maximum(table_ref[3:4, 3:4], crowded.astype(I32))
    found = (landing + 0.25).astype(I32) - jnp.where(kind == 2, 1, 0)
    found = jnp.where(kind == 1, over, found)
    found = jnp.where(kind == 3, table_ref[3:4, :], found)
    landing_ref[...] = found[0:4, :]


def make_plan(me, rings, pair_source, fields, weights, cap, extra, mcap):
    count, pairs = len(rings), rings[0].shape[1]
    blocks, channels, cells = fields.shape
    height = count * blocks // LANES
    spans, sends = messages(count, cap, extra)
    vmem = pl.BlockSpec(memory_space=pltpu.VMEM)
    hbm = pl.BlockSpec(memory_space=pl.ANY)
    keys, table, owner, pres, *sent = pl.pallas_call(
        functools.partial(plan_kernel, count, blocks, cap, extra, mcap),
        out_shape=[
            jax.ShapeDtypeStruct((count, 1, pairs), I32),
            jax.ShapeDtypeStruct((8, pairs), I32),
            jax.ShapeDtypeStruct((height, LANES), I32),
            jax.ShapeDtypeStruct((count, height, LANES), F32),
        ]
        + [jax.ShapeDtypeStruct((size, channels, cells), BF16) for _, size in spans],
        in_specs=[pl.BlockSpec(memory_space=pltpu.SMEM), vmem, hbm, hbm] + [vmem] * count,
        out_specs=[vmem] * 4 + [hbm] * (count - 1),
        scratch_shapes=[
            pltpu.VMEM((height * count, LANES), F32),
            pltpu.VMEM(fields.shape, BF16),
            pltpu.VMEM(weights.shape, BF16),
            pltpu.VMEM((sends + 1, channels, cells), F32),
            pltpu.VMEM((sends + 1, channels, cells), BF16),
            pltpu.VMEM((4, pairs), I32),
            pltpu.SMEM((4, pairs), I32),
            pltpu.SemaphoreType.DMA((8,)),
            pltpu.SemaphoreType.DMA,
            pltpu.SemaphoreType.DMA((count,)),
        ],
        compiler_params=pltpu.CompilerParams(vmem_limit_bytes=53 << 20),
        name="leaving",
    )(me, pair_source[None, :], fields, weights, *rings)
    return keys, table, owner, pres, sent


def finish_plan(me, keys, owner, pres, table, count, blocks, cap, extra, mcap, rim):
    pairs = keys.shape[2]
    entry_rows = -(-(cap + extra) // 8) * 8
    sends = messages(count, cap, extra)[1]
    vmem = pl.BlockSpec(memory_space=pltpu.VMEM)
    return pl.pallas_call(
        functools.partial(finish_kernel, count, blocks, sends, mcap, rim, entry_rows),
        out_shape=(
            jax.ShapeDtypeStruct((-(-count // 8) * 8, LANES), I32),
            jax.ShapeDtypeStruct((24, LANES), I32),
            jax.ShapeDtypeStruct((4, pairs), I32),
        ),
        in_specs=[pl.BlockSpec(memory_space=pltpu.SMEM)] + [vmem] * 4,
        out_specs=(vmem, vmem, vmem),
        compiler_params=pltpu.CompilerParams(vmem_limit_bytes=8 << 20),
        name="finish",
    )(me, keys, owner, pres, table)


def products(table, xs, ws, low, high, target, packed, first, last, dummy, after=None):
    def step(g, carry):
        base = g * GROUP
        results = []
        for u in range(GROUP):
            x, w = xs[table[2, base + u]], ws[table[0, base + u]]
            results.append(dot(x, w, ((1,), (1,))))
        for u in range(GROUP):
            i = base + u
            place = table[1, i]
            again = (i > low) & (table[1, jnp.maximum(i - 1, 0)] == place)
            inside = (place >= first) & (place < last)
            where = jnp.where(inside, place - first, dummy)
            value = results[u] + jnp.where(again, target[where], 0.0)
            target[where] = value
            if packed is not None:
                packed[where] = value.astype(BF16)
        return carry if after is None else after(carry, table[1, base + GROUP - 1])

    return lax.fori_loop(low // GROUP, high // GROUP, step, 0)


def moment_rows(value):
    days = value.shape[0] // 2
    temper, moist = value[:days], value[days:]
    return [
        jnp.sum(each, axis=0, keepdims=True)
        for each in (temper, moist, temper * temper, moist * moist, temper * moist)
    ]


def put_moments(landing, total, moments, begin, end):
    spare = moments.shape[0] // 8 - 1
    row_at, group_at = iota((8, LANES), 0), iota((8, LANES), 1) // WINDOW_HALF

    def tile(place):
        return pl.ds(pl.multiple_of(place * 8, 8), 8)

    def some(g, carry):
        for u in range(4):
            i = begin + g * 4 + u
            good = i < end
            at = jnp.where(good, i, 0)
            place = jnp.where(good, jnp.clip(landing[0, at], 0, spare), spare)
            value = jnp.zeros((8, LANES), F32)
            for k, row in enumerate(moment_rows(total[at])):
                value = jnp.where(row_at == k, row, value)
            moments[tile(place), :] = value
            code = landing[2, at]
            edge = jnp.where(good & (code >= 0), jnp.minimum(code >> 4, spare), spare)
            group = (code >> 1) & 7
            shift = (group * WINDOW_HALF + (code & 1) * (LANES - WINDOW_HALF) + WINDOW_HALF) % LANES
            moved = pltpu.roll(value, shift, 1)
            moments[tile(edge), :] = jnp.where(group_at == group, moved, moments[tile(edge), :])
        return carry

    lax.fori_loop(0, (end - begin + 3) // 4, some, 0)


def chunk_copies(source, target, sem, c):
    rows = pl.ds(c * CHUNK, CHUNK)
    return pltpu.make_async_copy(source.at[rows], target.at[rows], sem.at[c])


def local_kernel(
    sends, table, landing, fields, weights, local_ref, moments, total, xs, ws, load_sem, out_sem
):
    pairs = weights.shape[0]
    leaving, owned, several = table[3, 0], table[3, 1], table[3, 2]
    low = leaving // GROUP * GROUP
    loading = load_all((fields, weights), (xs, ws), load_sem)
    for copy in loading:
        copy.start()
    moments[...] = jnp.zeros(moments.shape, F32)
    for copy in loading:
        copy.wait()
    products(table, xs, ws, low, pairs, total, None, sends, sends + pairs, pairs)
    chunks = (several + CHUNK - 1) // CHUNK

    def begin(c, carry):
        chunk_copies(total, local_ref, out_sem, c).start()
        return carry

    lax.fori_loop(0, chunks, begin, 0)
    put_moments(landing, total, moments, several, owned)

    def end(c, carry):
        chunk_copies(total, local_ref, out_sem, c).wait()
        return carry

    lax.fori_loop(0, chunks, end, 0)


def merge_kernel(count, cap, extra, mcap, landing, entry, local_ref, moments_in, *refs):
    came_refs, refs = refs[: count - 1], refs[count - 1 :]
    out_refs, refs = refs[:count], refs[count:]
    total, came, moments, in_sem, came_sem, moment_sem = refs
    spans, _ = messages(count, cap, extra)
    several, me = landing[3, 2], landing[3, 4]
    half = count // 2
    spare = total.shape[0] - 1
    last = entry.shape[1] - 1
    chunks = (several + CHUNK - 1) // CHUNK

    def begin(c, carry):
        chunk_copies(local_ref, total, in_sem, c).start()
        return carry

    came_copies = [
        pltpu.make_async_copy(came_refs[m], came.at[pl.ds(begin_at, size)], came_sem.at[m])
        for m, (begin_at, size) in enumerate(spans)
    ]
    lax.fori_loop(0, chunks, begin, 0)
    for copy in came_copies:
        copy.start()
    moment_copy = pltpu.make_async_copy(moments_in, moments, moment_sem)
    moment_copy.start()

    def end(c, carry):
        chunk_copies(local_ref, total, in_sem, c).wait()
        return carry

    lax.fori_loop(0, chunks, end, 0)

    for m, (begin_at, size) in enumerate(spans):
        j, flip = (m, 1) if m < half else (m - half + 1, 0)
        source = (me // half + flip) % 2 * half + (me % half + half - j) % half
        number = jnp.minimum(entry[source, last], size)
        came_copies[m].wait()

        def some(g, carry, source=source, number=number, begin_at=begin_at):
            for u in range(4):
                r = g * 4 + u
                good = r < number
                at = jnp.where(good, r, 0)
                where = jnp.where(good, jnp.maximum(entry[source, at], 0), spare)
                total[where] = total[where] + came[begin_at + at].astype(F32)
            return carry

        lax.fori_loop(0, (number + 3) // 4, some, 0)

    moment_copy.wait()
    put_moments(landing, total, moments, 0, several)
    for j in range(count):
        base = pl.multiple_of((me + j) % count * (mcap * 8), 8)
        for k in range(5):
            out_refs[j][k] = moments[pl.ds(base + k, mcap, stride=8), :].astype(BF16)


def spread_kernel(count, mcap, me_ref, spot_ref, rim_ref, *refs):
    came, (map_ref, top_ref, bottom_ref, flat) = refs[:count], refs[count:]
    rows, blocks_wide = map_ref.shape[1], map_ref.shape[2] // LANES - 1
    for j in range(count):
        a = (me_ref[0] + count - j) % count
        place = pl.ds(pl.multiple_of(a * mcap, 16), mcap)
        for k in range(5):
            flat[place, k * LANES : (k + 1) * LANES] = came[j][k]
    slots = count * mcap

    def gather(row):
        chosen = (iota((row.shape[0], slots), 1) == row).astype(F32)
        return dot(chosen.astype(BF16), flat[...])

    laid = gather(spot_ref[...]).astype(BF16)
    code = rim_ref[...]
    rims = gather(code >> 3)
    kept = iota((2 * rows, LANES), 1) // WINDOW_HALF == (code & 7)
    source, target = iota((LANES, LANES), 0) % WINDOW_HALF, iota((LANES, LANES), 1)
    folds = [(source == target - i * WINDOW_HALF).astype(F32).astype(BF16) for i in range(2)]

    def put(k, lanes, tile):
        map_ref[k, :, lanes] = tile
        top_ref[k, :, lanes] = tile[:WINDOW_HALF]
        bottom_ref[k, :, lanes] = tile[rows - WINDOW_HALF :]

    for k in range(5):
        of_k = slice(k * LANES, (k + 1) * LANES)
        for q in range(blocks_wide):
            put(k, slice(q * LANES, (q + 1) * LANES), laid[q * rows : (q + 1) * rows, of_k])
        piece = jnp.where(kept, rims[:, of_k], 0.0).astype(BF16)
        side = dot(piece[:rows], folds[0]) + dot(piece[rows:], folds[1])
        put(k, slice(blocks_wide * LANES, (blocks_wide + 1) * LANES), side.astype(BF16))


def tap(offset):
    offset = offset.astype(F32)
    value = jnp.exp(-offset * offset / (0.5 * WINDOW_HALF * WINDOW_HALF))
    return jnp.where(jnp.abs(offset) <= WINDOW_HALF, value, 0.0)


def halved(value):
    upper = value.astype(BF16)
    return upper, (value - upper.astype(F32)).astype(BF16)


def bands_kernel(after_ref, upper_ref, lower_ref):
    shape = upper_ref.shape
    width = shape[1]
    at, inner = iota(shape, 0), iota(shape, 1)
    beyond = at - width
    beside = jnp.where(beyond < WINDOW_HALF, beyond - WINDOW_HALF, at - WINDOW_HALF)
    outer = jnp.where(beyond < 0, at, beside)
    used = beyond < 2 * WINDOW_HALF
    upper_ref[...], lower_ref[...] = halved(jnp.where(used, tap(outer - inner), 0.0))


def across(fields, upper, lower):
    return dot(fields, upper) + dot(fields, lower)


def center_kernel(map_ref, upper, lower, out_ref):
    fields = jnp.concatenate([map_ref[k] for k in range(5)], axis=0)
    rows = map_ref.shape[1]
    smooth = across(fields, upper[...], lower[...])
    shape = (rows, rows)
    weights = tap(iota(shape, 1) - iota(shape, 0))
    for k in range(5):
        out_ref[k] = dot(weights, smooth[k * rows : (k + 1) * rows], exact=True)


def result_kernel(height, days, lat_ref, before, after, upper, lower, partial, out_ref):
    rows, width = out_ref.shape
    half = WINDOW_HALF
    fields = jnp.concatenate([ref[k] for k in range(5) for ref in (before, after)], axis=0)
    smooth = across(fields, upper[...], lower[...])
    at = iota((rows, 2 * half), 1)
    weights = tap(jnp.where(at < half, at - half, rows + at - half) - iota((rows, 2 * half), 0))
    k_at = iota((rows, LANES), 1) - half
    row = lat_ref[0] * rows + iota((rows, LANES), 0) + k_at
    taps = tap(k_at)
    inside = jnp.where((row >= 0) & (row < height), taps, 0.0)
    weight = jnp.sum(inside, axis=1, keepdims=True) * (jnp.sum(taps, axis=1, keepdims=True) * days)
    scale = 1.0 / weight
    values = []
    for k in range(5):
        beside = dot(weights, smooth[2 * k * half : 2 * (k + 1) * half], exact=True)
        values.append((partial[k] + beside) * scale)
    mean_t, mean_m, square_t, square_m, cross = values
    var_t = square_t - mean_t * mean_t
    var_m = square_m - mean_m * mean_m
    covar = cross - mean_t * mean_m
    out_ref[...] = covar / jnp.sqrt(var_t * var_m + 1e-06)


def neighbours(low, high, axis, wrap):
    count = lax.axis_size(axis)
    up = [(i, (i + 1) % count) for i in range(count if wrap else count - 1)]
    down = [(j, i) for i, j in up]
    return lax.ppermute(high, axis, up), lax.ppermute(low, axis, down)


def correlate(days, moments, top, bottom, bands):
    vmem = pl.BlockSpec(memory_space=pltpu.VMEM)
    smem = pl.BlockSpec(memory_space=pltpu.SMEM)
    small = pltpu.CompilerParams(vmem_limit_bytes=16 << 20)
    rows, width = moments.shape[1], bands[0].shape[1]
    before, after = neighbours(top, bottom, "lat", False)
    partial = pl.pallas_call(
        center_kernel,
        out_shape=jax.ShapeDtypeStruct((5, rows, width), F32),
        in_specs=[vmem] * 3,
        out_specs=vmem,
        compiler_params=small,
        name="center",
    )(moments, *bands)
    before, after, partial = lax.optimization_barrier((before, after, partial))
    height = rows * lax.axis_size("lat")
    return pl.pallas_call(
        functools.partial(result_kernel, height, days),
        out_shape=jax.ShapeDtypeStruct((rows, width), F32),
        in_specs=[smem] + [vmem] * 5,
        out_specs=vmem,
        compiler_params=small,
        name="result",
    )(lax.axis_index("lat").astype(I32)[None], before, after, *bands, partial)


def direct(cap, extra, mcap, rim, source_fields, weight_blocks, me, keys, table, owner, pres, sent):
    count = lax.axis_size("lon")
    half = count // 2
    blocks, channels, cells = source_fields.shape
    pairs = weight_blocks.shape[0]
    spans, sends = messages(count, cap, extra)
    smem = pl.BlockSpec(memory_space=pltpu.SMEM)
    vmem = pl.BlockSpec(memory_space=pltpu.VMEM)
    hbm = pl.BlockSpec(memory_space=pl.ANY)
    came = []
    for m in range(count - 1):
        j, flip = (m, 1) if m < half else (m - half + 1, 0)
        turn = [(i, (i // half ^ flip) * half + (i % half + j) % half) for i in range(count)]
        came.append(lax.ppermute(sent[m], "lon", turn))
    entry, spot, landing = finish_plan(
        me, keys, owner, pres, table, count, blocks, cap, extra, mcap, rim
    )
    lat_count = lax.axis_size("lat")
    flag = landing[1:2, :LANES]
    flags = [flag]
    for j in range(1, lat_count):
        turn = [(i, (i + j) % lat_count) for i in range(lat_count)]
        flags.append(lax.ppermute(flag, "lat", turn))
    chunk_count = -(-pairs // CHUNK)
    local, moments = pl.pallas_call(
        functools.partial(local_kernel, sends),
        out_shape=(
            jax.ShapeDtypeStruct((pairs, channels, cells), F32),
            jax.ShapeDtypeStruct(((count * mcap + 1) * 8, cells), F32),
        ),
        in_specs=[smem, smem, hbm, hbm],
        out_specs=(hbm, vmem),
        scratch_shapes=[
            pltpu.VMEM((pairs + 1, channels, cells), F32),
            pltpu.VMEM(source_fields.shape, BF16),
            pltpu.VMEM(weight_blocks.shape, BF16),
            pltpu.SemaphoreType.DMA((8,)),
            pltpu.SemaphoreType.DMA((chunk_count,)),
        ],
        compiler_params=pltpu.CompilerParams(vmem_limit_bytes=50 << 20),
        name="staying",
    )(table, landing, source_fields, weight_blocks)
    came, flags = lax.optimization_barrier((came, flags))
    finished = pl.pallas_call(
        functools.partial(merge_kernel, count, cap, extra, mcap),
        out_shape=[jax.ShapeDtypeStruct((5, mcap, cells), BF16)] * count,
        in_specs=[smem, smem, hbm, hbm] + [hbm] * (count - 1),
        out_specs=[vmem] * count,
        scratch_shapes=[
            pltpu.VMEM((pairs + 1, channels, cells), F32),
            pltpu.VMEM((sends, channels, cells), BF16),
            pltpu.VMEM(((count * mcap + 1) * 8, cells), F32),
            pltpu.SemaphoreType.DMA((chunk_count,)),
            pltpu.SemaphoreType.DMA((count,)),
            pltpu.SemaphoreType.DMA,
        ],
        compiler_params=pltpu.CompilerParams(vmem_limit_bytes=50 << 20),
        name="merge",
    )(landing, entry, local, moments, *came)
    bands = pl.pallas_call(
        bands_kernel,
        out_shape=[jax.ShapeDtypeStruct((LON_DEV + LANES, LON_DEV), BF16)] * 2,
        in_specs=[hbm],
        out_specs=[vmem] * 2,
        compiler_params=pltpu.CompilerParams(vmem_limit_bytes=50 << 20),
        name="bands",
    )(finished[0])
    arrived = [finished[0]]
    for j in range(1, count):
        turn = [(i, (i + j) % count) for i in range(count)]
        arrived.append(lax.ppermute(finished[j], "lon", turn))
    wide = LON_DEV // cells
    tables = spot.reshape(3, 8 * LANES)[:, :blocks].reshape(3, LAT_DEV, wide)
    where = tables[0].T.reshape(blocks, 1)
    rims = jnp.concatenate([tables[1, :, wide - 1], tables[2, :, 0]])[:, None]
    moments, top, bottom = pl.pallas_call(
        functools.partial(spread_kernel, count, mcap),
        out_shape=[
            jax.ShapeDtypeStruct((5, each, LON_DEV + LANES), BF16)
            for each in (LAT_DEV, WINDOW_HALF, WINDOW_HALF)
        ],
        in_specs=[smem] + [vmem] * (2 + count),
        out_specs=[vmem] * 3,
        scratch_shapes=[pltpu.VMEM((count * mcap, 5 * cells), BF16)],
        compiler_params=pltpu.CompilerParams(vmem_limit_bytes=8 << 20),
        name="spread",
    )(me, where, rims, *arrived)
    arrived_flags = functools.reduce(jnp.maximum, flags)
    return correlate(channels // 2, moments, top, bottom, bands), arrived_flags


def padded_exchange(source_fields, weight_blocks, pair_source, targets, pair_block):
    lon_count = lax.axis_size("lon")
    pair_count = pair_source.shape[0]
    capacity = max(2, 2 * pair_count // lon_count)
    blocks_dev, channels, cell_count = source_fields.shape
    lanes = jnp.arange(lon_count, dtype=jnp.int32)
    matches = (targets[:, None] == lanes[None, :]).astype(jnp.int32)
    earlier = jnp.cumsum(matches, axis=0) - matches
    slots = jnp.sum(earlier * matches, axis=1)
    position = targets * capacity + slots
    outgoing = jnp.zeros((lon_count * capacity,), jnp.int32).at[position].set(pair_block)
    arriving = lax.all_to_all(
        outgoing.reshape(lon_count, capacity), "lon", split_axis=0, concat_axis=0, tiled=True
    )
    picked = source_fields[pair_source]
    terms = jnp.einsum("pck,pjk->pcj", picked, weight_blocks, preferred_element_type=jnp.float32)
    packed = (
        jnp.zeros((lon_count * capacity, channels, cell_count), jnp.float32).at[position].set(terms)
    )
    received = lax.all_to_all(
        packed.reshape(lon_count, capacity, channels, cell_count).astype(jnp.bfloat16),
        "lon",
        split_axis=0,
        concat_axis=0,
        tiled=True,
    ).astype(jnp.float32)
    remapped = jax.ops.segment_sum(
        received.reshape(lon_count * capacity, channels, cell_count),
        arriving.reshape(-1),
        num_segments=blocks_dev,
    )
    days = channels // 2
    temper = remapped[:, :days]
    moist = remapped[:, days:]
    moments = jnp.stack(
        [
            temper.sum(1),
            moist.sum(1),
            (temper * temper).sum(1),
            (moist * moist).sum(1),
            (temper * moist).sum(1),
        ]
    )
    return moments.reshape(5, LAT_DEV, LON_DEV).astype(BF16)


def padded_result(source_fields, weight_blocks, pair_source, targets, pair_block):
    moments = padded_exchange(source_fields, weight_blocks, pair_source, targets, pair_block)
    days = source_fields.shape[1] // 2
    lon_band = band_matrix(LON_DEV)
    lat_band = band_matrix(LAT_DEV)
    taller = padded(moments, (("lat", 1),), WINDOW_HALF, False)
    wider = padded(taller, (("lon", 2),), WINDOW_HALF, True).astype(F32)
    smoothed = smooth_lat(smooth_lon(wider, lon_band), lat_band)
    kernel = gaussian_taps()
    height = LAT_DEV * lax.axis_size("lat")
    rows = (
        lax.axis_index("lat") * LAT_DEV
        + jnp.arange(LAT_DEV, dtype=jnp.int32)[:, None]
        + jnp.arange(2 * WINDOW_HALF + 1, dtype=jnp.int32)[None, :]
        - WINDOW_HALF
    )
    inside = ((rows >= 0) & (rows < height)).astype(jnp.float32)
    lat_total = jnp.sum(inside * kernel[None, :], axis=1)
    weight_total = lat_total[:, None] * (jnp.sum(kernel) * days)
    mean_temper = smoothed[0] / weight_total
    mean_moist = smoothed[1] / weight_total
    var_temper = smoothed[2] / weight_total - mean_temper * mean_temper
    var_moist = smoothed[3] / weight_total - mean_moist * mean_moist
    covar = smoothed[4] / weight_total - mean_temper * mean_moist
    return covar / jnp.sqrt(var_temper * var_moist + 1e-06)


def local(source_fields, weight_blocks, pair_source, pair_target, pair_block):
    count = lax.axis_size("lon")
    blocks = source_fields.shape[0]
    pairs = pair_source.shape[0]
    share = -(-pairs // count)
    cap = max(share * 7 // 16, min(share, 8))
    extra = max(share * 3 // 16, 1)
    mcap = -(-share * 3 // 2 // 16) * 16
    rim = max(mcap // 16, 1)
    targets = pair_target[:, 0]
    keys = pair_target.reshape(1, pairs) * blocks + pair_block[None, :]
    rings = [keys]
    for j in range(1, count):
        rings.append(lax.ppermute(keys, "lon", [(i, (i + j) % count) for i in range(count)]))
    me = lax.axis_index("lon").astype(I32)[None]
    all_keys, table, owner, pres, sent = make_plan(
        me, rings, pair_source, source_fields, weight_blocks, cap, extra, mcap
    )
    sent, owner = lax.optimization_barrier((sent, owner))
    result, flags = direct(
        cap, extra, mcap, rim, source_fields, weight_blocks, me, all_keys, table, owner, pres, sent
    )
    return lax.cond(
        jnp.max(flags) == 0,
        lambda kept: kept,
        lambda kept: padded_result(
            source_fields, weight_blocks, pair_source, targets, pair_block
        ),
        result,
    )


def solution(mesh):
    placed = (
        P(("lat", "lon"), None, None),
        P(("lat", "lon"), None, None),
        P(("lat", "lon")),
        P(("lat", "lon"), None),
        P(("lat", "lon")),
    )
    return jax.shard_map(
        local, mesh=mesh, in_specs=placed, out_specs=P("lat", "lon"), check_vma=False
    )
```
